32 devices in a mesh: dp: 8 (over z, y), mp: 4 (over x, core).
Axes of the slice: x: 2, y: 2, z: 4, core: 2. Of those that a mesh axis runs over, the one named last changes fastest.
Arguments:
- tokens: bfloat16 [32768, 512], P(('dp', 'mp')), may hold values from -6 to 6
- cotangent: bfloat16 [32768, 512], P(('dp', 'mp')), may hold values from -6 to 6
- clip_ids: int32 [32768], P('dp'), may hold values from 15 to 511, as said below
- frame_ids: int32 [32768], P('dp'), may hold values from 0 to 15, as said below
- step: int32 [1], replicated, may hold values from 2 to 20
- w_qkv: float32 [3, 512, 512], P(None, 'dp', 'mp'), may hold values from -0.25 to 0.25
- w_out: float32 [512, 512], P('mp', 'dp'), may hold values from -0.75 to 0.75
- w_up: float32 [512, 2048], P('dp', 'mp'), may hold values from -0.25 to 0.25
- w_down: float32 [2048, 512], P('mp', 'dp'), may hold values from -0.125 to 0.125
- norm_params: float32 [4, 512], replicated, may hold values from -0.9 to 1.45, as said below
- moment_qkv: float32 [3, 512, 512], P(None, 'dp', 'mp'), may hold values from -0.00036621094 to 0.00036621094
- moment_out: float32 [512, 512], P('mp', 'dp'), may hold values from -0.00036621094 to 0.00036621094
- moment_up: float32 [512, 2048], P('dp', 'mp'), may hold values from -0.00036621094 to 0.00036621094
- moment_down: float32 [2048, 512], P('mp', 'dp'), may hold values from -0.00036621094 to 0.00036621094
- moment_norm: float32 [4, 512], replicated, may hold values from -0.0009765625 to 0.0009765625
- square_qkv: float32 [3, 512, 512], P(None, 'dp', 'mp'), may hold values from 1.588423e-08 to 6.353692e-08
- square_out: float32 [512, 512], P('mp', 'dp'), may hold values from 1.588423e-08 to 6.353692e-08
- square_up: float32 [512, 2048], P('dp', 'mp'), may hold values from 1.588423e-08 to 6.353692e-08
- square_down: float32 [2048, 512], P('mp', 'dp'), may hold values from 1.588423e-08 to 6.353692e-08
- square_norm: float32 [4, 512], replicated, may hold values from 1.4295807e-07 to 5.718323e-07
- average_qkv: float32 [3, 512, 512], P(None, 'dp', 'mp'), may hold values from -0.25 to 0.25
- average_out: float32 [512, 512], P('mp', 'dp'), may hold values from -0.75 to 0.75
- average_up: float32 [512, 2048], P('dp', 'mp'), may hold values from -0.25 to 0.25
- average_down: float32 [2048, 512], P('mp', 'dp'), may hold values from -0.125 to 0.125
- average_norm: float32 [4, 512], replicated, may hold values from 0.5 to 1.5
Outputs:
- block_out: bfloat16 [32768, 512], P(('dp', 'mp'))
- grad_tokens: float32 [32768, 512], P(('dp', 'mp'))
- grad_norm: float32 [], replicated
- new_qkv: float32 [3, 512, 512], P(None, 'dp', 'mp')
- new_out: float32 [512, 512], P('mp', 'dp')
- new_up: float32 [512, 2048], P('dp', 'mp')
- new_down: float32 [2048, 512], P('mp', 'dp')
- new_norm: float32 [4, 512], replicated
- new_moment_qkv: float32 [3, 512, 512], P(None, 'dp', 'mp')
- new_moment_out: float32 [512, 512], P('mp', 'dp')
- new_moment_up: float32 [512, 2048], P('dp', 'mp')
- new_moment_down: float32 [2048, 512], P('mp', 'dp')
- new_moment_norm: float32 [4, 512], replicated
- new_square_qkv: float32 [3, 512, 512], P(None, 'dp', 'mp')
- new_square_out: float32 [512, 512], P('mp', 'dp')
- new_square_up: float32 [512, 2048], P('dp', 'mp')
- new_square_down: float32 [2048, 512], P('mp', 'dp')
- new_square_norm: float32 [4, 512], replicated
- copy_qkv: bfloat16 [3, 512, 512], P(None, 'dp', 'mp')
- copy_out: bfloat16 [512, 512], P('mp', 'dp')
- copy_up: bfloat16 [512, 2048], P('dp', 'mp')
- copy_down: bfloat16 [2048, 512], P('mp', 'dp')
- new_average_qkv: float32 [3, 512, 512], P(None, 'dp', 'mp')
- new_average_out: float32 [512, 512], P('mp', 'dp')
- new_average_up: float32 [512, 2048], P('dp', 'mp')
- new_average_down: float32 [2048, 512], P('mp', 'dp')
- new_average_norm: float32 [4, 512], replicated
The draws below stay inside these ranges and needn't reach their ends.
Inputs may be any that keep to these rules, and one draw needn't show every extreme that they name: `clip_ids`: clips are runs of whole frames of 64 tokens with at most 1024 tokens; no clip crosses a boundary between aligned groups of 4096 tokens, and in every such group some clip has exactly 1024 tokens. A clip's number is the index, among all frames of 64 tokens, of its last frame, so numbers never fall along the tokens. `frame_ids`: A token's frame counts whole frames of 64 tokens from the start of its clip. `norm_params`: rows 0 and 2 are gains near one, rows 1 and 3 biases near zero.
All inputs are finite; a program needn't handle non-finite values.
Results may differ from the reference program's by a relative error of at most 0.02.
Values may be sent and summed in bfloat16 or wider, within the bound.
No kernel may reach another device: no remote copies, remote signals or barrier semaphores. Data moves between devices by JAX's collectives and lax.ppermute only.
A program may use at most 128 MiB of HBM per device.

```python
import math
import jax
import jax.numpy as jnp
from jax import lax

D = 512
HEADS = 8
HEAD = 64
FF = 2048
FRAME = 64
FRAMES = 16
CLIP = 1024
TOK_GRP = 4096
TOKENS = 32768


def clip_layout(key):
    groups = TOKENS // TOK_GRP
    frame_slots = TOK_GRP // FRAME
    lengths = jax.random.randint(jax.random.fold_in(key, 11), (groups, frame_slots), 1, FRAMES + 1)
    lengths = lengths.at[:, 0].set(FRAMES)
    finish = jnp.cumsum(lengths, axis=1)
    places = jnp.arange(frame_slots, dtype=jnp.int32)
    owners = jnp.sum((finish[:, None, :] <= places[None, :, None]).astype(jnp.int32), axis=2)
    beginning = finish - lengths
    first_slot = jnp.take_along_axis(beginning, owners, axis=1)
    last_slot = jnp.minimum(jnp.take_along_axis(finish, owners, axis=1) - 1, frame_slots - 1)
    frame_rows = places[None, :] - first_slot
    clip_rows = last_slot + jnp.arange(groups, dtype=jnp.int32)[:, None] * frame_slots
    clip_rows = jnp.repeat(clip_rows, FRAME, axis=1).reshape(TOKENS)
    frame_rows = jnp.repeat(frame_rows, FRAME, axis=1).reshape(TOKENS)
    return (clip_rows.astype(jnp.int32), frame_rows.astype(jnp.int32))


def draw_clip_ids(key, part):
    return clip_layout(key)[0]


def draw_frame_ids(key, part):
    return clip_layout(key)[1]


def draw_norm_params(key, part):
    base = jnp.clip(jax.random.normal(key, (4, D), jnp.float32), -3.0, 3.0)
    row_index = jnp.arange(4)[:, None]
    return jnp.where(row_index % 2 == 0, 1.0 + 0.15 * base, 0.3 * base).astype(jnp.float32)


def level_of(key, shape, pieces, smallest, top_value):
    loudness, own = 1.0, jax.random.fold_in(key, 6)
    for position, shards_of in pieces:
        heights = jnp.exp(jax.random.uniform(jax.random.fold_in(own, position), (shards_of,), jnp.float32, smallest / len(pieces), top_value / len(pieces)))
        loudness = loudness * jnp.repeat(heights, shape[position] // shards_of).reshape([-1 if axis == position else 1 for axis in range(len(shape))])
    return loudness


def scatter_about(own_key, dims, width, reach, pieces=(), held_as=jnp.bfloat16):
    loudness = level_of(own_key, dims, pieces, -0.22, 0.18) if pieces else 1.0
    array = jax.random.normal(own_key, dims, jnp.float32) * width * loudness
    return jnp.minimum(jnp.maximum(array, -reach), reach).astype(held_as)


def setup_inputs(seed: int = 0) -> dict:
    arg_keys = jax.random.split(jax.random.key(seed), 26)
    tokens = scatter_about(arg_keys[0], (TOKENS, D), 1.0, 6.0, ((0, 32),))
    cotangent = scatter_about(arg_keys[1], (TOKENS, D), 1.0, 6.0, ((0, 32),))
    clip_ids = draw_clip_ids(jax.random.fold_in(arg_keys[25], 71), 0)
    frame_ids = draw_frame_ids(jax.random.fold_in(arg_keys[25], 71), 0)
    step = jax.random.randint(arg_keys[4], (1,), 2, 21).astype(jnp.int32)
    w_qkv = scatter_about(arg_keys[5], (3, D, D), D ** -0.5, 0.25, ((1, 8), (2, 4)), jnp.float32)
    w_out = scatter_about(arg_keys[6], (D, D), (D // 8) ** -0.5, 0.75, ((0, 4), (1, 8)), jnp.float32)
    w_up = scatter_about(arg_keys[7], (D, FF), D ** -0.5, 0.25, ((0, 8), (1, 4)), jnp.float32)
    w_down = scatter_about(arg_keys[8], (FF, D), FF ** -0.5, 0.125, ((0, 4), (1, 8)), jnp.float32)
    norm_params = draw_norm_params(jax.random.fold_in(arg_keys[25], 71), 0)
    moment_qkv = scatter_about(arg_keys[10], (3, D, D), (0.11 * (4 * D * D + 2 * D * FF + 4 * D) ** -0.5), 0.00036621094, ((1, 8), (2, 4)), jnp.float32)
    moment_out = scatter_about(arg_keys[11], (D, D), (0.11 * (4 * D * D + 2 * D * FF + 4 * D) ** -0.5), 0.00036621094, ((0, 4), (1, 8)), jnp.float32)
    moment_up = scatter_about(arg_keys[12], (D, FF), (0.11 * (4 * D * D + 2 * D * FF + 4 * D) ** -0.5), 0.00036621094, ((0, 8), (1, 4)), jnp.float32)
    moment_down = scatter_about(arg_keys[13], (FF, D), (0.11 * (4 * D * D + 2 * D * FF + 4 * D) ** -0.5), 0.00036621094, ((0, 4), (1, 8)), jnp.float32)
    moment_norm = scatter_about(arg_keys[14], (4, D), (0.33 * (4 * D * D + 2 * D * FF + 4 * D) ** -0.5), 0.0009765625, (), jnp.float32)
    square_qkv = jnp.clip(jnp.exp(math.log(6.353692327820681e-08) - 1.3862944 * jax.random.uniform(arg_keys[15], (3, D, D), jnp.float32) ** level_of(arg_keys[15], (3, D, D), ((1, 8), (2, 4)), -0.2, 0.2)), 1.5884230819551703e-08, 6.353692327820681e-08)
    square_out = jnp.clip(jnp.exp(math.log(6.353692327820681e-08) - 1.3862944 * jax.random.uniform(arg_keys[16], (D, D), jnp.float32) ** level_of(arg_keys[16], (D, D), ((0, 4), (1, 8)), -0.2, 0.2)), 1.5884230819551703e-08, 6.353692327820681e-08)
    square_up = jnp.clip(jnp.exp(math.log(6.353692327820681e-08) - 1.3862944 * jax.random.uniform(arg_keys[17], (D, FF), jnp.float32) ** level_of(arg_keys[17], (D, FF), ((0, 8), (1, 4)), -0.2, 0.2)), 1.5884230819551703e-08, 6.353692327820681e-08)
    square_down = jnp.clip(jnp.exp(math.log(6.353692327820681e-08) - 1.3862944 * jax.random.uniform(arg_keys[18], (FF, D), jnp.float32) ** level_of(arg_keys[18], (FF, D), ((0, 4), (1, 8)), -0.2, 0.2)), 1.5884230819551703e-08, 6.353692327820681e-08)
    square_norm = jnp.clip(jnp.exp(jax.random.uniform(arg_keys[19], (4, D), jnp.float32, math.log(1.429580720468948e-07), math.log(5.718322881875793e-07))), 1.429580720468948e-07, 5.718322881875793e-07)
    average_qkv = scatter_about(arg_keys[20], (3, D, D), D ** -0.5, 0.25, ((1, 8), (2, 4)), jnp.float32)
    average_out = scatter_about(arg_keys[21], (D, D), (D // 8) ** -0.5, 0.75, ((0, 4), (1, 8)), jnp.float32)
    average_up = scatter_about(arg_keys[22], (D, FF), D ** -0.5, 0.25, ((0, 8), (1, 4)), jnp.float32)
    average_down = scatter_about(arg_keys[23], (FF, D), FF ** -0.5, 0.125, ((0, 4), (1, 8)), jnp.float32)
    average_norm = jnp.clip(1.0 + 0.1 * jax.random.normal(arg_keys[24], (4, D), jnp.float32), 0.5, 1.5)
    return dict(tokens=tokens, cotangent=cotangent, clip_ids=clip_ids, frame_ids=frame_ids, step=step, w_qkv=w_qkv, w_out=w_out, w_up=w_up, w_down=w_down, norm_params=norm_params, moment_qkv=moment_qkv, moment_out=moment_out, moment_up=moment_up, moment_down=moment_down, moment_norm=moment_norm, square_qkv=square_qkv, square_out=square_out, square_up=square_up, square_down=square_down, square_norm=square_norm, average_qkv=average_qkv, average_out=average_out, average_up=average_up, average_down=average_down, average_norm=average_norm)


@jax.custom_vjp
def low(v):
    return lax.optimization_barrier(v.astype(jnp.bfloat16)).astype(jnp.float32)

@jax.custom_vjp
def low_back(v):
    return v

def low_keep(v):
    return (low(v), None)

def low_pass(kept, grad):
    return (grad,)

def back_keep(v):
    return (v, None)

def back_low(kept, grad):
    return (low(grad),)
low.defvjp(low_keep, low_pass)
low_back.defvjp(back_keep, back_low)
norm_eps = 1e-05
beta_one = 0.9
beta_two = 0.95
adam_eps = 1e-08
clip_limit = 1.0
ema_decay = 0.75
highest = lax.Precision.HIGHEST

def layer_norm(values, gain_row, shift_term):
    center = values - lax.optimization_barrier(jnp.mean(values, axis=-1, keepdims=True))
    spread = lax.optimization_barrier(jnp.mean(center * center, axis=-1, keepdims=True))
    return center * lax.rsqrt(spread + norm_eps) * gain_row + shift_term

def attention(queries, key_rows, value_rows, clip_rows, frame_rows):
    group_rows = queries.shape[0]
    block_rows = min(1024, group_rows)
    head_count = queries.shape[1]
    pad_keys = jnp.concatenate([jnp.zeros((CLIP, head_count, HEAD), key_rows.dtype), key_rows])
    pad_values = jnp.concatenate([jnp.zeros((CLIP, head_count, HEAD), value_rows.dtype), value_rows])
    pad_clips = jnp.concatenate([jnp.full((CLIP,), -1, jnp.int32), clip_rows.astype(jnp.int32)])
    pad_frames = jnp.concatenate([jnp.zeros((CLIP,), jnp.int32), frame_rows.astype(jnp.int32)])
    score_scale = HEAD ** (-0.5)

    def one_block(offset):
        query_block = lax.dynamic_slice_in_dim(queries, offset, block_rows, 0)
        key_block = lax.dynamic_slice_in_dim(pad_keys, offset, block_rows + CLIP, 0)
        value_block = lax.dynamic_slice_in_dim(pad_values, offset, block_rows + CLIP, 0)
        clip_query = lax.dynamic_slice_in_dim(clip_rows, offset, block_rows, 0)
        frame_query = lax.dynamic_slice_in_dim(frame_rows, offset, block_rows, 0)
        clip_keys = lax.dynamic_slice_in_dim(pad_clips, offset, block_rows + CLIP, 0)
        frame_keys = lax.dynamic_slice_in_dim(pad_frames, offset, block_rows + CLIP, 0)
        visible = (clip_query[:, None] == clip_keys[None, :]) & (frame_keys[None, :] <= frame_query[:, None])
        raw_scores = jnp.einsum('qhe,khe->hqk', query_block, key_block, precision=highest) * score_scale
        scores = jnp.where(visible[None], low_back(raw_scores), -1e+30)
        row_max = lax.optimization_barrier(jnp.max(scores, axis=-1, keepdims=True))
        weights = jnp.exp(scores - row_max)
        probs = weights / lax.optimization_barrier(jnp.sum(weights, axis=-1, keepdims=True))
        return jnp.einsum('hqk,khe->qhe', low(probs), value_block, precision=highest)
    starts = jnp.arange(group_rows // block_rows, dtype=jnp.int32) * block_rows
    outcome = lax.map(jax.checkpoint(one_block), starts)
    return outcome.reshape(group_rows, head_count * HEAD)

def forward(tokens, params, clip_rows, frame_rows):
    w_qkv, w_out, w_up, w_down, norm_params = params
    group_rows = tokens.shape[0]
    normed_one = low(layer_norm(tokens, norm_params[0], norm_params[1]))
    project = jnp.einsum('td,sdc->stc', normed_one, low(w_qkv), precision=highest)
    project = low_back(low(project)).reshape(3, group_rows, HEADS, HEAD)
    mixture = low_back(low(attention(project[0], project[1], project[2], clip_rows, frame_rows)))
    attended = low_back(jnp.dot(mixture, low(w_out), precision=highest))
    middle = tokens + attended
    normed_two = low(layer_norm(middle, norm_params[2], norm_params[3]))
    hidden = low_back(jnp.dot(normed_two, low(w_up), precision=highest))
    active = low(jax.nn.gelu(hidden))
    return middle + low_back(jnp.dot(active, low(w_down), precision=highest))

def adam_update(weight, gradient, moment, square, average, step_rate, decay_rate, factor, step_count):
    gradient = gradient * factor
    moment = beta_one * moment + (1.0 - beta_one) * gradient
    square = beta_two * square + (1.0 - beta_two) * gradient * gradient
    fixed_one = 1.0 - jnp.power(beta_one, step_count)
    fixed_two = 1.0 - jnp.power(beta_two, step_count)
    weight = weight - step_rate * (moment / fixed_one / (jnp.sqrt(square / fixed_two) + adam_eps) + decay_rate * weight)
    average = ema_decay * average + (1.0 - ema_decay) * weight
    return (weight, moment, square, average)

def reference(tokens, cotangent, clip_ids, frame_ids, step, w_qkv, w_out, w_up, w_down, norm_params, moment_qkv, moment_out, moment_up, moment_down, moment_norm, square_qkv, square_out, square_up, square_down, square_norm, average_qkv, average_out, average_up, average_down, average_norm):
    groups = tokens.shape[0] // TOK_GRP
    params = (w_qkv, w_out, w_up, w_down, norm_params)

    def one_group(totals, scan_items):
        token_rows, back_rows, clip_rows, frame_rows = scan_items

        def run_group(inputs, weights):
            return forward(inputs, weights, clip_rows, frame_rows)
        block_out, pullback = jax.vjp(run_group, token_rows.astype(jnp.float32), params)
        grad_rows, grad_params = pullback(back_rows.astype(jnp.float32))
        totals = jax.tree.map(jnp.add, totals, grad_params)
        return (totals, (block_out.astype(jnp.bfloat16), grad_rows))
    zero_grads = jax.tree.map(jnp.zeros_like, params)
    scan_input = (tokens.reshape(groups, TOK_GRP, D), cotangent.reshape(groups, TOK_GRP, D), clip_ids.reshape(groups, TOK_GRP), frame_ids.reshape(groups, TOK_GRP))
    totals, (block_out, grad_tokens) = lax.scan(one_group, zero_grads, scan_input)
    square_sum = sum((jnp.sum(grad_part * grad_part) for grad_part in totals))
    grad_norm = jnp.sqrt(square_sum)
    factor = jnp.minimum(1.0, clip_limit / (grad_norm + 1e-06))
    step_count = step[0].astype(jnp.float32)
    one = adam_update(w_qkv, totals[0], moment_qkv, square_qkv, average_qkv, 0.03, 0.1, factor, step_count)
    two = adam_update(w_out, totals[1], moment_out, square_out, average_out, 0.09, 0.1, factor, step_count)
    three = adam_update(w_up, totals[2], moment_up, square_up, average_up, 0.03, 0.1, factor, step_count)
    four = adam_update(w_down, totals[3], moment_down, square_down, average_down, 0.015, 0.1, factor, step_count)
    five = adam_update(norm_params, totals[4], moment_norm, square_norm, average_norm, 0.2, 0.0, factor, step_count)
    return (block_out.reshape(tokens.shape[0], D), grad_tokens.reshape(tokens.shape[0], D), grad_norm, one[0], two[0], three[0], four[0], five[0], one[1], two[1], three[1], four[1], five[1], one[2], two[2], three[2], four[2], five[2], one[0].astype(jnp.bfloat16), two[0].astype(jnp.bfloat16), three[0].astype(jnp.bfloat16), four[0].astype(jnp.bfloat16), one[3], two[3], three[3], four[3], five[3])
```

```python
import functools

import jax
import jax.numpy as jnp
from jax import lax
from jax.experimental import pallas as pl
from jax.experimental.pallas import tpu as pltpu
from jax.sharding import PartitionSpec as P

HEAD = 64
CLIP = 1024
FRAME = 64

norm_eps = 1e-05
beta_one = 0.9
beta_two = 0.95
adam_eps = 1e-08
clip_limit = 1.0
ema_decay = 0.75

F32 = jnp.float32
BF16 = jnp.bfloat16
BOTH = ("dp", "mp")
VMEM = pltpu.VMEM
MASKED = -1e30
TQ = 128
TK = 256
ROWS = 256


def mm(a, b):
    return lax.dot_general(a, b, (((1,), (0,)), ((), ())), preferred_element_type=F32)


def mm_nt(a, b):
    return lax.dot_general(a, b, (((1,), (1,)), ((), ())), preferred_element_type=F32)


def mm_tn(a, b):
    return lax.dot_general(a, b, (((0,), (0,)), ((), ())), preferred_element_type=F32)


def call(body, outs, ins, scratch=(), smem=0, flops=0, moved=0):
    return pl.pallas_call(
        body,
        out_shape=outs,
        in_specs=[pl.BlockSpec(memory_space=pltpu.SMEM)] * smem
        + [pl.BlockSpec(memory_space=VMEM)] * (len(ins) - smem),
        out_specs=jax.tree.map(lambda _: pl.BlockSpec(memory_space=VMEM), outs),
        scratch_shapes=list(scratch),
        compiler_params=pltpu.CompilerParams(vmem_limit_bytes=60 << 20),
        cost_estimate=pl.CostEstimate(flops=flops, bytes_accessed=moved, transcendentals=0),
    )(*ins)


def normalize(rows):
    center = rows - jnp.mean(rows, axis=-1, keepdims=True)
    inverse = lax.rsqrt(jnp.mean(center * center, axis=-1, keepdims=True) + norm_eps)
    return center * inverse, inverse


def norm_back(grad, xhat, inverse, gain_row):
    gy = grad * gain_row
    return inverse * (
        gy
        - jnp.mean(gy, axis=-1, keepdims=True)
        - xhat * jnp.mean(gy * xhat, axis=-1, keepdims=True)
    )


def project_body(own_ref, halo_ref, norm_ref, w_ref, q_ref, k_ref, v_ref, kt_ref, vt_ref, xn_ref):
    gain, shift = norm_ref[0:1, :], norm_ref[1:2, :]

    def rows_of(ref, tile, base, with_query):
        at = pl.ds(pl.multiple_of(tile * ROWS, ROWS), ROWS)
        to = pl.ds(pl.multiple_of(base + tile * ROWS, ROWS), ROWS)
        xhat, _ = normalize(ref[at, :].astype(F32))
        xn = (xhat * gain + shift).astype(BF16)
        xn_ref[to, :] = xn
        if with_query:
            q_ref[at, :] = (mm(xn, w_ref[0]).astype(BF16).astype(F32) * HEAD**-0.5).astype(BF16)
        k = mm(xn, w_ref[1])
        v = mm(xn, w_ref[2])
        k_ref[to, :] = k.astype(BF16)
        v_ref[to, :] = v.astype(BF16)
        kt_ref[:, to] = k.T.astype(BF16)
        vt_ref[:, to] = v.T.astype(BF16)

    @pl.loop(0, CLIP // ROWS)
    def _(tile):
        rows_of(halo_ref, tile, 0, False)

    @pl.loop(0, own_ref.shape[0] // ROWS)
    def _(tile):
        rows_of(own_ref, tile, CLIP, True)


def project(own, halo, norms, w_qkv):
    n, d = own.shape
    total = n + CLIP
    shape = jax.ShapeDtypeStruct
    return call(
        project_body,
        (
            shape((n, d), BF16),
            shape((total, d), BF16),
            shape((total, d), BF16),
            shape((d, total), BF16),
            shape((d, total), BF16),
            shape((total, d), BF16),
        ),
        (own, halo, norms, w_qkv),
        flops=2 * d * d * (2 * total + n),
        moved=2 * d * (6 * total + 3 * n),
    )


def split_heads(pair, rows):
    lane = lax.broadcasted_iota(jnp.int32, (rows, 2 * HEAD), 1)
    zero = jnp.zeros_like(pair)
    return jnp.concatenate([jnp.where(lane < HEAD, pair, zero), jnp.where(lane < HEAD, zero, pair)])


def seen(low_row, query_tile, key_tile):
    shape = (TK, 2 * TQ)
    key_frame = (key_tile * TK + lax.broadcasted_iota(jnp.int32, shape, 0)) // FRAME
    spot = lax.rem(lax.broadcasted_iota(jnp.int32, shape, 1), TQ)
    query_frame = (CLIP + query_tile * TQ + spot) // FRAME
    return (key_frame >= low_row) & (key_frame <= query_frame)


def attend_body(first_ref, low_ref, q_ref, k_ref, vt_ref, mix_ref, log_ref, qz, acc, top, total):
    pairs = q_ref.shape[1] // (2 * HEAD)

    @pl.loop(0, q_ref.shape[0] // TQ)
    def _(i):
        at = pl.ds(pl.multiple_of(i * TQ, TQ), TQ)
        low = low_ref[0:1, at]
        low = jnp.concatenate([low, low], axis=1)
        for p in range(pairs):
            qz[p] = split_heads(q_ref[at, p * 128 : (p + 1) * 128], TQ)
        acc[...] = jnp.zeros_like(acc)
        top[...] = jnp.full_like(top, MASKED)
        total[...] = jnp.zeros_like(total)

        def step(j, carry):
            keys = pl.ds(pl.multiple_of(j * TK, TK), TK)
            visible = seen(low, i, j)
            for p in range(pairs):
                lanes = slice(p * 128, (p + 1) * 128)
                scores = jnp.where(visible, mm_nt(k_ref[keys, lanes], qz[p]), MASKED)
                old = top[p]
                new = jnp.maximum(old, jnp.max(scores, axis=0, keepdims=True))
                weights = jnp.exp(scores - new)
                keep = jnp.exp(old - new)
                top[p] = new
                total[p] = total[p] * keep + jnp.sum(weights, axis=0, keepdims=True)
                low_weights = weights.astype(BF16)
                for h in range(2):
                    half = slice(h * HEAD, (h + 1) * HEAD)
                    wide = slice(h * TQ, (h + 1) * TQ)
                    values = vt_ref[p * 128 + h * HEAD : p * 128 + (h + 1) * HEAD, keys]
                    acc[p, half, :] = acc[p, half, :] * keep[:, wide] + mm(
                        values, low_weights[:, wide]
                    )
            return carry

        lax.fori_loop(first_ref[i], pl.cdiv(CLIP + (i + 1) * TQ, TK), step, 0)
        for p in range(pairs):
            sums = total[p]
            for h in range(2):
                half = slice(h * HEAD, (h + 1) * HEAD)
                wide = slice(h * TQ, (h + 1) * TQ)
                acc[p, half, :] = acc[p, half, :] / sums[:, wide]
                log_ref[2 * p + h : 2 * p + h + 1, at] = top[p][:, wide] + jnp.log(sums[:, wide])
            mix_ref[at, p * 128 : (p + 1) * 128] = acc[p].T.astype(BF16)


def attend(first, low, q, k, vt):
    n, d = q.shape
    pairs = d // 128
    return call(
        attend_body,
        (jax.ShapeDtypeStruct((n, d), BF16), jax.ShapeDtypeStruct((d // HEAD, n), F32)),
        (first, low, q, k, vt),
        scratch=(
            VMEM((pairs, 2 * TQ, 128), BF16),
            VMEM((pairs, 128, TQ), F32),
            VMEM((pairs, 1, 2 * TQ), F32),
            VMEM((pairs, 1, 2 * TQ), F32),
        ),
        smem=1,
        flops=8 * n * 1024 * d,
        moved=2 * d * (2 * n + 4 * k.shape[0]),
    )


def attend_back_body(
    first_ref, low_ref, q_ref, k_ref, v_ref, kt_ref, mix_ref, log_ref, grad_ref,
    dq_ref, dk_ref, dv_ref, qz, gz, acc, dk_acc, dv_acc,
):
    pairs = q_ref.shape[1] // (2 * HEAD)
    dk_acc[...] = jnp.zeros_like(dk_acc)
    dv_acc[...] = jnp.zeros_like(dv_acc)

    @pl.loop(0, q_ref.shape[0] // TQ)
    def _(i):
        at = pl.ds(pl.multiple_of(i * TQ, TQ), TQ)
        low = low_ref[0:1, at]
        low = jnp.concatenate([low, low], axis=1)
        logs, inners = [], []
        for p in range(pairs):
            lanes = slice(p * 128, (p + 1) * 128)
            grad = grad_ref[at, lanes]
            qz[p] = split_heads(q_ref[at, lanes], TQ)
            gz[p] = split_heads(grad, TQ)
            both = (grad.astype(F32) * mix_ref[at, lanes].astype(F32)).T
            inners.append(
                jnp.concatenate(
                    [
                        jnp.sum(both[:HEAD], axis=0, keepdims=True),
                        jnp.sum(both[HEAD:], axis=0, keepdims=True),
                    ],
                    axis=1,
                )
            )
            logs.append(
                jnp.concatenate(
                    [log_ref[2 * p : 2 * p + 1, at], log_ref[2 * p + 1 : 2 * p + 2, at]], axis=1
                )
            )
        acc[...] = jnp.zeros_like(acc)

        def step(j, carry):
            keys = pl.ds(pl.multiple_of(j * TK, TK), TK)
            visible = seen(low, i, j)
            for p in range(pairs):
                lanes = slice(p * 128, (p + 1) * 128)
                scores = jnp.where(visible, mm_nt(k_ref[keys, lanes], qz[p]), MASKED)
                probs = jnp.exp(scores - logs[p])
                grad_probs = mm_nt(v_ref[keys, lanes], gz[p])
                grad_scores = (probs * (grad_probs - inners[p])).astype(BF16)
                dv_acc[keys, lanes] += mm(probs.astype(BF16), gz[p])
                dk_acc[keys, lanes] += mm(grad_scores, qz[p])
                for h in range(2):
                    half = slice(h * HEAD, (h + 1) * HEAD)
                    wide = slice(h * TQ, (h + 1) * TQ)
                    rows = kt_ref[p * 128 + h * HEAD : p * 128 + (h + 1) * HEAD, keys]
                    acc[p, half, :] += mm(rows, grad_scores[:, wide])
            return carry

        lax.fori_loop(first_ref[i], pl.cdiv(CLIP + (i + 1) * TQ, TK), step, 0)
        for p in range(pairs):
            dq_ref[at, p * 128 : (p + 1) * 128] = (acc[p].T * HEAD**-0.5).astype(BF16)

    dk_ref[...] = dk_acc[...].astype(BF16)
    dv_ref[...] = dv_acc[...].astype(BF16)


def attend_back(first, low, q, k, v, kt, mixture, logs, grad):
    n, d = q.shape
    total = k.shape[0]
    pairs = d // 128
    shape = jax.ShapeDtypeStruct
    return call(
        attend_back_body,
        (shape((n, d), BF16), shape((total, d), BF16), shape((total, d), BF16)),
        (first, low, q, k, v, kt, mixture, logs, grad),
        scratch=(
            VMEM((pairs, 2 * TQ, 128), BF16),
            VMEM((pairs, 2 * TQ, 128), BF16),
            VMEM((pairs, 128, TQ), F32),
            VMEM((total, d), F32),
            VMEM((total, d), F32),
        ),
        smem=1,
        flops=20 * n * 1024 * d,
        moved=2 * d * (4 * n + 5 * total),
    )


def feed_body(
    x_ref, mix_ref, cot_ref, norm_ref, wo_ref, up_ref, down_ref,
    out_ref, gmix_ref, gmid_ref, low_ref, n2_ref, act_ref, gh_ref, gain_ref,
):
    gain, shift = norm_ref[2:3, :], norm_ref[3:4, :]
    ff = up_ref.shape[1]
    wide = min(512, ff)
    root = 0.7978845608028654
    gain_ref[...] = jnp.zeros_like(gain_ref)

    @pl.loop(0, x_ref.shape[0] // ROWS)
    def _(tile):
        at = pl.ds(pl.multiple_of(tile * ROWS, ROWS), ROWS)
        cot = cot_ref[at, :]
        middle = x_ref[at, :].astype(F32) + mm_nt(mix_ref[at, :], wo_ref[...])
        xhat, inverse = normalize(middle)
        n2 = (xhat * gain + shift).astype(BF16)
        n2_ref[at, :] = n2
        out = middle
        second = jnp.zeros_like(middle)
        for c in range(ff // wide):
            cols = slice(c * wide, (c + 1) * wide)
            hidden = mm(n2, up_ref[:, cols])
            square = hidden * hidden
            bent = jnp.tanh(root * hidden * (1.0 + 0.044715 * square))
            half = 0.5 * (1.0 + bent)
            active = (hidden * half).astype(BF16)
            slope = half + hidden * (0.5 * root) * (1.0 - bent * bent) * (
                1.0 + (3 * 0.044715) * square
            )
            act_ref[at, cols] = active
            out += mm_nt(active, down_ref[:, cols])
            gh = (mm(cot, down_ref[:, cols]) * slope).astype(BF16)
            gh_ref[at, cols] = gh
            second += mm_nt(gh, up_ref[:, cols])
        out_ref[at, :] = out.astype(BF16)
        gain_ref[0:1, :] += jnp.sum(second * xhat, axis=0, keepdims=True)
        gain_ref[1:2, :] += jnp.sum(second, axis=0, keepdims=True)
        gmid = cot.astype(F32) + norm_back(second, xhat, inverse, gain)
        gmid_ref[at, :] = gmid
        low = gmid.astype(BF16)
        low_ref[at, :] = low
        gmix_ref[at, :] = mm(low, wo_ref[...]).astype(BF16)


def feed(x, mixture, cot, norms, wo, up, down):
    n, d = x.shape
    ff = up.shape[1]
    shape = jax.ShapeDtypeStruct
    return call(
        feed_body,
        (
            shape((n, d), BF16),
            shape((n, d), BF16),
            shape((n, d), F32),
            shape((n, d), BF16),
            shape((n, d), BF16),
            shape((n, ff), BF16),
            shape((n, ff), BF16),
            shape((2, d), F32),
        ),
        (x, mixture, cot, norms, wo, up, down),
        flops=2 * n * d * (4 * ff + 2 * d),
        moved=2 * n * (9 * d + 2 * ff) + 4 * d * ff,
    )


def feed_weights_body(n2_ref, gh_ref, cot_ref, act_ref, low_ref, mix_ref, gup_ref, gdown_ref, gout_ref):
    ff = gh_ref.shape[1]
    wide = min(512, ff)
    for c in range(ff // wide):
        cols = slice(c * wide, (c + 1) * wide)
        gup_ref[:, cols] = mm_tn(n2_ref[...], gh_ref[:, cols]).astype(BF16)
        gdown_ref[:, cols] = mm_tn(cot_ref[...], act_ref[:, cols]).astype(BF16)
    gout_ref[...] = mm_tn(low_ref[...], mix_ref[...]).astype(BF16)


def feed_weights(n2, gh, cot, act, low, mixture):
    n, d = n2.shape
    ff = gh.shape[1]
    shape = jax.ShapeDtypeStruct
    return call(
        feed_weights_body,
        (shape((d, ff), BF16), shape((d, ff), BF16), shape((d, d), BF16)),
        (n2, gh, cot, act, low, mixture),
        flops=2 * n * d * (2 * ff + d),
        moved=2 * n * (4 * d + 2 * ff) + 4 * d * ff,
    )


def project_weights_body(xn_ref, dq_ref, dk_ref, dv_ref, g_ref):
    g_ref[0] = mm_tn(xn_ref[CLIP:, :], dq_ref[...]).astype(BF16)
    g_ref[1] = mm_tn(xn_ref[...], dk_ref[...]).astype(BF16)
    g_ref[2] = mm_tn(xn_ref[...], dv_ref[...]).astype(BF16)


def project_weights(xn, dq, dk, dv):
    n, d = dq.shape
    total = xn.shape[0]
    return call(
        project_weights_body,
        jax.ShapeDtypeStruct((3, d, d), BF16),
        (xn, dq, dk, dv),
        flops=2 * d * d * (2 * total + n),
        moved=2 * d * (3 * total + n) + 6 * d * d,
    )


def first_back_body(own_ref, halo_ref, norm_ref, w_ref, dq_ref, dk_ref, dv_ref, gmid_ref,
                    grad_ref, back_ref, gain_ref):
    gain = norm_ref[0:1, :]
    gain_ref[...] = jnp.zeros_like(gain_ref)

    def rows_of(ref, tile, base, own):
        at = pl.ds(pl.multiple_of(tile * ROWS, ROWS), ROWS)
        to = pl.ds(pl.multiple_of(base + tile * ROWS, ROWS), ROWS)
        first = mm_nt(dk_ref[to, :], w_ref[1]) + mm_nt(dv_ref[to, :], w_ref[2])
        if own:
            first += mm_nt(dq_ref[at, :], w_ref[0])
        xhat, inverse = normalize(ref[at, :].astype(F32))
        gain_ref[0:1, :] += jnp.sum(first * xhat, axis=0, keepdims=True)
        gain_ref[1:2, :] += jnp.sum(first, axis=0, keepdims=True)
        grad = norm_back(first, xhat, inverse, gain)
        if own:
            grad_ref[at, :] = gmid_ref[at, :] + grad
        else:
            back_ref[at, :] = grad.astype(BF16)

    @pl.loop(0, CLIP // ROWS)
    def _(tile):
        rows_of(halo_ref, tile, 0, False)

    @pl.loop(0, own_ref.shape[0] // ROWS)
    def _(tile):
        rows_of(own_ref, tile, CLIP, True)


def first_back(own, halo, norms, w_qkv, dq, dk, dv, gmid):
    n, d = own.shape
    total = n + CLIP
    shape = jax.ShapeDtypeStruct
    return call(
        first_back_body,
        (shape((n, d), F32), shape((CLIP, d), BF16), shape((2, d), F32)),
        (own, halo, norms, w_qkv, dq, dk, dv, gmid),
        flops=2 * d * d * (2 * total + n),
        moved=2 * d * (4 * total + 6 * n),
    )


class Grid:
    def __init__(self, dp, mp):
        self.dp, self.mp = dp, mp
        self.fast = (dp, mp) == (8, 4)

    def pairs(self, move):
        found = []
        for i in range(self.dp * self.mp):
            z, y, x, c = i >> 3, (i >> 2) & 1, (i >> 1) & 1, i & 1
            z, y, x, c = move(z, y, x, c)
            found.append((i, (((z * 2 + y) * 2 + x) * 2 + c)))
        return found

    def spot(self):
        dp, mp = lax.axis_index("dp"), lax.axis_index("mp")
        return dp // 2, dp % 2, mp // 2, mp % 2

    def along_z(self, value, k):
        return lax.ppermute(value, BOTH, self.pairs(lambda z, y, x, c: ((z + k) % 4, y, x, c)))

    def second(self, value):
        return lax.ppermute(
            value, BOTH,
            self.pairs(lambda z, y, x, c: (z, y ^ 1, x, c) if c else (z, y, x ^ 1, c)),
        )

    def third(self, value):
        return lax.ppermute(
            value, BOTH,
            self.pairs(lambda z, y, x, c: (z, y, x ^ 1, c) if c else (z, y ^ 1, x, c)),
        )

    def core(self, value):
        return lax.ppermute(value, BOTH, self.pairs(lambda z, y, x, c: (z, y, x, c ^ 1)))

    def slots(self):
        z, y, x, c = self.spot()
        s = jnp.arange(self.dp * self.mp, dtype=jnp.int32)
        oz, oy, ox, oc = s >> 3, (s >> 2) & 1, (s >> 1) & 1, s & 1
        fx, fy = ox ^ x, oy ^ y
        early = jnp.where(oc == 0, fx, fy)
        late = jnp.where(oc == 0, fy, fx)
        return (oc ^ c) * 16 + late * 8 + early * 4 + (oz - z) % 4

    def gather(self, block):
        near = jnp.stack([block] + [self.along_z(block, 4 - k) for k in (1, 2, 3)])
        near = jnp.concatenate([near, self.second(near)])
        near = jnp.concatenate([near, self.third(near)])
        return jnp.concatenate([near, self.core(near)])

    def scatter(self, blocks):
        def add(a, b):
            return (a.astype(F32) + b.astype(F32)).astype(BF16)

        held = add(blocks[:16], self.core(blocks[16:]))
        held = add(held[:8], self.third(held[8:]))
        held = add(held[:4], self.second(held[4:]))
        total = held[0].astype(F32)
        for k in (1, 2, 3):
            total += self.along_z(held[k], k).astype(F32)
        return total

    def total(self, value):
        for move in (
            lambda z, y, x, c: (z, y, x, c ^ 1),
            lambda z, y, x, c: (z, y, x ^ 1, c),
            lambda z, y, x, c: (z, y ^ 1, x, c),
            lambda z, y, x, c: (z ^ 1, y, x, c),
            lambda z, y, x, c: (z ^ 2, y, x, c),
        ):
            value = value + lax.ppermute(value, BOTH, self.pairs(move))
        return value


def whole_of(grid, block, slots):
    lead, (rows, cols) = block.shape[:-2], block.shape[-2:]
    if not grid.fast:
        half = lax.all_gather(block, "dp", axis=len(lead), tiled=True)
        return lax.all_gather(half, "mp", axis=len(lead) + 1, tiled=True)
    pieces = jnp.take(grid.gather(block), slots, axis=0)
    pieces = pieces.reshape((grid.dp, grid.mp) + lead + (rows, cols))
    m = len(lead)
    order = tuple(range(2, 2 + m)) + (0, 2 + m, 1, 3 + m)
    return pieces.transpose(order).reshape(lead + (grid.dp * rows, grid.mp * cols))


def share_of(grid, whole, slots):
    lead, (rows, cols) = whole.shape[:-2], whole.shape[-2:]
    m = len(lead)
    if not grid.fast:
        half = lax.psum_scatter(whole, "mp", scatter_dimension=m + 1, tiled=True)
        return lax.psum_scatter(half, "dp", scatter_dimension=m, tiled=True).astype(F32)
    blocks = whole.reshape(lead + (grid.dp, rows // grid.dp, grid.mp, cols // grid.mp))
    order = (m, m + 2) + tuple(range(m)) + (m + 1, m + 3)
    blocks = blocks.transpose(order)
    blocks = blocks.reshape((grid.dp * grid.mp,) + blocks.shape[2:])
    back = jnp.zeros_like(slots).at[slots].set(jnp.arange(slots.shape[0], dtype=jnp.int32))
    return grid.scatter(jnp.take(blocks, back, axis=0))


def adam_update(
    weight, gradient, moment, square, average, step_rate, decay_rate, factor, step_count
):
    gradient = gradient * factor
    moment = beta_one * moment + (1.0 - beta_one) * gradient
    square = beta_two * square + (1.0 - beta_two) * gradient * gradient
    fixed_one = 1.0 - jnp.power(beta_one, step_count)
    fixed_two = 1.0 - jnp.power(beta_two, step_count)
    weight = weight - step_rate * (
        moment / fixed_one / (jnp.sqrt(square / fixed_two) + adam_eps) + decay_rate * weight
    )
    average = ema_decay * average + (1.0 - ema_decay) * weight
    return (weight, moment, square, average)


def per_device(
    grid,
    tokens,
    cotangent,
    clip_ids,
    frame_ids,
    step,
    w_qkv,
    w_out,
    w_up,
    w_down,
    norm_params,
    moment_qkv,
    moment_out,
    moment_up,
    moment_down,
    moment_norm,
    square_qkv,
    square_out,
    square_up,
    square_down,
    square_norm,
    average_qkv,
    average_out,
    average_up,
    average_down,
    average_norm,
):
    n, d = tokens.shape
    back_steps = CLIP // n
    mp_index = lax.axis_index("mp")
    slots = grid.slots() if grid.fast else None

    def shifted(value, k):
        pairs = [(i, i + k) for i in range(grid.mp) if 0 <= i + k < grid.mp]
        return lax.ppermute(value, "mp", pairs)

    halo = jnp.concatenate([shifted(tokens, k) for k in range(back_steps, 0, -1)])
    full_qkv = whole_of(grid, w_qkv.astype(BF16), slots)
    full_out = whole_of(grid, w_out.T.astype(BF16), slots)
    full_up = whole_of(grid, w_up.astype(BF16), slots)
    full_down = whole_of(grid, w_down.T.astype(BF16), slots)

    frames = lax.dynamic_slice_in_dim(frame_ids, mp_index * n, n, 0)
    low = (CLIP + jnp.arange(n, dtype=jnp.int32)) // FRAME - frames
    first = low[::TQ] * FRAME // TK
    low = low.reshape(1, n)

    q, k, v, kt, vt, xn = project(tokens, halo, norm_params, full_qkv)
    mixture, logs = attend(first, low, q, k, vt)
    block_out, gmix, gmid, gmid_low, n2, act, gh, gains_two = feed(
        tokens, mixture, cotangent, norm_params, full_out, full_up, full_down
    )
    gup, gdown, gout = feed_weights(n2, gh, cotangent, act, gmid_low, mixture)
    grad_up = share_of(grid, gup, slots)
    grad_down = share_of(grid, gdown, slots)
    grad_out = share_of(grid, gout, slots)
    dq, dk, dv = attend_back(first, low, q, k, v, kt, mixture, logs, gmix)
    grad_qkv = share_of(grid, project_weights(xn, dq, dk, dv), slots)
    grad_rows, back, gains_one = first_back(
        tokens, halo, norm_params, full_qkv, dq, dk, dv, gmid
    )
    grad_tokens = grad_rows
    for i, hop in enumerate(range(back_steps, 0, -1)):
        grad_tokens = grad_tokens + shifted(back[i * n : (i + 1) * n], -hop).astype(F32)

    def total(value):
        return grid.total(value) if grid.fast else lax.psum(value, BOTH)

    gain_grads = total(jnp.concatenate([gains_one, gains_two]))
    weight_square = (
        jnp.sum(grad_qkv * grad_qkv)
        + jnp.sum(grad_out * grad_out)
        + jnp.sum(grad_up * grad_up)
        + jnp.sum(grad_down * grad_down)
    )
    square_sum = total(jnp.broadcast_to(weight_square, (8, 128)))[0, 0] + jnp.sum(
        gain_grads * gain_grads
    )
    norm_value = jnp.sqrt(square_sum)
    factor = jnp.minimum(1.0, clip_limit / (norm_value + 1e-06))
    step_count = step[0].astype(F32)
    one = adam_update(
        w_qkv, grad_qkv, moment_qkv, square_qkv, average_qkv, 0.03, 0.1, factor, step_count
    )
    two = adam_update(
        w_out, grad_out.T, moment_out, square_out, average_out, 0.09, 0.1, factor, step_count
    )
    three = adam_update(
        w_up, grad_up, moment_up, square_up, average_up, 0.03, 0.1, factor, step_count
    )
    four = adam_update(
        w_down, grad_down.T, moment_down, square_down, average_down, 0.015, 0.1, factor, step_count
    )
    five = adam_update(
        norm_params,
        gain_grads,
        moment_norm,
        square_norm,
        average_norm,
        0.2,
        0.0,
        factor,
        step_count,
    )
    sets = (one, two, three, four, five)
    return (
        (block_out, grad_tokens, norm_value)
        + tuple(s[0] for s in sets)
        + tuple(s[1] for s in sets)
        + tuple(s[2] for s in sets)
        + tuple(s[0].astype(BF16) for s in sets[:4])
        + tuple(s[3] for s in sets)
    )


def solution(mesh):
    rows = P(BOTH, None)
    weights = (P(None, "dp", "mp"), P("mp", "dp"), P("dp", "mp"), P("mp", "dp"))
    states = weights + (P(),)
    return jax.shard_map(
        functools.partial(per_device, Grid(mesh.shape["dp"], mesh.shape["mp"])),
        mesh=mesh,
        in_specs=(rows, rows, P("dp"), P("dp"), P()) + states * 4,
        out_specs=(rows, rows, P()) + states * 3 + weights + states,
        check_vma=False,
    )
```

```python
import functools

import jax
import jax.numpy as jnp
from jax import lax
from jax.experimental import pallas as pl
from jax.experimental.pallas import tpu as pltpu
from jax.sharding import PartitionSpec as P

HEAD = 64
CLIP = 1024
FRAME = 64

norm_eps = 1e-05
beta_one = 0.9
beta_two = 0.95
adam_eps = 1e-08
clip_limit = 1.0
ema_decay = 0.75

F32 = jnp.float32
BF16 = jnp.bfloat16
BOTH = ("dp", "mp")
VMEM = pltpu.VMEM
MASKED = -1e30
PAIR = 2 * HEAD
TQ = 256
TK = 256
ROWS = 256


def mm(a, b):
    return lax.dot_general(a, b, (((1,), (0,)), ((), ())), preferred_element_type=F32)


def mm_nt(a, b):
    return lax.dot_general(a, b, (((1,), (1,)), ((), ())), preferred_element_type=F32)


def mm_tn(a, b):
    return lax.dot_general(a, b, (((0,), (0,)), ((), ())), preferred_element_type=F32)


def shape(dims, kind):
    return jax.ShapeDtypeStruct(tuple(dims), kind)


def call(body, outs, smem, ins, far=(), scratch=(), flops=0, moved=0, room=60, loose=()):
    return pl.pallas_call(
        body,
        out_shape=outs,
        in_specs=[pl.BlockSpec(memory_space=pltpu.SMEM)] * len(smem)
        + [pl.BlockSpec(memory_space=VMEM)] * len(ins)
        + [pl.BlockSpec(memory_space=pl.ANY)] * len(far),
        out_specs=tuple(
            pl.BlockSpec(memory_space=pl.ANY if i in loose else VMEM) for i in range(len(outs))
        ),
        scratch_shapes=list(scratch),
        compiler_params=pltpu.CompilerParams(vmem_limit_bytes=room << 20),
        cost_estimate=pl.CostEstimate(
            flops=int(flops), bytes_accessed=int(moved), transcendentals=0
        ),
    )(*smem, *ins, *far)


def rows_at(tile, base=0):
    return pl.ds(pl.multiple_of(base + tile * ROWS, ROWS), ROWS)


def normalize(rows):
    center = rows - jnp.mean(rows, axis=-1, keepdims=True)
    inverse = lax.rsqrt(jnp.mean(center * center, axis=-1, keepdims=True) + norm_eps)
    return center * inverse, inverse


def norm_back(grad, xhat, inverse, gain_row):
    gy = grad * gain_row
    return inverse * (
        gy
        - jnp.mean(gy, axis=-1, keepdims=True)
        - xhat * jnp.mean(gy * xhat, axis=-1, keepdims=True)
    )


def place(spots_ref, far, sems, parts):
    copies = []
    for s in range(32):
        row, col = spots_ref[s] // 4, spots_ref[s] % 4
        for t, (start, wide, whole) in enumerate(parts):
            block = far[s // 4].at[s % 4]
            rows = block.shape[-2]
            at = (
                pl.ds(pl.multiple_of(row * rows, rows), rows),
                pl.ds(pl.multiple_of(col * wide, wide), wide),
            )
            lead = (slice(None),) * (len(block.shape) - 2)
            copies.append(
                pltpu.make_async_copy(
                    block.at[lead + (slice(None), pl.ds(start, wide))],
                    whole.at[lead + at],
                    sems.at[s * len(parts) + t],
                )
            )
    for copy in copies:
        copy.start()
    return copies


def project_body(fast, first_ref, *refs):
    if fast:
        spots_ref, own_ref, halo_ref, norm_ref = refs[:4]
        far, refs = refs[4:12], refs[12:]
        q_ref, k_ref, v_ref, vt_ref, w_ref, sems = refs
        for copy in place(spots_ref, far, sems, [(0, far[0].shape[-1], w_ref)]):
            copy.wait()
    else:
        own_ref, halo_ref, norm_ref, w_ref, q_ref, k_ref, v_ref, vt_ref = refs
    gain, shift = norm_ref[0:1, :], norm_ref[1:2, :]

    def rows_of(ref, tile, base, own):
        at, to = rows_at(tile), rows_at(tile, base)
        xhat, _ = normalize(ref[at, :].astype(F32))
        xn = (xhat * gain + shift).astype(BF16)
        if own:
            q = mm(xn, w_ref[0]).astype(BF16).astype(F32)
            q_ref[at, :] = (q * HEAD**-0.5).astype(BF16)
        k_ref[to, :] = mm(xn, w_ref[1]).astype(BF16)
        v = mm(xn, w_ref[2])
        v_ref[to, :] = v.astype(BF16)
        vt_ref[:, to] = v.T.astype(BF16)

    @pl.loop(jnp.minimum(first_ref[0], CLIP // ROWS), CLIP // ROWS)
    def _(tile):
        rows_of(halo_ref, tile, 0, False)

    @pl.loop(0, own_ref.shape[0] // ROWS)
    def _(tile):
        rows_of(own_ref, tile, CLIP, True)


def project(first, own, halo, norms, w_qkv, spots=None, far=()):
    n, d = own.shape
    total = n + CLIP
    fast = len(far) > 0
    outs = (
        shape((n, d), BF16),
        shape((total, d), BF16),
        shape((total, d), BF16),
        shape((d, total), BF16),
    )
    if fast:
        outs += (shape((3, d, d), BF16),)
    return call(
        functools.partial(project_body, fast),
        outs,
        (first, spots) if fast else (first,),
        (own, halo, norms) + (() if fast else (w_qkv,)),
        far,
        (pltpu.SemaphoreType.DMA((32,)),) if fast else (),
        flops=2 * d * d * (2 * total + n),
        moved=2 * d * (4 * total + 2 * n) + 6 * d * d,
        room=32,
    )


def split_heads(pair):
    lane = lax.broadcasted_iota(jnp.int32, pair.shape, 1)
    zero = jnp.zeros_like(pair)
    return jnp.concatenate([jnp.where(lane < HEAD, pair, zero), jnp.where(lane < HEAD, zero, pair)])


def twice(row):
    return jnp.concatenate([row, row], axis=1)


def sight(low_ref, at, i):
    spot = lax.broadcasted_iota(jnp.int32, (1, TQ), 1)
    last = ((CLIP + i * TQ) + spot) >> 6
    frame = lax.broadcasted_iota(jnp.int32, (TK, 2 * TQ), 0) >> 6
    return twice(low_ref[0:1, at]), twice(last), frame


def attend_body(
    first_ref, low_ref, q_ref, k_ref, vt_ref, mix_ref, log_ref, qt, acc, top, total, s_ref, p_ref
):
    pairs = q_ref.shape[1] // PAIR

    @pl.loop(0, q_ref.shape[0] // TQ)
    def _(i):
        at = pl.ds(pl.multiple_of(i * TQ, TQ), TQ)
        low, last, frame = sight(low_ref, at, i)
        for p in range(pairs):
            qt[p] = split_heads(q_ref[at, p * PAIR : (p + 1) * PAIR]).T
        acc[...] = jnp.zeros_like(acc)
        top[...] = jnp.full_like(top, MASKED)
        total[...] = jnp.zeros_like(total)

        def step(j, carry):
            keys = pl.ds(pl.multiple_of(j * TK, TK), TK)
            shift = j * (TK // FRAME)
            visible = (frame >= low - shift) & (frame <= last - shift)
            for p in range(pairs):
                scores = mm(k_ref[keys, p * PAIR : (p + 1) * PAIR], qt[p])
                s_ref[p] = jnp.where(visible, scores, MASKED)
            for p in range(pairs):
                scores = s_ref[p]
                old = top[p]
                new = jnp.maximum(old, jnp.max(scores, axis=0, keepdims=True))
                weights = jnp.exp(scores - new)
                keep = jnp.exp(old - new)
                top[p] = new
                total[p] = total[p] * keep + jnp.sum(weights, axis=0, keepdims=True)
                p_ref[p] = weights.astype(BF16)
                for h in range(2):
                    part = slice(h * HEAD, (h + 1) * HEAD)
                    acc[p, part, :] = acc[p, part, :] * keep[:, h * TQ : (h + 1) * TQ]
            for p in range(pairs):
                for h in range(2):
                    part = slice(h * HEAD, (h + 1) * HEAD)
                    values = vt_ref[p * PAIR + h * HEAD : p * PAIR + (h + 1) * HEAD, keys]
                    acc[p, part, :] += mm(values, p_ref[p, :, h * TQ : (h + 1) * TQ])
            return carry

        lax.fori_loop(first_ref[i], (CLIP + (i + 1) * TQ + TK - 1) // TK, step, 0)
        for p in range(pairs):
            sums = total[p]
            logs = top[p] + jnp.log(sums)
            inverse = 1.0 / sums
            for h in range(2):
                part = slice(h * HEAD, (h + 1) * HEAD)
                wide = slice(h * TQ, (h + 1) * TQ)
                acc[p, part, :] = acc[p, part, :] * inverse[:, wide]
                log_ref[2 * p + h : 2 * p + h + 1, at] = logs[:, wide]
            mix_ref[at, p * PAIR : (p + 1) * PAIR] = acc[p].T.astype(BF16)


def attend(first, low, q, k, vt):
    n, d = q.shape
    pairs = d // PAIR
    return call(
        attend_body,
        (shape((n, d), BF16), shape((d // HEAD, n), F32)),
        (first,),
        (low, q, k, vt),
        scratch=(
            VMEM((pairs, PAIR, 2 * TQ), BF16),
            VMEM((pairs, PAIR, TQ), F32),
            VMEM((pairs, 1, 2 * TQ), F32),
            VMEM((pairs, 1, 2 * TQ), F32),
            VMEM((pairs, TK, 2 * TQ), F32),
            VMEM((pairs, TK, 2 * TQ), BF16),
        ),
        flops=16 * n * 1024 * d,
        moved=2 * d * (2 * n + 2 * k.shape[0]),
        room=32,
    )


def put_blocks(slots_ref, m, grad, rows, put):
    for r in range(8):
        put(slots_ref[r * 4 + m] & 15, grad[r * rows : (r + 1) * rows])


def attend_back_body(fast, first_ref, *refs):
    if fast:
        slots_ref, side_ref, refs = refs[0], refs[1], refs[2:]
    (
        low_ref, q_ref, k_ref, v_ref, mix_ref, log_ref, grad_ref, own_ref, halo_ref, norm_ref,
        dq_ref, dk_ref, dv_ref,
    ) = refs[:13]
    outs, refs = refs[13 : 15 if fast else 14], refs[15 if fast else 14 :]
    kt_ref, xt_ref, qz, gz, qt, gt, acc, dk_acc, dv_acc, s_ref, d_ref, p_ref, ds_ref, rows_ref, g_acc = refs
    n, d = q_ref.shape
    pairs = d // PAIR
    start = first_ref[0]
    tiles = k_ref.shape[0] // ROWS
    gain, shift_row = norm_ref[0:1, :], norm_ref[1:2, :]

    def prepare(ref, tile, base):
        to = rows_at(tile, base)
        kt_ref[:, to] = k_ref[to, :].T
        xhat, _ = normalize(ref[rows_at(tile), :].astype(F32))
        xt_ref[:, to] = (xhat * gain + shift_row).T.astype(BF16)
        dk_acc[to, :] = jnp.zeros((ROWS, d), F32)
        dv_acc[to, :] = jnp.zeros((ROWS, d), F32)

    @pl.loop(jnp.minimum(start, CLIP // ROWS), CLIP // ROWS)
    def _(tile):
        prepare(halo_ref, tile, 0)

    @pl.loop(0, n // ROWS)
    def _(tile):
        prepare(own_ref, tile, CLIP)

    @pl.loop(0, n // TQ)
    def _(i):
        at = pl.ds(pl.multiple_of(i * TQ, TQ), TQ)
        low, last, frame = sight(low_ref, at, i)
        for p in range(pairs):
            lanes = slice(p * PAIR, (p + 1) * PAIR)
            grad = grad_ref[at, lanes]
            query_two, grad_two = split_heads(q_ref[at, lanes]), split_heads(grad)
            qz[p] = query_two
            gz[p] = grad_two
            qt[p] = query_two.T
            gt[p] = grad_two.T
            both = (grad.astype(F32) * mix_ref[at, lanes].astype(F32)).T
            for h in range(2):
                wide = slice(h * TQ, (h + 1) * TQ)
                rows_ref[p, 0:1, wide] = jnp.sum(
                    both[h * HEAD : (h + 1) * HEAD], axis=0, keepdims=True
                )
                rows_ref[p, 1:2, wide] = log_ref[2 * p + h : 2 * p + h + 1, at]
        acc[...] = jnp.zeros_like(acc)

        def step(j, carry):
            keys = pl.ds(pl.multiple_of(j * TK, TK), TK)
            shift = j * (TK // FRAME)
            visible = (frame >= low - shift) & (frame <= last - shift)
            for p in range(pairs):
                lanes = slice(p * PAIR, (p + 1) * PAIR)
                s_ref[p] = jnp.where(visible, mm(k_ref[keys, lanes], qt[p]), MASKED)
                d_ref[p] = mm(v_ref[keys, lanes], gt[p])
            for p in range(pairs):
                probs = jnp.exp(s_ref[p] - rows_ref[p, 1:2, :])
                p_ref[p] = probs.astype(BF16)
                ds_ref[p] = (probs * (d_ref[p] - rows_ref[p, 0:1, :])).astype(BF16)
            for p in range(pairs):
                lanes = slice(p * PAIR, (p + 1) * PAIR)
                dv_acc[keys, lanes] += mm(p_ref[p], gz[p])
                dk_acc[keys, lanes] += mm(ds_ref[p], qz[p])
                for h in range(2):
                    part = slice(h * HEAD, (h + 1) * HEAD)
                    rows = kt_ref[p * PAIR + h * HEAD : p * PAIR + (h + 1) * HEAD, keys]
                    acc[p, part, :] += mm(rows, ds_ref[p, :, h * TQ : (h + 1) * TQ])
            return carry

        lax.fori_loop(first_ref[i], (CLIP + (i + 1) * TQ + TK - 1) // TK, step, 0)
        for p in range(pairs):
            dq_ref[at, p * PAIR : (p + 1) * PAIR] = (acc[p].T * HEAD**-0.5).astype(BF16)

    @pl.loop(jnp.minimum(start, CLIP // ROWS), tiles)
    def _(tile):
        dk_ref[rows_at(tile), :] = dk_acc[rows_at(tile), :].astype(BF16)
        dv_ref[rows_at(tile), :] = dv_acc[rows_at(tile), :].astype(BF16)

    wide = g_acc.shape[2]

    def weights(m, put):
        cols = pl.ds(pl.multiple_of(m * wide, wide), wide)
        g_acc[0] = mm(xt_ref[:, CLIP:], dq_ref[:, cols])
        for s, grads in ((1, dk_ref), (2, dv_ref)):
            g_acc[s] = mm(xt_ref[:, CLIP:], grads[CLIP:, cols])

        @pl.loop(jnp.minimum(start, CLIP // ROWS), CLIP // ROWS)
        def _(tile):
            for s, grads in ((1, dk_ref), (2, dv_ref)):
                g_acc[s] += mm(xt_ref[:, rows_at(tile)], grads[rows_at(tile), cols])

        put(m)

    if not fast:
        for m in range(d // wide):

            def put(m):
                outs[0][:, :, m * wide : (m + 1) * wide] = g_acc[...].astype(BF16)

            weights(m, put)
        return
    rows = d // 8
    for side in range(2):
        for x in range(2):

            def put(m, out=outs[side]):
                for r in range(8):
                    slot = slots_ref[r * 4 + m] & 15
                    out[slot] = g_acc[:, r * rows : (r + 1) * rows, :].astype(BF16)

            weights(2 * x + side_ref[side], put)


def attend_back(first, low, q, k, v, mixture, logs, grad, own, halo, norms, slots=None, side=None):
    n, d = q.shape
    total = k.shape[0]
    pairs = d // PAIR
    fast = slots is not None
    outs = (shape((n, d), BF16), shape((total, d), BF16), shape((total, d), BF16))
    if fast:
        outs += (shape((16, 3, d // 8, d // 4), BF16),) * 2
    else:
        outs += (shape((3, d, d), BF16),)
    return call(
        functools.partial(attend_back_body, fast),
        outs,
        (first, slots, side) if fast else (first,),
        (low, q, k, v, mixture, logs, grad, own, halo, norms),
        scratch=(
            VMEM((d, total), BF16),
            VMEM((d, total), BF16),
            VMEM((pairs, 2 * TQ, PAIR), BF16),
            VMEM((pairs, 2 * TQ, PAIR), BF16),
            VMEM((pairs, PAIR, 2 * TQ), BF16),
            VMEM((pairs, PAIR, 2 * TQ), BF16),
            VMEM((pairs, PAIR, TQ), F32),
            VMEM((total, d), F32),
            VMEM((total, d), F32),
            VMEM((pairs, TK, 2 * TQ), F32),
            VMEM((pairs, TK, 2 * TQ), F32),
            VMEM((pairs, TK, 2 * TQ), BF16),
            VMEM((pairs, TK, 2 * TQ), BF16),
            VMEM((pairs, 8, 2 * TQ), F32),
            VMEM((3, d, d // 4), F32),
        ),
        flops=40 * n * 1024 * d,
        moved=2 * d * (4 * n + 4 * total),
        room=56,
    )


def feed_body(fast, *refs):
    if fast:
        spots_ref, slots_ref, side_ref, x_ref, mix_ref, cot_ref, norm_ref = refs[:7]
        far, refs = refs[7:15], refs[15:]
        out_ref, gmix_ref, gmid_ref, gain_ref = refs[:4]
        outs, refs = refs[4:6], refs[6:]
        wo_ref, up_ref, down_ref, sems = refs[:4]
        refs = refs[4:]
        one, ff = wo_ref.shape[1] // 4, up_ref.shape[1] // 4
        copies = place(
            spots_ref, far, sems,
            [(0, one, wo_ref), (one, ff, up_ref), (one + ff, ff, down_ref)],
        )
        for copy in copies:
            copy.wait()
    else:
        x_ref, mix_ref, cot_ref, norm_ref, wo_ref, up_ref, down_ref = refs[:7]
        out_ref, gmix_ref, gmid_ref, gain_ref = refs[7:11]
        outs, refs = refs[11:14], refs[14:]
    act_ref, gh_ref, n2t_ref, lowt_ref, cott_ref = refs
    gain, shift = norm_ref[2:3, :], norm_ref[3:4, :]
    ff = up_ref.shape[1]
    d = x_ref.shape[1]
    wide = min(512, ff)
    root = 0.7978845608028654
    gain_ref[...] = jnp.zeros_like(gain_ref)

    @pl.loop(0, x_ref.shape[0] // ROWS)
    def _(tile):
        at = rows_at(tile)
        cot = cot_ref[at, :]
        cott_ref[:, at] = cot.T
        middle = x_ref[at, :].astype(F32) + mm_nt(mix_ref[at, :], wo_ref[...])
        xhat, inverse = normalize(middle)
        n2 = xhat * gain + shift
        n2t_ref[:, at] = n2.T.astype(BF16)
        n2 = n2.astype(BF16)
        out = middle
        second = jnp.zeros_like(middle)
        for c in range(ff // wide):
            cols = slice(c * wide, (c + 1) * wide)
            hidden = mm(n2, up_ref[:, cols])
            square = hidden * hidden
            bent = jnp.tanh(hidden * (root + (root * 0.044715) * square))
            half = 0.5 + 0.5 * bent
            active = (hidden * half).astype(BF16)
            slope = half + hidden * (1.0 - bent * bent) * (
                0.5 * root + (0.5 * root * 3 * 0.044715) * square
            )
            act_ref[at, cols] = active
            out += mm_nt(active, down_ref[:, cols])
            gh = (mm(cot, down_ref[:, cols]) * slope).astype(BF16)
            gh_ref[at, cols] = gh
            second += mm_nt(gh, up_ref[:, cols])
        out_ref[at, :] = out.astype(BF16)
        gain_ref[0:1, :] += jnp.sum(second * xhat, axis=0, keepdims=True)
        gain_ref[1:2, :] += jnp.sum(second, axis=0, keepdims=True)
        gmid = cot.astype(F32) + norm_back(second, xhat, inverse, gain)
        gmid_ref[at, :] = gmid
        lowt_ref[:, at] = gmid.T.astype(BF16)
        gmix_ref[at, :] = mm(gmid.astype(BF16), wo_ref[...]).astype(BF16)

    if not fast:
        gup_ref, gdown_ref, gout_ref = outs
        for c in range(ff // wide):
            cols = slice(c * wide, (c + 1) * wide)
            gup_ref[:, cols] = mm(n2t_ref[...], gh_ref[:, cols]).astype(BF16)
            gdown_ref[:, cols] = mm(cott_ref[...], act_ref[:, cols]).astype(BF16)
        gout_ref[...] = mm(lowt_ref[...], mix_ref[...]).astype(BF16)
        return
    one, wide, rows = d // 4, ff // 4, d // 8
    for side in range(2):
        for x in range(2):
            m = 2 * x + side_ref[side]
            cols = pl.ds(pl.multiple_of(m * wide, wide), wide)
            small = pl.ds(pl.multiple_of(m * one, one), one)
            spots = [slots_ref[r * 4 + m] & 15 for r in range(8)]
            for start, size, left, right in (
                (0, one, lowt_ref, mix_ref[:, small]),
                (one, wide, n2t_ref, gh_ref[:, cols]),
                (one + wide, wide, cott_ref, act_ref[:, cols]),
            ):
                grad = mm(left[...], right).astype(BF16)
                for r in range(8):
                    outs[side][spots[r], :, start : start + size] = grad[r * rows : (r + 1) * rows]


def feed(x, mixture, cot, norms, full, ff, spots=None, slots=None, side=None, far=()):
    n, d = x.shape
    fast = len(far) > 0
    outs = (shape((n, d), BF16), shape((n, d), BF16), shape((n, d), F32), shape((2, d), F32))
    if fast:
        outs += (shape((16, d // 8, d // 4 + ff // 2), BF16),) * 2
    else:
        outs += (shape((d, ff), BF16), shape((d, ff), BF16), shape((d, d), BF16))
    return call(
        functools.partial(feed_body, fast),
        outs,
        (spots, slots, side) if fast else (),
        (x, mixture, cot, norms) + (() if fast else tuple(full)),
        far,
        (
            (
                VMEM((d, d), BF16),
                VMEM((d, ff), BF16),
                VMEM((d, ff), BF16),
                pltpu.SemaphoreType.DMA((96,)),
            )
            if fast
            else ()
        )
        + (
            VMEM((n, ff), BF16),
            VMEM((n, ff), BF16),
            VMEM((d, n), BF16),
            VMEM((d, n), BF16),
            VMEM((d, n), BF16),
        ),
        flops=2 * n * d * (6 * ff + 3 * d),
        moved=2 * n * 6 * d + 8 * d * ff,
        room=56,
    )


def first_back_body(
    first_ref, own_ref, halo_ref, norm_ref, w_ref, gmid_ref, dq_ref, dk_ref, dv_ref,
    grad_ref, back_ref, gain_ref,
):
    gain = norm_ref[0:1, :]
    gain_ref[...] = jnp.zeros_like(gain_ref)
    start = jnp.minimum(first_ref[0], CLIP // ROWS)

    def rows_of(ref, tile, base, own):
        at, to = rows_at(tile), rows_at(tile, base)
        first = mm_nt(dk_ref[to, :], w_ref[1]) + mm_nt(dv_ref[to, :], w_ref[2])
        if own:
            first += mm_nt(dq_ref[at, :], w_ref[0])
        xhat, inverse = normalize(ref[at, :].astype(F32))
        gain_ref[0:1, :] += jnp.sum(first * xhat, axis=0, keepdims=True)
        gain_ref[1:2, :] += jnp.sum(first, axis=0, keepdims=True)
        grad = norm_back(first, xhat, inverse, gain)
        if own:
            grad_ref[at, :] = gmid_ref[at, :] + grad
        else:
            back_ref[at, :] = grad.astype(BF16)

    @pl.loop(0, start)
    def _(tile):
        back_ref[rows_at(tile), :] = jnp.zeros((ROWS, back_ref.shape[1]), BF16)

    @pl.loop(start, CLIP // ROWS)
    def _(tile):
        rows_of(halo_ref, tile, 0, False)

    @pl.loop(0, own_ref.shape[0] // ROWS)
    def _(tile):
        rows_of(own_ref, tile, CLIP, True)


def first_back(first, own, halo, norms, w_qkv, gmid, dq, dk, dv):
    n, d = own.shape
    total = n + CLIP
    return call(
        first_back_body,
        (shape((n, d), F32), shape((CLIP, d), BF16), shape((2, d), F32)),
        (first,),
        (own, halo, norms, w_qkv, gmid, dq, dk, dv),
        flops=2 * d * d * (2 * total + n),
        moved=2 * d * (4 * total + 6 * n),
        room=32,
    )


class Grid:
    def __init__(self, dp, mp):
        self.dp, self.mp = dp, mp
        self.fast = (dp, mp) == (8, 4)

    def swap(self, value, z=0, y=0, x=0, c=0, swapped=False):
        pairs = []
        for i in range(self.dp * self.mp):
            dy, dx = (x, y) if swapped and i & 1 else (y, x)
            pairs.append((i, i ^ (z * 8 + dy * 4 + dx * 2 + c)))
        return lax.ppermute(value, BOTH, pairs)

    def early(self, value):
        return self.swap(value, x=1, swapped=True)

    def late(self, value):
        return self.swap(value, y=1, swapped=True)

    def spot(self):
        dp, mp = lax.axis_index("dp"), lax.axis_index("mp")
        return dp // 2, dp % 2, mp // 2, mp % 2

    def slots(self):
        z, y, x, c = self.spot()
        s = jnp.arange(32, dtype=jnp.int32)
        oz, oy, ox, oc = s >> 3, (s >> 2) & 1, (s >> 1) & 1, s & 1
        fx, fy = ox ^ x, oy ^ y
        return (
            (oc ^ c) * 16
            + jnp.where(oc == 0, fy, fx) * 8
            + jnp.where(oc == 0, fx, fy) * 4
            + (oz ^ z)
        )

    def spots(self):
        z, y, x, c = self.spot()
        s = jnp.arange(32, dtype=jnp.int32)
        oc, late, early, oz = (s >> 4) ^ c, (s >> 3) & 1, (s >> 2) & 1, (s & 3) ^ z
        oy = y ^ jnp.where(oc == 0, late, early)
        ox = x ^ jnp.where(oc == 0, early, late)
        return ((oz * 2 + oy) * 2 + ox) * 2 + oc

    def sides(self):
        c = lax.axis_index("mp") % 2
        return jnp.stack([c, 1 - c]).astype(jnp.int32)

    def gather_z(self, block):
        return jnp.stack([block] + [self.swap(block, z=k) for k in (1, 2, 3)])

    def across(self, held):
        return tuple(self.swap(a, c=1) for a in held)

    def scatter_core(self, sent):
        return self.swap(sent, c=1)

    def scatter_late(self, kept, got):
        return added(kept[:8], got[:8]), self.late(added(kept[8:], got[8:]))

    def scatter_early(self, kept, got):
        return added(kept[:4], got[:4]), self.early(added(kept[4:], got[4:]))

    def scatter_z(self, kept, got):
        parts = [added(kept[k], got[k]) for k in range(4)]
        near = [parts[0]] + [self.swap(parts[k], z=k) for k in (1, 2, 3)]
        near = [a.astype(F32) for a in near]
        return (near[0] + near[1]) + (near[2] + near[3])

    def total(self, value):
        value = value + self.swap(value, c=1)
        x, y, xy = (self.swap(value, x=a, y=b) for a, b in ((1, 0), (0, 1), (1, 1)))
        value = (value + x) + (y + xy)
        one, two, three = (self.swap(value, z=k) for k in (1, 2, 3))
        return (value + one) + (two + three)


def added(a, b):
    return (a.astype(F32) + b.astype(F32)).astype(BF16)


def whole_of(block):
    m = block.ndim - 2
    half = lax.all_gather(block, "dp", axis=m, tiled=True)
    return lax.all_gather(half, "mp", axis=m + 1, tiled=True)


def share_of(whole):
    m = whole.ndim - 2
    half = lax.psum_scatter(whole, "mp", scatter_dimension=m + 1, tiled=True)
    return lax.psum_scatter(half, "dp", scatter_dimension=m, tiled=True).astype(F32)


def after(value, *others):
    return lax.optimization_barrier((value,) + others)[0]


def joined(*values):
    return lax.optimization_barrier(values)


def adam_update(
    weight, gradient, moment, square, average, step_rate, decay_rate, factor, step_count
):
    gradient = gradient * factor
    moment = beta_one * moment + (1.0 - beta_one) * gradient
    square = beta_two * square + (1.0 - beta_two) * gradient * gradient
    fixed_one = 1.0 - jnp.power(beta_one, step_count)
    fixed_two = 1.0 - jnp.power(beta_two, step_count)
    weight = weight - step_rate * (
        moment / fixed_one / (jnp.sqrt(square / fixed_two) + adam_eps) + decay_rate * weight
    )
    average = ema_decay * average + (1.0 - ema_decay) * weight
    return (weight, moment, square, average)


def per_device(
    grid,
    tokens,
    cotangent,
    clip_ids,
    frame_ids,
    step,
    w_qkv,
    w_out,
    w_up,
    w_down,
    norm_params,
    moment_qkv,
    moment_out,
    moment_up,
    moment_down,
    moment_norm,
    square_qkv,
    square_out,
    square_up,
    square_down,
    square_norm,
    average_qkv,
    average_out,
    average_up,
    average_down,
    average_norm,
):
    n, d = tokens.shape
    back_steps = CLIP // n
    mp_index = lax.axis_index("mp")

    def shifted(value, k):
        pairs = [(i, i + k) for i in range(grid.mp) if 0 <= i + k < grid.mp]
        return lax.ppermute(value, "mp", pairs)

    frames = lax.dynamic_slice_in_dim(frame_ids, mp_index * n, n, 0)
    low = (CLIP + jnp.arange(n, dtype=jnp.int32)) // FRAME - frames
    first = low[::TQ] * FRAME // TK
    low = low.reshape(1, n)

    low_qkv, low_out, low_up, low_down = (
        w_qkv.astype(BF16),
        w_out.T.astype(BF16),
        w_up.astype(BF16),
        w_down.T.astype(BF16),
    )
    if grid.fast:
        slots, spots, side = grid.slots(), grid.spots(), grid.sides()
        rest = jnp.concatenate([low_out, low_up, low_down], axis=1)
        near, halo = joined(grid.gather_z(low_qkv), shifted(tokens, 1))
        rest = after(rest, near)
        near_rest = grid.gather_z(rest)
        one, two = grid.early(near), grid.late(near)
        one, two = joined(one, two)
        held = (near, one, two, grid.late(one))
        near_rest, *held = joined(near_rest, *held)
        far = tuple(held) + grid.across(held)
        one, two = grid.early(near_rest), grid.late(near_rest)
        q, k, v, vt, full_qkv = project(first, tokens, halo, norm_params, None, spots, far)
        one, two, q = joined(one, two, q)
        three = grid.late(one)
        mixture, logs = attend(first, low, q, k, vt)
        three, mixture = joined(three, mixture)
        held = (near_rest, one, two, three)
        far = held + grid.across(held)
        block_out, gmix, gmid, gains_two, kept, sent = feed(
            tokens, mixture, cotangent, norm_params, None, 4 * low_up.shape[1], spots, slots, side, far
        )
        got = grid.scatter_core(sent)
        got, gmix = joined(got, gmix)
        kept, got = grid.scatter_late(kept, got)
        dq, dk, dv, kept_qkv, sent = attend_back(
            first, low, q, k, v, mixture, logs, gmix, tokens, halo, norm_params, slots, side
        )
        got, sent, dq = joined(got, sent, dq)
        got_qkv = grid.scatter_core(sent)
        kept, got = grid.scatter_early(kept, got)
        kept_qkv, got_qkv = grid.scatter_late(kept_qkv, got_qkv)
        grad_rows, back, gains_one = first_back(
            first, tokens, halo, norm_params, full_qkv, gmid, dq, dk, dv
        )
        got, got_qkv, back = joined(got, got_qkv, back)
        grad_rest = grid.scatter_z(kept, got)
        kept_qkv, got_qkv = grid.scatter_early(kept_qkv, got_qkv)
        grad_qkv = grid.scatter_z(kept_qkv, got_qkv)
        wide = d // 4
        grad_out, grad_up, grad_down = (
            grad_rest[:, :wide],
            grad_rest[:, wide : wide + low_up.shape[1]],
            grad_rest[:, wide + low_up.shape[1] :],
        )
    else:
        halo = jnp.concatenate([shifted(tokens, k) for k in range(back_steps, 0, -1)])
        full_qkv = whole_of(low_qkv)
        full = tuple(whole_of(a) for a in (low_out, low_up, low_down))
        q, k, v, vt = project(first, tokens, halo, norm_params, full_qkv)
        mixture, logs = attend(first, low, q, k, vt)
        block_out, gmix, gmid, gains_two, gup, gdown, gout = feed(
            tokens, mixture, cotangent, norm_params, full, full[1].shape[1]
        )
        grad_up, grad_down, grad_out = share_of(gup), share_of(gdown), share_of(gout)
        dq, dk, dv, gqkv = attend_back(
            first, low, q, k, v, mixture, logs, gmix, tokens, halo, norm_params
        )
        grad_qkv = share_of(gqkv)
        grad_rows, back, gains_one = first_back(
            first, tokens, halo, norm_params, full_qkv, gmid, dq, dk, dv
        )
    grad_tokens = grad_rows
    for i, hop in enumerate(range(back_steps, 0, -1)):
        grad_tokens = grad_tokens + shifted(back[i * n : (i + 1) * n], -hop).astype(F32)

    weight_square = (
        jnp.sum(grad_qkv * grad_qkv)
        + jnp.sum(grad_out * grad_out)
        + jnp.sum(grad_up * grad_up)
        + jnp.sum(grad_down * grad_down)
    )
    sums = jnp.concatenate(
        [gains_one, gains_two, jnp.broadcast_to(weight_square, (4, gains_one.shape[1]))]
    )
    sums = grid.total(sums) if grid.fast else lax.psum(sums, BOTH)
    gain_grads = sums[:4]
    norm_value = jnp.sqrt(sums[4, 0] + jnp.sum(gain_grads * gain_grads))
    factor = jnp.minimum(1.0, clip_limit / (norm_value + 1e-06))
    step_count = step[0].astype(F32)
    sets = (
        adam_update(
            w_qkv, grad_qkv, moment_qkv, square_qkv, average_qkv, 0.03, 0.1, factor, step_count
        ),
        adam_update(
            w_out, grad_out.T, moment_out, square_out, average_out, 0.09, 0.1, factor, step_count
        ),
        adam_update(
            w_up, grad_up, moment_up, square_up, average_up, 0.03, 0.1, factor, step_count
        ),
        adam_update(
            w_down, grad_down.T, moment_down, square_down, average_down, 0.015, 0.1, factor, step_count
        ),
        adam_update(
            norm_params, gain_grads, moment_norm, square_norm, average_norm, 0.2, 0.0, factor, step_count
        ),
    )
    return (
        (block_out, grad_tokens, norm_value)
        + tuple(s[0] for s in sets)
        + tuple(s[1] for s in sets)
        + tuple(s[2] for s in sets)
        + tuple(s[0].astype(BF16) for s in sets[:4])
        + tuple(s[3] for s in sets)
    )


def solution(mesh):
    rows = P(BOTH, None)
    weights = (P(None, "dp", "mp"), P("mp", "dp"), P("dp", "mp"), P("mp", "dp"))
    states = weights + (P(),)
    return jax.shard_map(
        functools.partial(per_device, Grid(mesh.shape["dp"], mesh.shape["mp"])),
        mesh=mesh,
        in_specs=(rows, rows, P("dp"), P("dp"), P()) + states * 4,
        out_specs=(rows, rows, P()) + states * 3 + weights + states,
        check_vma=False,
    )
```

```python
import functools

import jax
import jax.numpy as jnp
from jax import lax
from jax.experimental import pallas as pl
from jax.experimental.pallas import tpu as pltpu
from jax.sharding import PartitionSpec as P

HEAD = 64
CLIP = 1024
FRAME = 64

norm_eps = 1e-05
beta_one = 0.9
beta_two = 0.95
adam_eps = 1e-08
clip_limit = 1.0
ema_decay = 0.75

F32 = jnp.float32
BF16 = jnp.bfloat16
BOTH = ("dp", "mp")
VMEM = pltpu.VMEM
MASKED = -1e30
PAIR = 2 * HEAD
TQ = 256
TK = 256
ROWS = 256
FEED_ROWS = 512


def mm(a, b):
    return lax.dot_general(a, b, (((1,), (0,)), ((), ())), preferred_element_type=F32)


def mm_nt(a, b):
    return lax.dot_general(a, b, (((1,), (1,)), ((), ())), preferred_element_type=F32)


def mm_tn(a, b):
    return lax.dot_general(a, b, (((0,), (0,)), ((), ())), preferred_element_type=F32)


def shape(dims, kind):
    return jax.ShapeDtypeStruct(tuple(dims), kind)


def call(body, outs, smem, ins, far=(), scratch=(), flops=0, moved=0, room=60, loose=(), small=()):
    return pl.pallas_call(
        body,
        out_shape=outs,
        in_specs=[pl.BlockSpec(memory_space=pltpu.SMEM)] * len(smem)
        + [pl.BlockSpec(memory_space=VMEM)] * len(ins)
        + [pl.BlockSpec(memory_space=pl.ANY)] * len(far),
        out_specs=tuple(
            pl.BlockSpec(
                memory_space=pl.ANY if i in loose else pltpu.SMEM if i in small else VMEM
            )
            for i in range(len(outs))
        ),
        scratch_shapes=list(scratch),
        compiler_params=pltpu.CompilerParams(vmem_limit_bytes=room << 20),
        cost_estimate=pl.CostEstimate(
            flops=int(flops), bytes_accessed=int(moved), transcendentals=0
        ),
    )(*smem, *ins, *far)


def rows_at(tile, base=0):
    return pl.ds(pl.multiple_of(base + tile * ROWS, ROWS), ROWS)


def normalize(rows):
    center = rows - jnp.mean(rows, axis=-1, keepdims=True)
    inverse = lax.rsqrt(jnp.mean(center * center, axis=-1, keepdims=True) + norm_eps)
    return center * inverse, inverse


def norm_back(grad, xhat, inverse, gain_row):
    gy = grad * gain_row
    return inverse * (
        gy
        - jnp.mean(gy, axis=-1, keepdims=True)
        - xhat * jnp.mean(gy * xhat, axis=-1, keepdims=True)
    )


def place(spots_ref, far, sems, parts):
    copies = []
    for s in range(32):
        row, col = spots_ref[s] // 4, spots_ref[s] % 4
        for t, (start, wide, whole) in enumerate(parts):
            block = far[s // 4].at[s % 4]
            rows = block.shape[-2]
            at = (
                pl.ds(pl.multiple_of(row * rows, rows), rows),
                pl.ds(pl.multiple_of(col * wide, wide), wide),
            )
            lead = (slice(None),) * (len(block.shape) - 2)
            copies.append(
                pltpu.make_async_copy(
                    block.at[lead + (slice(None), pl.ds(start, wide))],
                    whole.at[lead + at],
                    sems.at[s * len(parts) + t],
                )
            )
    for copy in copies:
        copy.start()
    return copies


def fetch(pairs, sems, start=0):
    copies = [
        pltpu.make_async_copy(far, near, sems.at[start + k]) for k, (far, near) in enumerate(pairs)
    ]
    for copy in copies:
        copy.start()
    return copies


def project_body(fast, first_ref, *refs):
    if fast:
        spots_ref, norm_ref, own_far, halo_far = refs[:4]
        far, refs = refs[4:12], refs[12:]
        qkv_ref, kt_ref, vt_ref, xt_ref, w_ref, own_ref, halo_ref, sems = refs
        copies = place(spots_ref, far, sems, [(0, far[0].shape[-1], w_ref)])
        copies += fetch(((own_far, own_ref), (halo_far, halo_ref)), sems, 32)
        for copy in copies:
            copy.wait()
    else:
        own_ref, halo_ref, norm_ref, w_ref, qkv_ref, kt_ref, vt_ref, xt_ref = refs
    gain, shift = norm_ref[0:1, :], norm_ref[1:2, :]
    pairs = w_ref.shape[1] // (3 * PAIR)

    def rows_of(ref, tile, base):
        to = rows_at(tile, base)
        xhat, _ = normalize(ref[rows_at(tile), :].astype(F32))
        xn = xhat * gain + shift
        xt_ref[:, to] = xn.T.astype(BF16)
        xn = xn.astype(BF16)
        for p in range(pairs):
            at, lanes = p * 3 * PAIR, slice(p * PAIR, (p + 1) * PAIR)
            qkv = mm(xn, w_ref[:, at : at + 3 * PAIR])
            qkv_ref[to, at : at + 3 * PAIR] = qkv.astype(BF16)
            kt_ref[lanes, to] = qkv[:, PAIR : 2 * PAIR].T.astype(BF16)
            vt_ref[lanes, to] = qkv[:, 2 * PAIR :].T.astype(BF16)

    @pl.loop(jnp.minimum(first_ref[0], CLIP // ROWS), CLIP // ROWS)
    def _(tile):
        rows_of(halo_ref, tile, 0)

    @pl.loop(0, own_ref.shape[0] // ROWS)
    def _(tile):
        rows_of(own_ref, tile, CLIP)


def project(first, own, halo, norms, w_qkv, spots=None, far=()):
    n, d = own.shape
    total = n + CLIP
    fast = len(far) > 0
    outs = (
        shape((total, 3 * d), BF16),
        shape((d, total), BF16),
        shape((d, total), BF16),
        shape((d, total), BF16),
    )
    if fast:
        outs += (shape((d, 3 * d), BF16),)
    return call(
        functools.partial(project_body, fast),
        outs,
        (first, spots) if fast else (first,),
        (norms,) if fast else (own, halo, norms, w_qkv),
        (own, halo) + tuple(far) if fast else (),
        (VMEM(own.shape, BF16), VMEM(halo.shape, BF16), pltpu.SemaphoreType.DMA((34,)))
        if fast
        else (),
        flops=6 * d * d * total,
        moved=2 * d * (6 * total + 2 * n) + 6 * d * d,
        room=24,
    )


def split_heads(pair):
    zero = jnp.zeros((HEAD, pair.shape[1]), pair.dtype)
    return jnp.concatenate(
        [
            jnp.concatenate([pair[:HEAD], zero], axis=1),
            jnp.concatenate([zero, pair[HEAD:]], axis=1),
        ]
    )


def twice(row):
    return jnp.concatenate([row, row], axis=1)


def sight(low_ref, at, i):
    spot = lax.broadcasted_iota(jnp.int32, (1, TQ), 1)
    last = ((CLIP + i * TQ) + spot) >> 6
    frame = lax.broadcasted_iota(jnp.int32, (TK, 2 * TQ), 0) >> 6
    return twice(low_ref[0:1, at]), twice(last), frame


def attend_body(
    first_ref, low_ref, qkv_ref, vt_ref, mix_ref, log_ref, qt, acc, top, total, s_ref, p_ref
):
    pairs = mix_ref.shape[1] // PAIR

    @pl.loop(0, mix_ref.shape[0] // TQ)
    def _(i):
        at = pl.ds(pl.multiple_of(i * TQ, TQ), TQ)
        low, last, frame = sight(low_ref, at, i)
        here = pl.ds(pl.multiple_of(CLIP + i * TQ, TQ), TQ)
        for p in range(pairs):
            query = qkv_ref[here, p * 3 * PAIR : (p * 3 + 1) * PAIR] * HEAD**-0.5
            qt[p] = split_heads(query.T)
        acc[...] = jnp.zeros_like(acc)
        top[...] = jnp.full_like(top, MASKED)
        total[...] = jnp.zeros_like(total)

        def step(j, carry):
            keys = pl.ds(pl.multiple_of(j * TK, TK), TK)
            shift = j * (TK // FRAME)
            visible = (frame >= low - shift) & (frame <= last - shift)
            for p in range(pairs):
                scores = mm(qkv_ref[keys, (p * 3 + 1) * PAIR : (p * 3 + 2) * PAIR], qt[p])
                s_ref[p] = jnp.where(visible, scores, MASKED)
            for p in range(pairs):
                scores = s_ref[p]
                old = top[p]
                new = jnp.maximum(old, jnp.max(scores, axis=0, keepdims=True))
                weights = jnp.exp(scores - new)
                keep = jnp.exp(old - new)
                top[p] = new
                total[p] = total[p] * keep + jnp.sum(weights, axis=0, keepdims=True)
                p_ref[p] = weights.astype(BF16)
                for h in range(2):
                    part = slice(h * HEAD, (h + 1) * HEAD)
                    acc[p, part, :] = acc[p, part, :] * keep[:, h * TQ : (h + 1) * TQ]
            for p in range(pairs):
                for h in range(2):
                    part = slice(h * HEAD, (h + 1) * HEAD)
                    values = vt_ref[p * PAIR + h * HEAD : p * PAIR + (h + 1) * HEAD, keys]
                    acc[p, part, :] += mm(values, p_ref[p, :, h * TQ : (h + 1) * TQ])
            return carry

        lax.fori_loop(first_ref[i], (CLIP + (i + 1) * TQ + TK - 1) // TK, step, 0)
        for p in range(pairs):
            sums = total[p]
            logs = top[p] + jnp.log(sums)
            inverse = 1.0 / sums
            for h in range(2):
                part = slice(h * HEAD, (h + 1) * HEAD)
                wide = slice(h * TQ, (h + 1) * TQ)
                acc[p, part, :] = acc[p, part, :] * inverse[:, wide]
                log_ref[2 * p + h : 2 * p + h + 1, at] = logs[:, wide]
            mix_ref[at, p * PAIR : (p + 1) * PAIR] = acc[p].T.astype(BF16)


def attend(first, low, qkv, vt):
    d, total = vt.shape
    n = total - CLIP
    pairs = d // PAIR
    return call(
        attend_body,
        (shape((n, d), BF16), shape((d // HEAD, n), F32)),
        (first,),
        (low, qkv, vt),
        scratch=(
            VMEM((pairs, PAIR, 2 * TQ), BF16),
            VMEM((pairs, PAIR, TQ), F32),
            VMEM((pairs, 1, 2 * TQ), F32),
            VMEM((pairs, 1, 2 * TQ), F32),
            VMEM((pairs, TK, 2 * TQ), F32),
            VMEM((pairs, TK, 2 * TQ), BF16),
        ),
        flops=16 * n * 1024 * d,
        moved=2 * d * (2 * n + 4 * total),
        room=24,
    )


def attend_back_body(fast, first_ref, *refs):
    if fast:
        slots_ref, side_ref, refs = refs[0], refs[1], refs[2:]
    low_ref, qkv_ref, kt_ref, xt_ref, mix_ref, log_ref, grad_ref, gt_ref = refs[:8]
    outs, refs = refs[8 : 10 if fast else 9], refs[10 if fast else 9 :]
    qt, gt, qs, gs, acc, dk_acc, dv_acc, s_ref, d_ref, p_ref, ds_ref, rows_ref, g_acc = refs
    n, d = grad_ref.shape
    pairs = d // PAIR
    start = jnp.minimum(first_ref[0], CLIP // ROWS)
    tiles = qkv_ref.shape[0] // ROWS

    @pl.loop(start, tiles)
    def _(tile):
        dk_acc[:, rows_at(tile)] = jnp.zeros((d, ROWS), F32)
        dv_acc[:, rows_at(tile)] = jnp.zeros((d, ROWS), F32)

    @pl.loop(start, CLIP // ROWS)
    def _(tile):
        for p in range(pairs):
            gt_ref[p * 3 * PAIR : (p * 3 + 1) * PAIR, rows_at(tile)] = jnp.zeros((PAIR, ROWS), BF16)

    @pl.loop(0, n // TQ)
    def _(i):
        at = pl.ds(pl.multiple_of(i * TQ, TQ), TQ)
        here = pl.ds(pl.multiple_of(CLIP + i * TQ, TQ), TQ)
        low, last, frame = sight(low_ref, at, i)
        for p in range(pairs):
            lanes = slice(p * PAIR, (p + 1) * PAIR)
            query = (qkv_ref[here, p * 3 * PAIR : (p * 3 + 1) * PAIR] * HEAD**-0.5).T
            grad = grad_ref[at, lanes]
            both = (grad.astype(F32) * mix_ref[at, lanes].astype(F32)).T
            grad = grad.T
            qt[p] = query
            gt[p] = grad
            qs[p] = split_heads(query)
            gs[p] = split_heads(grad)
            for h in range(2):
                wide = slice(h * TQ, (h + 1) * TQ)
                rows_ref[p, 0:1, wide] = jnp.sum(
                    both[h * HEAD : (h + 1) * HEAD], axis=0, keepdims=True
                )
                rows_ref[p, 1:2, wide] = log_ref[2 * p + h : 2 * p + h + 1, at]
        acc[...] = jnp.zeros_like(acc)

        def step(j, carry):
            keys = pl.ds(pl.multiple_of(j * TK, TK), TK)
            shift = j * (TK // FRAME)
            visible = (frame >= low - shift) & (frame <= last - shift)
            for p in range(pairs):
                one = (p * 3 + 1) * PAIR
                scores = mm(qkv_ref[keys, one : one + PAIR], qs[p])
                s_ref[p] = jnp.where(visible, scores, MASKED)
                d_ref[p] = mm(qkv_ref[keys, one + PAIR : one + 2 * PAIR], gs[p])
            for p in range(pairs):
                probs = jnp.exp(s_ref[p] - rows_ref[p, 1:2, :])
                p_ref[p] = probs.astype(BF16)
                ds_ref[p] = (probs * (d_ref[p] - rows_ref[p, 0:1, :])).astype(BF16)
            for p in range(pairs):
                for h in range(2):
                    part = slice(h * HEAD, (h + 1) * HEAD)
                    rows = slice(p * PAIR + h * HEAD, p * PAIR + (h + 1) * HEAD)
                    wide = slice(h * TQ, (h + 1) * TQ)
                    dv_acc[rows, keys] += mm_nt(gt[p, part, :], p_ref[p, :, wide])
                    dk_acc[rows, keys] += mm_nt(qt[p, part, :], ds_ref[p, :, wide])
                    acc[p, part, :] += mm(kt_ref[rows, keys], ds_ref[p, :, wide])
            return carry

        lax.fori_loop(first_ref[i], (CLIP + (i + 1) * TQ + TK - 1) // TK, step, 0)
        for p in range(pairs):
            gt_ref[p * 3 * PAIR : (p * 3 + 1) * PAIR, here] = (acc[p] * HEAD**-0.5).astype(BF16)

    @pl.loop(start, tiles)
    def _(tile):
        at = rows_at(tile)
        for p in range(pairs):
            one, rows = (p * 3 + 1) * PAIR, slice(p * PAIR, (p + 1) * PAIR)
            gt_ref[one : one + PAIR, at] = dk_acc[rows, at].astype(BF16)
            gt_ref[one + PAIR : one + 2 * PAIR, at] = dv_acc[rows, at].astype(BF16)

    wide = 6 * PAIR

    def weights(side):
        rows = pl.ds(pl.multiple_of(side * wide, wide), wide)
        g_acc[...] = mm_nt(xt_ref[:, CLIP:], gt_ref[rows, CLIP:])

        @pl.loop(start, CLIP // ROWS)
        def _(tile):
            g_acc[...] += mm_nt(xt_ref[:, rows_at(tile)], gt_ref[rows, rows_at(tile)])

    if not fast:
        for side in range(d // (2 * PAIR)):
            weights(side)
            outs[0][:, side * wide : (side + 1) * wide] = g_acc[...].astype(BF16)
        return
    rows = d // 8
    for k in range(2):
        side = side_ref[k]
        weights(side)
        for x in range(2):
            for r in range(8):
                slot = slots_ref[r * 4 + side * 2 + x] & 15
                outs[k][slot] = g_acc[
                    r * rows : (r + 1) * rows, x * 3 * PAIR : (x + 1) * 3 * PAIR
                ].astype(BF16)


def attend_back(first, low, qkv, kt, xt, mixture, logs, grad, slots=None, side=None):
    n, d = grad.shape
    total = qkv.shape[0]
    pairs = d // PAIR
    fast = slots is not None
    outs = (shape((3 * d, total), BF16),)
    if fast:
        outs += (shape((16, d // 8, 3 * d // 4), BF16),) * 2
    else:
        outs += (shape((d, 3 * d), BF16),)
    return call(
        functools.partial(attend_back_body, fast),
        outs,
        (first, slots, side) if fast else (first,),
        (low, qkv, kt, xt, mixture, logs, grad),
        scratch=(
            VMEM((pairs, PAIR, TQ), BF16),
            VMEM((pairs, PAIR, TQ), BF16),
            VMEM((pairs, PAIR, 2 * TQ), BF16),
            VMEM((pairs, PAIR, 2 * TQ), BF16),
            VMEM((pairs, PAIR, TQ), F32),
            VMEM((d, total), F32),
            VMEM((d, total), F32),
            VMEM((pairs, TK, 2 * TQ), F32),
            VMEM((pairs, TK, 2 * TQ), F32),
            VMEM((pairs, TK, 2 * TQ), BF16),
            VMEM((pairs, TK, 2 * TQ), BF16),
            VMEM((pairs, 8, 2 * TQ), F32),
            VMEM((d, 6 * PAIR), F32),
        ),
        flops=40 * n * 1024 * d,
        moved=2 * d * (2 * n + 8 * total),
        room=38,
    )


def feed_body(fast, *refs):
    if fast:
        spots_ref, slots_ref, side_ref, mix_ref, norm_ref, x_far, cot_far = refs[:7]
        far, refs = refs[7:15], refs[15:]
        out_ref, gmix_ref, gmid_ref, gain_ref = refs[:4]
        outs, refs = refs[4:6], refs[6:]
        wo_ref, up_ref, down_ref, x_ref, cot_ref, sems = refs[:6]
        refs = refs[6:]
        one, ff = wo_ref.shape[1] // 4, up_ref.shape[1] // 4
        copies = place(
            spots_ref, far, sems,
            [(0, one, wo_ref), (one, ff, up_ref), (one + ff, ff, down_ref)],
        )
        copies += fetch(((x_far, x_ref), (cot_far, cot_ref)), sems, 96)
        for copy in copies:
            copy.wait()
    else:
        x_ref, mix_ref, cot_ref, norm_ref, wo_ref, up_ref, down_ref = refs[:7]
        out_ref, gmix_ref, gmid_ref, gain_ref = refs[7:11]
        outs, refs = refs[11:14], refs[14:]
    act_ref, gh_ref, n2t_ref, lowt_ref, cott_ref = refs
    gain, shift = norm_ref[2:3, :], norm_ref[3:4, :]
    ff = up_ref.shape[1]
    d = x_ref.shape[1]
    wide = min(512, ff)
    root = 0.7978845608028654
    gain_ref[...] = jnp.zeros_like(gain_ref)

    rows = min(FEED_ROWS, x_ref.shape[0])

    @pl.loop(0, x_ref.shape[0] // rows)
    def _(tile):
        at = pl.ds(pl.multiple_of(tile * rows, rows), rows)
        cot = cot_ref[at, :]
        cott_ref[:, at] = cot.T
        middle = x_ref[at, :].astype(F32) + mm_nt(mix_ref[at, :], wo_ref[...])
        xhat, inverse = normalize(middle)
        n2 = xhat * gain + shift
        n2t_ref[:, at] = n2.T.astype(BF16)
        n2 = n2.astype(BF16)
        out = middle
        second = jnp.zeros_like(middle)
        for c in range(ff // wide):
            cols = slice(c * wide, (c + 1) * wide)
            hidden = mm(n2, up_ref[:, cols])
            square = hidden * hidden
            bent = jnp.tanh(hidden * (root + (root * 0.044715) * square))
            half = 0.5 + 0.5 * bent
            active = (hidden * half).astype(BF16)
            slope = half + hidden * (1.0 - bent * bent) * (
                0.5 * root + (0.5 * root * 3 * 0.044715) * square
            )
            act_ref[at, cols] = active
            out += mm_nt(active, down_ref[:, cols])
            gh = (mm(cot, down_ref[:, cols]) * slope).astype(BF16)
            gh_ref[at, cols] = gh
            second += mm_nt(gh, up_ref[:, cols])
        out_ref[at, :] = out.astype(BF16)
        gain_ref[0:1, :] += jnp.sum(second * xhat, axis=0, keepdims=True)
        gain_ref[1:2, :] += jnp.sum(second, axis=0, keepdims=True)
        gmid = cot.astype(F32) + norm_back(second, xhat, inverse, gain)
        gmid_ref[at, :] = gmid
        lowt_ref[:, at] = gmid.T.astype(BF16)
        gmix_ref[at, :] = mm(gmid.astype(BF16), wo_ref[...]).astype(BF16)

    if not fast:
        gup_ref, gdown_ref, gout_ref = outs
        for c in range(ff // wide):
            cols = slice(c * wide, (c + 1) * wide)
            gup_ref[:, cols] = mm(n2t_ref[...], gh_ref[:, cols]).astype(BF16)
            gdown_ref[:, cols] = mm(cott_ref[...], act_ref[:, cols]).astype(BF16)
        gout_ref[...] = mm(lowt_ref[...], mix_ref[...]).astype(BF16)
        return
    one, wide, rows = d // 4, ff // 4, d // 8
    for k in range(2):
        side = side_ref[k]
        cols = pl.ds(pl.multiple_of(side * 2 * wide, 2 * wide), 2 * wide)
        small = pl.ds(pl.multiple_of(side * 2 * one, 2 * one), 2 * one)
        spots = [[slots_ref[r * 4 + side * 2 + x] & 15 for r in range(8)] for x in range(2)]
        for start, size, left, right in (
            (0, one, lowt_ref, mix_ref[:, small]),
            (one, wide, n2t_ref, gh_ref[:, cols]),
            (one + wide, wide, cott_ref, act_ref[:, cols]),
        ):
            for x in range(2):
                grad = mm(left[...], right[:, x * size : (x + 1) * size]).astype(BF16)
                for r in range(8):
                    outs[k][spots[x][r], :, start : start + size] = grad[
                        r * rows : (r + 1) * rows
                    ]


def feed(x, mixture, cot, norms, full, ff, spots=None, slots=None, side=None, far=()):
    n, d = x.shape
    fast = len(far) > 0
    outs = (shape((n, d), BF16), shape((n, d), BF16), shape((n, d), F32), shape((2, d), F32))
    if fast:
        outs += (shape((16, d // 8, d // 4 + ff // 2), BF16),) * 2
    else:
        outs += (shape((d, ff), BF16), shape((d, ff), BF16), shape((d, d), BF16))
    return call(
        functools.partial(feed_body, fast),
        outs,
        (spots, slots, side) if fast else (),
        (mixture, norms) if fast else (x, mixture, cot, norms) + tuple(full),
        (x, cot) + tuple(far) if fast else (),
        (
            (
                VMEM((d, d), BF16),
                VMEM((d, ff), BF16),
                VMEM((d, ff), BF16),
                VMEM((n, d), BF16),
                VMEM((n, d), BF16),
                pltpu.SemaphoreType.DMA((98,)),
            )
            if fast
            else ()
        )
        + (
            VMEM((n, ff), BF16),
            VMEM((n, ff), BF16),
            VMEM((d, n), BF16),
            VMEM((d, n), BF16),
            VMEM((d, n), BF16),
        ),
        flops=2 * n * d * (6 * ff + 3 * d),
        moved=2 * n * 6 * d + 8 * d * ff,
        room=38,
    )


def first_back_body(
    first_ref, norm_ref, w_ref, gmid_ref, gt_ref, own_far, halo_far, grad_ref, back_ref, gain_ref,
    own_ref, halo_ref, sems,
):
    for copy in fetch(((own_far, own_ref), (halo_far, halo_ref)), sems):
        copy.wait()
    gain = norm_ref[0:1, :]
    gain_ref[...] = jnp.zeros_like(gain_ref)
    start = jnp.minimum(first_ref[0], CLIP // ROWS)

    def rows_of(ref, tile, base, own):
        at = rows_at(tile)
        first = mm(w_ref[...], gt_ref[:, rows_at(tile, base)]).T
        xhat, inverse = normalize(ref[at, :].astype(F32))
        gain_ref[0:1, :] += jnp.sum(first * xhat, axis=0, keepdims=True)
        gain_ref[1:2, :] += jnp.sum(first, axis=0, keepdims=True)
        grad = norm_back(first, xhat, inverse, gain)
        if own:
            grad_ref[at, :] = gmid_ref[at, :] + grad
        else:
            back_ref[at, :] = grad.astype(BF16)

    @pl.loop(0, start)
    def _(tile):
        back_ref[rows_at(tile), :] = jnp.zeros((ROWS, back_ref.shape[1]), BF16)

    @pl.loop(start, CLIP // ROWS)
    def _(tile):
        rows_of(halo_ref, tile, 0, False)

    @pl.loop(0, own_ref.shape[0] // ROWS)
    def _(tile):
        rows_of(own_ref, tile, CLIP, True)


def first_back(first, own, halo, norms, w_qkv, gmid, gt):
    n, d = own.shape
    total = n + CLIP
    return call(
        first_back_body,
        (shape((n, d), F32), shape((CLIP, d), BF16), shape((2, d), F32)),
        (first,),
        (norms, w_qkv, gmid, gt),
        (own, halo),
        (VMEM(own.shape, BF16), VMEM(halo.shape, BF16), pltpu.SemaphoreType.DMA((2,))),
        flops=6 * d * d * total,
        moved=2 * d * (4 * total + 6 * n),
        room=24,
    )


class Grid:
    def __init__(self, dp, mp):
        self.dp, self.mp = dp, mp
        self.fast = (dp, mp) == (8, 4)

    def swap(self, value, z=0, y=0, x=0, c=0):
        bits = z * 8 + y * 4 + x * 2 + c
        return lax.ppermute(value, BOTH, [(i, i ^ bits) for i in range(self.dp * self.mp)])

    def spot(self):
        dp, mp = lax.axis_index("dp"), lax.axis_index("mp")
        return dp // 2, dp % 2, mp // 2, mp % 2

    def slots(self):
        z, y, x, c = self.spot()
        s = jnp.arange(32, dtype=jnp.int32)
        oz, oy, oc, ox = s >> 3, (s >> 2) & 1, (s >> 1) & 1, s & 1
        return (oc ^ c) * 16 + (ox ^ x) * 8 + (oy ^ y) * 4 + (oz ^ z)

    def spots(self):
        z, y, x, c = self.spot()
        s = jnp.arange(32, dtype=jnp.int32)
        oc, ox, oy, oz = (s >> 4) ^ c, ((s >> 3) & 1) ^ x, ((s >> 2) & 1) ^ y, (s & 3) ^ z
        return ((oz * 2 + oy) * 2 + oc) * 2 + ox

    def sides(self):
        c = lax.axis_index("mp") % 2
        return jnp.stack([c, 1 - c]).astype(jnp.int32)

    def gather_z(self, block):
        return jnp.stack([block] + [self.swap(block, z=k) for k in (1, 2, 3)])

    def across(self, held):
        return tuple(self.swap(a, c=1) for a in held)

    def gather_plane(self, near):
        return near, self.swap(near, y=1), self.swap(near, x=1), self.swap(near, y=1, x=1)

    def scatter_core(self, sent):
        return self.swap(sent, c=1)

    def scatter_plane(self, kept, got):
        own, one, two, three = (added(kept[k : k + 4], got[k : k + 4]) for k in (0, 4, 8, 12))
        return own, self.swap(one, y=1), self.swap(two, x=1), self.swap(three, y=1, x=1)

    def scatter_z(self, held):
        parts = [sum(a[k].astype(F32) for a in held).astype(BF16) for k in range(4)]
        return [parts[0]] + [self.swap(parts[k], z=k) for k in (1, 2, 3)]


def added(a, b):
    return (a.astype(F32) + b.astype(F32)).astype(BF16)


def whole_of(block):
    m = block.ndim - 2
    half = lax.all_gather(block, "dp", axis=m, tiled=True)
    return lax.all_gather(half, "mp", axis=m + 1, tiled=True)


def share_of(whole):
    m = whole.ndim - 2
    half = lax.psum_scatter(whole, "mp", scatter_dimension=m + 1, tiled=True)
    return lax.psum_scatter(half, "dp", scatter_dimension=m, tiled=True).astype(F32)


def beside(whole):
    d = whole.shape[1]
    return whole.reshape(3, d, d // PAIR, PAIR).transpose(1, 2, 0, 3).reshape(d, 3 * d)


def apart(wide):
    d = wide.shape[0]
    return wide.reshape(d, d // PAIR, 3, PAIR).transpose(2, 0, 1, 3).reshape(3, d, d)


def after(value, *others):
    return lax.optimization_barrier((value,) + others)[0]


def joined(*values):
    return lax.optimization_barrier(values)


def adam_update(
    weight, gradient, moment, square, average, step_rate, decay_rate, factor, fixed_one, fixed_two
):
    gradient = gradient * factor
    moment = beta_one * moment + (1.0 - beta_one) * gradient
    square = beta_two * square + (1.0 - beta_two) * gradient * gradient
    weight = weight - step_rate * (
        moment / fixed_one / (jnp.sqrt(square / fixed_two) + adam_eps) + decay_rate * weight
    )
    average = ema_decay * average + (1.0 - ema_decay) * weight
    return (weight, moment, square, average)


RATES = ((0.03, 0.1), (0.09, 0.1), (0.03, 0.1), (0.015, 0.1), (0.2, 0.0))


def total_body(*refs):
    rest, qkv, (one_ref, two_ref) = refs[:4], refs[4:8], refs[8:10]
    out_ref, up_ref, down_ref, qkv_ref, sums_ref = refs[10:]
    small, wide = out_ref.shape[1], up_ref.shape[1]
    width = sums_ref.shape[1]

    def sum_of(parts, at, size):
        a, b, c, d = (p[:, at : at + size].astype(F32) for p in parts)
        return (a + b) + (c + d)

    def squares(value):
        row = jnp.sum(value * value, axis=0, keepdims=True)
        return row if row.shape[1] == width else jnp.concatenate([row] + [jnp.zeros_like(row)] * (width // row.shape[1] - 1), axis=1)

    grad = sum_of(rest, 0, small)
    out_ref[...] = grad
    square = squares(grad)
    for ref, at in ((up_ref, small), (down_ref, small + wide)):
        grad = sum_of(rest, at, wide)
        ref[...] = grad
        square += squares(grad)
    for k in range(3):
        grad = sum_of(qkv, k * PAIR, PAIR)
        qkv_ref[k] = grad
        square += squares(grad)
    sums_ref[...] = jnp.zeros_like(sums_ref)
    sums_ref[0:2, :] = one_ref[...]
    sums_ref[2:4, :] = two_ref[...]
    sums_ref[4:5, :] = square


def totals(rest, qkv, gains_one, gains_two):
    rows, wide = rest[0].shape
    small = qkv[0].shape[1] // 3
    wide = (wide - small) // 2
    return call(
        total_body,
        (
            shape((rows, small), F32),
            shape((rows, wide), F32),
            shape((rows, wide), F32),
            shape((3, rows, small), F32),
            shape((8, gains_one.shape[1]), F32),
        ),
        (),
        tuple(rest) + tuple(qkv) + (gains_one, gains_two),
        moved=12 * rest[0].size,
        room=16,
    )


def adam_body(parts, scale_ref, *refs):
    sums, grads, refs = refs[:parts], refs[parts : parts + 4], refs[parts + 4 :]
    far, outs, norm_ref, held, sems = refs[:20], refs[20:44], refs[44], refs[45:65], refs[65]
    copies = fetch(tuple(zip(far, held)), sems)
    total = sums[0][...]
    if parts == 4:
        total = (total + sums[1][...]) + (sums[2][...] + sums[3][...])
    gains = total[0:4]
    square = jnp.sum(total[4:5]) + jnp.sum(gains * gains)
    norm = jnp.sqrt(jnp.broadcast_to(square, (1, 1)))
    norm_ref[0, 0] = jnp.sum(norm)
    factor = jnp.minimum(1.0, clip_limit / (norm + 1e-06))
    fixed_one, fixed_two = scale_ref[0], scale_ref[1]
    for copy in copies:
        copy.wait()
    for k, (rate, decay) in enumerate(RATES):
        weight, moment, square, average = (ref[...] for ref in held[4 * k : 4 * k + 4])
        grad = grads[k][...] if k < 4 else gains
        new = adam_update(
            weight, grad, moment, square, average, rate, decay, factor, fixed_one, fixed_two
        )
        for i in range(4):
            outs[4 * k + i][...] = new[i]
        if k < 4:
            outs[20 + k][...] = new[0].astype(BF16)


def adam(sums, scales, grads, sets):
    outs = tuple(shape(s[0].shape, F32) for s in sets for _ in range(4))
    outs += tuple(shape(s[0].shape, BF16) for s in sets[:4]) + (shape((1, 1), F32),)
    got = call(
        functools.partial(adam_body, len(sums)),
        outs,
        (scales,),
        tuple(sums) + tuple(grads),
        sum((tuple(s) for s in sets), ()),
        tuple(VMEM(a.shape, F32) for s in sets for a in s) + (pltpu.SemaphoreType.DMA((20,)),),
        flops=30 * sum(s[0].size for s in sets),
        moved=38 * sum(s[0].size for s in sets),
        room=16,
        small=(24,),
    )
    return [got[4 * k : 4 * k + 4] for k in range(5)], got[20:24], got[24]


def per_device(
    grid,
    tokens,
    cotangent,
    clip_ids,
    frame_ids,
    step,
    w_qkv,
    w_out,
    w_up,
    w_down,
    norm_params,
    moment_qkv,
    moment_out,
    moment_up,
    moment_down,
    moment_norm,
    square_qkv,
    square_out,
    square_up,
    square_down,
    square_norm,
    average_qkv,
    average_out,
    average_up,
    average_down,
    average_norm,
):
    n, d = tokens.shape
    back_steps = CLIP // n
    mp_index = lax.axis_index("mp")

    def shifted(value, k):
        pairs = [(i, i + k) for i in range(grid.mp) if 0 <= i + k < grid.mp]
        return lax.ppermute(value, "mp", pairs)

    frames = lax.dynamic_slice_in_dim(frame_ids, mp_index * n, n, 0)
    low = (CLIP + jnp.arange(n, dtype=jnp.int32)) // FRAME - frames
    first = low[::TQ] * FRAME // TK
    low = low.reshape(1, n)

    low_qkv, low_out, low_up, low_down = (
        jnp.concatenate([w_qkv[0], w_qkv[1], w_qkv[2]], axis=1).astype(BF16)
        if grid.fast
        else w_qkv.astype(BF16),
        w_out.T.astype(BF16),
        w_up.astype(BF16),
        w_down.T.astype(BF16),
    )
    if grid.fast:
        slots, spots, side = grid.slots(), grid.spots(), grid.sides()
        rest = jnp.concatenate([low_out, low_up, low_down], axis=1)
        near, halo = joined(grid.gather_z(low_qkv), shifted(tokens, 1))
        rest = after(rest, near)
        near_rest = grid.gather_z(rest)
        near_rest, *held = joined(near_rest, *grid.gather_plane(near))
        far = tuple(held) + grid.across(held)
        held = grid.gather_plane(near_rest)
        qkv, kt, vt, xt, full_qkv = project(first, tokens, halo, norm_params, None, spots, far)
        mixture, logs = attend(first, low, qkv, vt)
        mixture, *held = joined(mixture, *held)
        far = tuple(held) + grid.across(held)
        block_out, gmix, gmid, gains_two, kept, sent = feed(
            tokens, mixture, cotangent, norm_params, None, 4 * low_up.shape[1], spots, slots, side, far
        )
        got, gmix = joined(grid.scatter_core(sent), gmix)
        held = grid.scatter_plane(kept, got)
        gt, kept_qkv, sent = attend_back(
            first, low, qkv, kt, xt, mixture, logs, gmix, slots, side
        )
        sent, gt, *held = joined(sent, gt, *held)
        near_rest = grid.scatter_z(held)
        held = grid.scatter_plane(kept_qkv, grid.scatter_core(sent))
        grad_rows, back, gains_one = first_back(
            first, tokens, halo, norm_params, full_qkv, gmid, gt
        )
        back, *got = joined(back, *near_rest, *held)
        near_rest, held = got[:4], got[4:]
        near_qkv = grid.scatter_z(held)
        back, *near_qkv = joined(shifted(back, -1), *near_qkv)
        grad_out, grad_up, grad_down, grad_qkv, sums = totals(
            near_rest, near_qkv, gains_one, gains_two
        )
        sums = sums + grid.swap(sums, c=1)
        plane = [grid.swap(sums, y=b, x=a) for a, b in ((1, 0), (0, 1), (1, 1))]
        grad_tokens = after(grad_rows, sums) + back.astype(F32)
        sums = (sums + plane[0]) + (plane[1] + plane[2])
        sums = [sums] + [grid.swap(sums, z=k) for k in (1, 2, 3)]
        *sums, grad_tokens = joined(*sums, grad_tokens)
    else:
        halo = jnp.concatenate([shifted(tokens, k) for k in range(back_steps, 0, -1)])
        full_qkv = beside(whole_of(low_qkv))
        full = tuple(whole_of(a) for a in (low_out, low_up, low_down))
        qkv, kt, vt, xt = project(first, tokens, halo, norm_params, full_qkv)
        mixture, logs = attend(first, low, qkv, vt)
        block_out, gmix, gmid, gains_two, gup, gdown, gout = feed(
            tokens, mixture, cotangent, norm_params, full, full[1].shape[1]
        )
        grad_up, grad_down, grad_out = share_of(gup), share_of(gdown), share_of(gout)
        gt, gqkv = attend_back(first, low, qkv, kt, xt, mixture, logs, gmix)
        grad_qkv = share_of(apart(gqkv))
        grad_rows, back, gains_one = first_back(
            first, tokens, halo, norm_params, full_qkv, gmid, gt
        )
        grad_tokens = grad_rows
        for i, hop in enumerate(range(back_steps, 0, -1)):
            grad_tokens = grad_tokens + shifted(back[i * n : (i + 1) * n], -hop).astype(F32)
        weight_square = (
            jnp.sum(grad_qkv * grad_qkv)
            + jnp.sum(grad_out * grad_out)
            + jnp.sum(grad_up * grad_up)
            + jnp.sum(grad_down * grad_down)
        )
        row = jnp.zeros((4, d), F32).at[0, 0].set(weight_square)
        sums = [lax.psum(jnp.concatenate([gains_one, gains_two, row]), BOTH)]
    step_count = step[0].astype(F32)
    scales = jnp.stack(
        [1.0 - jnp.power(beta_one, step_count), 1.0 - jnp.power(beta_two, step_count)]
    )
    sets, copies, norm_value = adam(
        sums,
        scales,
        (grad_qkv, grad_out, grad_up, grad_down),
        (
            (w_qkv, moment_qkv, square_qkv, average_qkv),
            (w_out.T, moment_out.T, square_out.T, average_out.T),
            (w_up, moment_up, square_up, average_up),
            (w_down.T, moment_down.T, square_down.T, average_down.T),
            (norm_params, moment_norm, square_norm, average_norm),
        ),
    )
    norm_value = norm_value.reshape(())

    def turned(k, value):
        return value.T if k in (1, 3) else value

    return (
        (block_out, grad_tokens, norm_value)
        + tuple(turned(k, s[0]) for k, s in enumerate(sets))
        + tuple(turned(k, s[1]) for k, s in enumerate(sets))
        + tuple(turned(k, s[2]) for k, s in enumerate(sets))
        + tuple(turned(k, c) for k, c in enumerate(copies))
        + tuple(turned(k, s[3]) for k, s in enumerate(sets))
    )


def solution(mesh):
    rows = P(BOTH, None)
    weights = (P(None, "dp", "mp"), P("mp", "dp"), P("dp", "mp"), P("mp", "dp"))
    states = weights + (P(),)
    return jax.shard_map(
        functools.partial(per_device, Grid(mesh.shape["dp"], mesh.shape["mp"])),
        mesh=mesh,
        in_specs=(rows, rows, P("dp"), P("dp"), P()) + states * 4,
        out_specs=(rows, rows, P()) + states * 3 + weights + states,
        check_vma=False,
    )
```

```python
import functools

import jax
import jax.numpy as jnp
from jax import lax
from jax.experimental import pallas as pl
from jax.experimental.pallas import tpu as pltpu
from jax.sharding import PartitionSpec as P

HEAD = 64
CLIP = 1024
FRAME = 64

norm_eps = 1e-05
beta_one = 0.9
beta_two = 0.95
adam_eps = 1e-08
clip_limit = 1.0
ema_decay = 0.75

F32 = jnp.float32
BF16 = jnp.bfloat16
BOTH = ("dp", "mp")
VMEM = pltpu.VMEM
MASKED = -1e30
PAIR = 2 * HEAD
TQ = 256
TK = 256
ROWS = 256
FEED_ROWS = 1024


def mm(a, b):
    return lax.dot_general(a, b, (((1,), (0,)), ((), ())), preferred_element_type=F32)


def mm_nt(a, b):
    return lax.dot_general(a, b, (((1,), (1,)), ((), ())), preferred_element_type=F32)


def mm_tn(a, b):
    return lax.dot_general(a, b, (((0,), (0,)), ((), ())), preferred_element_type=F32)


def shape(dims, kind):
    return jax.ShapeDtypeStruct(tuple(dims), kind)


def call(body, outs, smem, ins, far=(), scratch=(), flops=0, moved=0, room=60, loose=(), small=()):
    return pl.pallas_call(
        body,
        out_shape=outs,
        in_specs=[pl.BlockSpec(memory_space=pltpu.SMEM)] * len(smem)
        + [pl.BlockSpec(memory_space=VMEM)] * len(ins)
        + [pl.BlockSpec(memory_space=pl.ANY)] * len(far),
        out_specs=tuple(
            pl.BlockSpec(
                memory_space=pl.ANY if i in loose else pltpu.SMEM if i in small else VMEM
            )
            for i in range(len(outs))
        ),
        scratch_shapes=list(scratch),
        compiler_params=pltpu.CompilerParams(vmem_limit_bytes=room << 20),
        cost_estimate=pl.CostEstimate(
            flops=int(flops), bytes_accessed=int(moved), transcendentals=0
        ),
    )(*smem, *ins, *far)


def rows_at(tile, base=0):
    return pl.ds(pl.multiple_of(base + tile * ROWS, ROWS), ROWS)


def normalize(rows):
    center = rows - jnp.mean(rows, axis=-1, keepdims=True)
    inverse = lax.rsqrt(jnp.mean(center * center, axis=-1, keepdims=True) + norm_eps)
    return center * inverse, inverse


def norm_back(grad, xhat, inverse, gain_row):
    gy = grad * gain_row
    return inverse * (
        gy
        - jnp.mean(gy, axis=-1, keepdims=True)
        - xhat * jnp.mean(gy * xhat, axis=-1, keepdims=True)
    )


def place(spots_ref, far, sems, parts):
    copies = []
    for s in range(32):
        row, col = spots_ref[s] // 4, spots_ref[s] % 4
        for t, (start, wide, whole) in enumerate(parts):
            block = far[s // 4].at[s % 4]
            rows = block.shape[-2]
            at = (
                pl.ds(pl.multiple_of(row * rows, rows), rows),
                pl.ds(pl.multiple_of(col * wide, wide), wide),
            )
            lead = (slice(None),) * (len(block.shape) - 2)
            copies.append(
                pltpu.make_async_copy(
                    block.at[lead + (slice(None), pl.ds(start, wide))],
                    whole.at[lead + at],
                    sems.at[s * len(parts) + t],
                )
            )
    for copy in copies:
        copy.start()
    return copies


def fetch(pairs, sems, start=0):
    copies = [
        pltpu.make_async_copy(far, near, sems.at[start + k]) for k, (far, near) in enumerate(pairs)
    ]
    for copy in copies:
        copy.start()
    return copies


def project_body(fast, first_ref, *refs):
    if fast:
        spots_ref, norm_ref, own_far, halo_far = refs[:4]
        far, refs = refs[4:12], refs[12:]
        qkv_ref, kt_ref, vt_ref, xt_ref, w_ref, own_ref, halo_ref, sems = refs
        copies = place(spots_ref, far, sems, [(0, far[0].shape[-1], w_ref)])
        copies += fetch(((own_far, own_ref), (halo_far, halo_ref)), sems, 32)
        for copy in copies:
            copy.wait()
    else:
        own_ref, halo_ref, norm_ref, w_ref, qkv_ref, kt_ref, vt_ref, xt_ref = refs
    gain, shift = norm_ref[0:1, :], norm_ref[1:2, :]
    pairs = w_ref.shape[1] // (3 * PAIR)

    def rows_of(ref, tile, base):
        to = rows_at(tile, base)
        xhat, _ = normalize(ref[rows_at(tile), :].astype(F32))
        xn = xhat * gain + shift
        xt_ref[:, to] = xn.T.astype(BF16)
        xn = xn.astype(BF16)
        for p in range(pairs):
            at, lanes = p * 3 * PAIR, slice(p * PAIR, (p + 1) * PAIR)
            qkv = mm(xn, w_ref[:, at : at + 3 * PAIR])
            qkv_ref[to, at : at + 3 * PAIR] = qkv.astype(BF16)
            kt_ref[lanes, to] = qkv[:, PAIR : 2 * PAIR].T.astype(BF16)
            vt_ref[lanes, to] = qkv[:, 2 * PAIR :].T.astype(BF16)

    @pl.loop(jnp.minimum(first_ref[0], CLIP // ROWS), CLIP // ROWS)
    def _(tile):
        rows_of(halo_ref, tile, 0)

    @pl.loop(0, own_ref.shape[0] // ROWS)
    def _(tile):
        rows_of(own_ref, tile, CLIP)


def project(first, own, halo, norms, w_qkv, spots=None, far=()):
    n, d = own.shape
    total = n + CLIP
    fast = len(far) > 0
    outs = (
        shape((total, 3 * d), BF16),
        shape((d, total), BF16),
        shape((d, total), BF16),
        shape((d, total), BF16),
    )
    if fast:
        outs += (shape((d, 3 * d), BF16),)
    return call(
        functools.partial(project_body, fast),
        outs,
        (first, spots) if fast else (first,),
        (norms,) if fast else (own, halo, norms, w_qkv),
        (own, halo) + tuple(far) if fast else (),
        (VMEM(own.shape, BF16), VMEM(halo.shape, BF16), pltpu.SemaphoreType.DMA((34,)))
        if fast
        else (),
        flops=6 * d * d * total,
        moved=2 * d * (6 * total + 2 * n) + 6 * d * d,
        room=24,
    )


def split_heads(pair):
    zero = jnp.zeros((HEAD, pair.shape[1]), pair.dtype)
    return jnp.concatenate(
        [
            jnp.concatenate([pair[:HEAD], zero], axis=1),
            jnp.concatenate([zero, pair[HEAD:]], axis=1),
        ]
    )


def twice(row):
    return jnp.concatenate([row, row], axis=1)


def sight(low_ref, at, i):
    spot = lax.broadcasted_iota(jnp.int32, (1, TQ), 1)
    last = ((CLIP + i * TQ) + spot) >> 6
    frame = lax.broadcasted_iota(jnp.int32, (TK, 2 * TQ), 0) >> 6
    return twice(low_ref[0:1, at]), twice(last), frame


def attend_body(
    first_ref, low_ref, qkv_ref, vt_ref, mix_ref, log_ref, qt, acc, top, total, s_ref, p_ref
):
    pairs = mix_ref.shape[1] // PAIR

    @pl.loop(0, mix_ref.shape[0] // TQ)
    def _(i):
        at = pl.ds(pl.multiple_of(i * TQ, TQ), TQ)
        low, last, frame = sight(low_ref, at, i)
        here = pl.ds(pl.multiple_of(CLIP + i * TQ, TQ), TQ)
        for p in range(pairs):
            query = qkv_ref[here, p * 3 * PAIR : (p * 3 + 1) * PAIR] * HEAD**-0.5
            qt[p] = split_heads(query.T)
        acc[...] = jnp.zeros_like(acc)
        top[...] = jnp.full_like(top, MASKED)
        total[...] = jnp.zeros_like(total)

        def step(j, carry):
            keys = pl.ds(pl.multiple_of(j * TK, TK), TK)
            shift = j * (TK // FRAME)
            visible = (frame >= low - shift) & (frame <= last - shift)
            for p in range(pairs):
                scores = mm(qkv_ref[keys, (p * 3 + 1) * PAIR : (p * 3 + 2) * PAIR], qt[p])
                s_ref[p] = jnp.where(visible, scores, MASKED)
            for p in range(pairs):
                scores = s_ref[p]
                old = top[p]
                new = jnp.maximum(old, jnp.max(scores, axis=0, keepdims=True))
                weights = jnp.exp(scores - new)
                keep = jnp.exp(old - new)
                top[p] = new
                total[p] = total[p] * keep + jnp.sum(weights, axis=0, keepdims=True)
                p_ref[p] = weights.astype(BF16)
                for h in range(2):
                    part = slice(h * HEAD, (h + 1) * HEAD)
                    acc[p, part, :] = acc[p, part, :] * keep[:, h * TQ : (h + 1) * TQ]
            for p in range(pairs):
                for h in range(2):
                    part = slice(h * HEAD, (h + 1) * HEAD)
                    values = vt_ref[p * PAIR + h * HEAD : p * PAIR + (h + 1) * HEAD, keys]
                    acc[p, part, :] += mm(values, p_ref[p, :, h * TQ : (h + 1) * TQ])
            return carry

        lax.fori_loop(first_ref[i], (CLIP + (i + 1) * TQ + TK - 1) // TK, step, 0)
        for p in range(pairs):
            sums = total[p]
            logs = top[p] + jnp.log(sums)
            inverse = 1.0 / sums
            for h in range(2):
                part = slice(h * HEAD, (h + 1) * HEAD)
                wide = slice(h * TQ, (h + 1) * TQ)
                acc[p, part, :] = acc[p, part, :] * inverse[:, wide]
                log_ref[2 * p + h : 2 * p + h + 1, at] = logs[:, wide]
            mix_ref[at, p * PAIR : (p + 1) * PAIR] = acc[p].T.astype(BF16)


def attend(first, low, qkv, vt):
    d, total = vt.shape
    n = total - CLIP
    pairs = d // PAIR
    return call(
        attend_body,
        (shape((n, d), BF16), shape((d // HEAD, n), F32)),
        (first,),
        (low, qkv, vt),
        scratch=(
            VMEM((pairs, PAIR, 2 * TQ), BF16),
            VMEM((pairs, PAIR, TQ), F32),
            VMEM((pairs, 1, 2 * TQ), F32),
            VMEM((pairs, 1, 2 * TQ), F32),
            VMEM((pairs, TK, 2 * TQ), F32),
            VMEM((pairs, TK, 2 * TQ), BF16),
        ),
        flops=16 * n * 1024 * d,
        moved=2 * d * (2 * n + 4 * total),
        room=24,
    )


def attend_back_body(fast, first_ref, *refs):
    if fast:
        slots_ref, side_ref, refs = refs[0], refs[1], refs[2:]
    low_ref, qkv_ref, kt_ref, xt_ref, mix_ref, log_ref, grad_ref, gt_ref = refs[:8]
    outs, refs = refs[8 : 10 if fast else 9], refs[10 if fast else 9 :]
    qt, gt, qs, gs, acc, dk_acc, dv_acc, s_ref, d_ref, p_ref, ds_ref, rows_ref, g_acc = refs
    n, d = grad_ref.shape
    pairs = d // PAIR
    start = jnp.minimum(first_ref[0], CLIP // ROWS)
    tiles = qkv_ref.shape[0] // ROWS

    @pl.loop(start, tiles)
    def _(tile):
        dk_acc[:, rows_at(tile)] = jnp.zeros((d, ROWS), F32)
        dv_acc[:, rows_at(tile)] = jnp.zeros((d, ROWS), F32)

    @pl.loop(start, CLIP // ROWS)
    def _(tile):
        for p in range(pairs):
            gt_ref[p * 3 * PAIR : (p * 3 + 1) * PAIR, rows_at(tile)] = jnp.zeros((PAIR, ROWS), BF16)

    @pl.loop(0, n // TQ)
    def _(i):
        at = pl.ds(pl.multiple_of(i * TQ, TQ), TQ)
        here = pl.ds(pl.multiple_of(CLIP + i * TQ, TQ), TQ)
        low, last, frame = sight(low_ref, at, i)
        for p in range(pairs):
            lanes = slice(p * PAIR, (p + 1) * PAIR)
            query = (qkv_ref[here, p * 3 * PAIR : (p * 3 + 1) * PAIR] * HEAD**-0.5).T
            grad = grad_ref[at, lanes]
            both = (grad.astype(F32) * mix_ref[at, lanes].astype(F32)).T
            grad = grad.T
            qt[p] = query
            gt[p] = grad
            qs[p] = split_heads(query)
            gs[p] = split_heads(grad)
            for h in range(2):
                wide = slice(h * TQ, (h + 1) * TQ)
                rows_ref[p, 0:1, wide] = jnp.sum(
                    both[h * HEAD : (h + 1) * HEAD], axis=0, keepdims=True
                )
                rows_ref[p, 1:2, wide] = log_ref[2 * p + h : 2 * p + h + 1, at]
        acc[...] = jnp.zeros_like(acc)

        def step(j, carry):
            keys = pl.ds(pl.multiple_of(j * TK, TK), TK)
            shift = j * (TK // FRAME)
            visible = (frame >= low - shift) & (frame <= last - shift)
            for p in range(pairs):
                one = (p * 3 + 1) * PAIR
                scores = mm(qkv_ref[keys, one : one + PAIR], qs[p])
                s_ref[p] = jnp.where(visible, scores, MASKED)
                d_ref[p] = mm(qkv_ref[keys, one + PAIR : one + 2 * PAIR], gs[p])
            for p in range(pairs):
                probs = jnp.exp(s_ref[p] - rows_ref[p, 1:2, :])
                p_ref[p] = probs.astype(BF16)
                ds_ref[p] = (probs * (d_ref[p] - rows_ref[p, 0:1, :])).astype(BF16)
            for p in range(pairs):
                for h in range(2):
                    part = slice(h * HEAD, (h + 1) * HEAD)
                    rows = slice(p * PAIR + h * HEAD, p * PAIR + (h + 1) * HEAD)
                    wide = slice(h * TQ, (h + 1) * TQ)
                    dv_acc[rows, keys] += mm_nt(gt[p, part, :], p_ref[p, :, wide])
                    dk_acc[rows, keys] += mm_nt(qt[p, part, :], ds_ref[p, :, wide])
                    acc[p, part, :] += mm(kt_ref[rows, keys], ds_ref[p, :, wide])
            return carry

        lax.fori_loop(first_ref[i], (CLIP + (i + 1) * TQ + TK - 1) // TK, step, 0)
        for p in range(pairs):
            gt_ref[p * 3 * PAIR : (p * 3 + 1) * PAIR, here] = (acc[p] * HEAD**-0.5).astype(BF16)

    @pl.loop(start, tiles)
    def _(tile):
        at = rows_at(tile)
        for p in range(pairs):
            one, rows = (p * 3 + 1) * PAIR, slice(p * PAIR, (p + 1) * PAIR)
            gt_ref[one : one + PAIR, at] = dk_acc[rows, at].astype(BF16)
            gt_ref[one + PAIR : one + 2 * PAIR, at] = dv_acc[rows, at].astype(BF16)

    wide = 6 * PAIR

    def weights(side):
        rows = pl.ds(pl.multiple_of(side * wide, wide), wide)
        g_acc[...] = mm_nt(xt_ref[:, CLIP:], gt_ref[rows, CLIP:])

        @pl.loop(start, CLIP // ROWS)
        def _(tile):
            g_acc[...] += mm_nt(xt_ref[:, rows_at(tile)], gt_ref[rows, rows_at(tile)])

    if not fast:
        for side in range(d // (2 * PAIR)):
            weights(side)
            outs[0][:, side * wide : (side + 1) * wide] = g_acc[...].astype(BF16)
        return
    rows = d // 8
    for k in range(2):
        side = side_ref[k]
        weights(side)
        for x in range(2):
            for r in range(8):
                slot = slots_ref[r * 4 + side * 2 + x] & 15
                outs[k][slot] = g_acc[
                    r * rows : (r + 1) * rows, x * 3 * PAIR : (x + 1) * 3 * PAIR
                ].astype(BF16)


def attend_back(first, low, qkv, kt, xt, mixture, logs, grad, slots=None, side=None):
    n, d = grad.shape
    total = qkv.shape[0]
    pairs = d // PAIR
    fast = slots is not None
    outs = (shape((3 * d, total), BF16),)
    if fast:
        outs += (shape((16, d // 8, 3 * d // 4), BF16),) * 2
    else:
        outs += (shape((d, 3 * d), BF16),)
    return call(
        functools.partial(attend_back_body, fast),
        outs,
        (first, slots, side) if fast else (first,),
        (low, qkv, kt, xt, mixture, logs, grad),
        scratch=(
            VMEM((pairs, PAIR, TQ), BF16),
            VMEM((pairs, PAIR, TQ), BF16),
            VMEM((pairs, PAIR, 2 * TQ), BF16),
            VMEM((pairs, PAIR, 2 * TQ), BF16),
            VMEM((pairs, PAIR, TQ), F32),
            VMEM((d, total), F32),
            VMEM((d, total), F32),
            VMEM((pairs, TK, 2 * TQ), F32),
            VMEM((pairs, TK, 2 * TQ), F32),
            VMEM((pairs, TK, 2 * TQ), BF16),
            VMEM((pairs, TK, 2 * TQ), BF16),
            VMEM((pairs, 8, 2 * TQ), F32),
            VMEM((d, 6 * PAIR), F32),
        ),
        flops=40 * n * 1024 * d,
        moved=2 * d * (2 * n + 8 * total),
        room=38,
    )


def chunks_of(far, near, size):
    return [
        (far.at[pl.ds(i, size), :], near.at[pl.ds(i, size), :])
        for i in range(0, near.shape[0], size)
    ]


def feed_blocks(slots_ref, side, mix_ref, act_ref, gh_ref, n2t_ref, lowt_ref, cott_ref, out_ref):
    d = n2t_ref.shape[0]
    one, wide, rows = d // 4, act_ref.shape[1] // 2, d // 8
    small = pl.ds(pl.multiple_of(side * 2 * one, 2 * one), 2 * one)
    spots = [[slots_ref[r * 4 + side * 2 + x] & 15 for r in range(8)] for x in range(2)]
    for start, size, left, right in (
        (0, one, lowt_ref, mix_ref[:, small]),
        (one, wide, n2t_ref, gh_ref),
        (one + wide, wide, cott_ref, act_ref),
    ):
        for x in range(2):
            grad = mm(left[...], right[:, x * size : (x + 1) * size]).astype(BF16)
            for r in range(8):
                out_ref[spots[x][r], :, start : start + size] = grad[r * rows : (r + 1) * rows]


def feed_kept_body(slots_ref, side_ref, *refs):
    feed_blocks(slots_ref, side_ref[0], *refs)


def feed_kept(slots, side, mixture, act, gh, n2t, lowt, cott):
    n, half = act.shape
    d = n2t.shape[0]
    return call(
        feed_kept_body,
        (shape((16, d // 8, d // 4 + half), BF16),),
        (slots, side),
        (mixture, act, gh, n2t, lowt, cott),
        flops=n * d * (4 * half + d),
        moved=2 * n * (4 * d + 2 * half),
        room=20,
    )[0]


def feed_body(fast, *refs):
    late = []
    if fast:
        spots_ref, slots_ref, side_ref, mix_ref, norm_ref, x_far, cot_far = refs[:7]
        far, refs = refs[7:15], refs[15:]
        out_ref, gmix_ref, gmid_ref, gain_ref, sent_ref, act_kept, gh_kept = refs[:7]
        (n2t_ref, lowt_ref, cott_ref), refs = refs[7:10], refs[10:]
        wo_ref, up_ref, down_ref, x_ref, cot_ref, sems, act_sent, gh_sent = refs
        acts, ghs = (act_kept, act_sent), (gh_kept, gh_sent)
        one, ff = wo_ref.shape[1] // 4, up_ref.shape[1] // 4
        near = fetch(chunks_of(x_far, x_ref, 256) + chunks_of(cot_far, cot_ref, 256), sems, 96)
        copies = place(
            spots_ref, far, sems,
            [(0, one, wo_ref), (one, ff, up_ref), (one + ff, ff, down_ref)],
        )
        late = [copy for k, copy in enumerate(copies) if k % 3]
        for copy in near + copies[::3]:
            copy.wait()
    else:
        x_ref, mix_ref, cot_ref, norm_ref, wo_ref, up_ref, down_ref = refs[:7]
        out_ref, gmix_ref, gmid_ref, gain_ref = refs[7:11]
        outs, refs = refs[11:14], refs[14:]
        act_ref, gh_ref, n2t_ref, lowt_ref, cott_ref = refs
        acts, ghs = (act_ref,), (gh_ref,)
    gain, shift = norm_ref[2:3, :], norm_ref[3:4, :]
    ff = up_ref.shape[1]
    d = x_ref.shape[1]
    wide = min(512, ff)
    held = acts[0].shape[1]
    root = 0.7978845608028654
    gain_ref[...] = jnp.zeros_like(gain_ref)
    rows = min(FEED_ROWS, x_ref.shape[0])

    @pl.loop(0, x_ref.shape[0] // rows)
    def _(tile):
        at = pl.ds(pl.multiple_of(tile * rows, rows), rows)
        cot = cot_ref[at, :]
        cott_ref[:, at] = cot.T
        middle = x_ref[at, :].astype(F32) + mm_nt(mix_ref[at, :], wo_ref[...])
        xhat, inverse = normalize(middle)
        n2 = xhat * gain + shift
        n2t_ref[:, at] = n2.T.astype(BF16)
        n2 = n2.astype(BF16)
        if late:

            @pl.when(tile == 0)
            def _():
                for copy in late:
                    copy.wait()

        out = middle
        second = jnp.zeros_like(middle)
        for k in range(len(acts)):
            base = side_ref[k] * held if fast else 0
            for c in range(held // wide):
                cols = pl.ds(pl.multiple_of(base + c * wide, wide), wide)
                to = slice(c * wide, (c + 1) * wide)
                hidden = mm(n2, up_ref[:, cols])
                square = hidden * hidden
                bent = jnp.tanh(hidden * (root + (root * 0.044715) * square))
                half = 0.5 + 0.5 * bent
                active = (hidden * half).astype(BF16)
                slope = half + hidden * (1.0 - bent * bent) * (
                    0.5 * root + (0.5 * root * 3 * 0.044715) * square
                )
                acts[k][at, to] = active
                out += mm_nt(active, down_ref[:, cols])
                gh = (mm(cot, down_ref[:, cols]) * slope).astype(BF16)
                ghs[k][at, to] = gh
                second += mm_nt(gh, up_ref[:, cols])
        out_ref[at, :] = out.astype(BF16)
        gain_ref[0:1, :] += jnp.sum(second * xhat, axis=0, keepdims=True)
        gain_ref[1:2, :] += jnp.sum(second, axis=0, keepdims=True)
        gmid = cot.astype(F32) + norm_back(second, xhat, inverse, gain)
        gmid_ref[at, :] = gmid
        lowt_ref[:, at] = gmid.T.astype(BF16)
        gmix_ref[at, :] = mm(gmid.astype(BF16), wo_ref[...]).astype(BF16)

    if fast:
        feed_blocks(
            slots_ref, side_ref[1], mix_ref, acts[1], ghs[1], n2t_ref, lowt_ref, cott_ref, sent_ref
        )
        return
    gup_ref, gdown_ref, gout_ref = outs
    for c in range(ff // wide):
        cols = slice(c * wide, (c + 1) * wide)
        gup_ref[:, cols] = mm(n2t_ref[...], gh_ref[:, cols]).astype(BF16)
        gdown_ref[:, cols] = mm(cott_ref[...], act_ref[:, cols]).astype(BF16)
    gout_ref[...] = mm(lowt_ref[...], mix_ref[...]).astype(BF16)


def feed(x, mixture, cot, norms, full, ff, spots=None, slots=None, side=None, far=()):
    n, d = x.shape
    fast = len(far) > 0
    outs = (shape((n, d), BF16), shape((n, d), BF16), shape((n, d), F32), shape((2, d), F32))
    turned = (shape((d, n), BF16),) * 3
    if fast:
        outs += (shape((16, d // 8, d // 4 + ff // 2), BF16),)
        outs += (shape((n, ff // 2), BF16),) * 2 + turned
        scratch = (
            VMEM((d, d), BF16),
            VMEM((d, ff), BF16),
            VMEM((d, ff), BF16),
            VMEM((n, d), BF16),
            VMEM((n, d), BF16),
            pltpu.SemaphoreType.DMA((96 + 2 * (n // 256),)),
            VMEM((n, ff // 2), BF16),
            VMEM((n, ff // 2), BF16),
        )
    else:
        outs += (shape((d, ff), BF16), shape((d, ff), BF16), shape((d, d), BF16))
        scratch = (VMEM((n, ff), BF16),) * 2 + tuple(VMEM(t.shape, BF16) for t in turned)
    return call(
        functools.partial(feed_body, fast),
        outs,
        (spots, slots, side) if fast else (),
        (mixture, norms) if fast else (x, mixture, cot, norms) + tuple(full),
        (x, cot) + tuple(far) if fast else (),
        scratch,
        flops=2 * n * d * (6 * ff + 3 * d),
        moved=2 * n * 6 * d + 8 * d * ff,
        room=34,
    )


def first_back_body(
    first_ref, norm_ref, w_ref, gmid_ref, gt_ref, own_far, halo_far, grad_ref, back_ref, gain_ref,
    own_ref, halo_ref, sems,
):
    for copy in fetch(((own_far, own_ref), (halo_far, halo_ref)), sems):
        copy.wait()
    gain = norm_ref[0:1, :]
    gain_ref[...] = jnp.zeros_like(gain_ref)
    start = jnp.minimum(first_ref[0], CLIP // ROWS)

    def rows_of(ref, tile, base, own):
        at = rows_at(tile)
        first = mm(w_ref[...], gt_ref[:, rows_at(tile, base)]).T
        xhat, inverse = normalize(ref[at, :].astype(F32))
        gain_ref[0:1, :] += jnp.sum(first * xhat, axis=0, keepdims=True)
        gain_ref[1:2, :] += jnp.sum(first, axis=0, keepdims=True)
        grad = norm_back(first, xhat, inverse, gain)
        if own:
            grad_ref[at, :] = gmid_ref[at, :] + grad
        else:
            back_ref[at, :] = grad.astype(BF16)

    @pl.loop(0, start)
    def _(tile):
        back_ref[rows_at(tile), :] = jnp.zeros((ROWS, back_ref.shape[1]), BF16)

    @pl.loop(start, CLIP // ROWS)
    def _(tile):
        rows_of(halo_ref, tile, 0, False)

    @pl.loop(0, own_ref.shape[0] // ROWS)
    def _(tile):
        rows_of(own_ref, tile, CLIP, True)


def first_back(first, own, halo, norms, w_qkv, gmid, gt):
    n, d = own.shape
    total = n + CLIP
    return call(
        first_back_body,
        (shape((n, d), F32), shape((CLIP, d), BF16), shape((2, d), F32)),
        (first,),
        (norms, w_qkv, gmid, gt),
        (own, halo),
        (VMEM(own.shape, BF16), VMEM(halo.shape, BF16), pltpu.SemaphoreType.DMA((2,))),
        flops=6 * d * d * total,
        moved=2 * d * (4 * total + 6 * n),
        room=24,
    )


class Grid:
    def __init__(self, dp, mp):
        self.dp, self.mp = dp, mp
        self.fast = (dp, mp) == (8, 4)

    def swap(self, value, z=0, y=0, x=0, c=0):
        bits = z * 8 + y * 4 + x * 2 + c
        return lax.ppermute(value, BOTH, [(i, i ^ bits) for i in range(self.dp * self.mp)])

    def spot(self):
        dp, mp = lax.axis_index("dp"), lax.axis_index("mp")
        return dp // 2, dp % 2, mp // 2, mp % 2

    def slots(self):
        z, y, x, c = self.spot()
        s = jnp.arange(32, dtype=jnp.int32)
        oz, oy, oc, ox = s >> 3, (s >> 2) & 1, (s >> 1) & 1, s & 1
        return (oc ^ c) * 16 + (ox ^ x) * 8 + (oy ^ y) * 4 + (oz ^ z)

    def spots(self):
        z, y, x, c = self.spot()
        s = jnp.arange(32, dtype=jnp.int32)
        oc, ox, oy, oz = (s >> 4) ^ c, ((s >> 3) & 1) ^ x, ((s >> 2) & 1) ^ y, (s & 3) ^ z
        return ((oz * 2 + oy) * 2 + oc) * 2 + ox

    def sides(self):
        c = lax.axis_index("mp") % 2
        return jnp.stack([c, 1 - c]).astype(jnp.int32)

    def gather_z(self, block):
        return jnp.stack([block] + [self.swap(block, z=k) for k in (1, 2, 3)])

    def across(self, held):
        return tuple(self.swap(a, c=1) for a in held)

    def gather_plane(self, near):
        return near, self.swap(near, y=1), self.swap(near, x=1), self.swap(near, y=1, x=1)

    def scatter_core(self, sent):
        return self.swap(sent, c=1)

    def scatter_plane(self, kept, got):
        own, one, two, three = (added(kept[k : k + 4], got[k : k + 4]) for k in (0, 4, 8, 12))
        return own, self.swap(one, y=1), self.swap(two, x=1), self.swap(three, y=1, x=1)

    def scatter_z(self, held):
        parts = [sum(a[k].astype(F32) for a in held).astype(BF16) for k in range(4)]
        return [parts[0]] + [self.swap(parts[k], z=k) for k in (1, 2, 3)]


def added(a, b):
    return (a.astype(F32) + b.astype(F32)).astype(BF16)


def whole_of(block):
    m = block.ndim - 2
    half = lax.all_gather(block, "dp", axis=m, tiled=True)
    return lax.all_gather(half, "mp", axis=m + 1, tiled=True)


def share_of(whole):
    m = whole.ndim - 2
    half = lax.psum_scatter(whole, "mp", scatter_dimension=m + 1, tiled=True)
    return lax.psum_scatter(half, "dp", scatter_dimension=m, tiled=True).astype(F32)


def beside(whole):
    d = whole.shape[1]
    return whole.reshape(3, d, d // PAIR, PAIR).transpose(1, 2, 0, 3).reshape(d, 3 * d)


def apart(wide):
    d = wide.shape[0]
    return wide.reshape(d, d // PAIR, 3, PAIR).transpose(2, 0, 1, 3).reshape(3, d, d)


def after(value, *others):
    return lax.optimization_barrier((value,) + others)[0]


def in_hbm(value):
    return pltpu.with_memory_space_constraint(value, pltpu.HBM)


def joined(*values):
    return lax.optimization_barrier(values)


def adam_update(
    weight, gradient, moment, square, average, step_rate, decay_rate, factor, fixed_one, fixed_two
):
    gradient = gradient * factor
    moment = beta_one * moment + (1.0 - beta_one) * gradient
    square = beta_two * square + (1.0 - beta_two) * gradient * gradient
    weight = weight - step_rate * (
        moment / fixed_one / (jnp.sqrt(square / fixed_two) + adam_eps) + decay_rate * weight
    )
    average = ema_decay * average + (1.0 - ema_decay) * weight
    return (weight, moment, square, average)


RATES = ((0.03, 0.1), (0.09, 0.1), (0.03, 0.1), (0.015, 0.1), (0.2, 0.0))


def total_body(*refs):
    rest, qkv, (one_ref, two_ref) = refs[:4], refs[4:8], refs[8:10]
    out_ref, up_ref, down_ref, qkv_ref, sums_ref = refs[10:]
    small, wide = out_ref.shape[1], up_ref.shape[1]
    width = sums_ref.shape[1]

    def sum_of(parts, at, size):
        a, b, c, d = (p[:, at : at + size].astype(F32) for p in parts)
        return (a + b) + (c + d)

    def squares(value):
        row = jnp.sum(value * value, axis=0, keepdims=True)
        return row if row.shape[1] == width else jnp.concatenate([row] + [jnp.zeros_like(row)] * (width // row.shape[1] - 1), axis=1)

    grad = sum_of(rest, 0, small)
    out_ref[...] = grad
    square = squares(grad)
    for ref, at in ((up_ref, small), (down_ref, small + wide)):
        grad = sum_of(rest, at, wide)
        ref[...] = grad
        square += squares(grad)
    for k in range(3):
        grad = sum_of(qkv, k * PAIR, PAIR)
        qkv_ref[k] = grad
        square += squares(grad)
    sums_ref[...] = jnp.zeros_like(sums_ref)
    sums_ref[0:2, :] = one_ref[...]
    sums_ref[2:4, :] = two_ref[...]
    sums_ref[4:5, :] = square


def totals(rest, qkv, gains_one, gains_two):
    rows, wide = rest[0].shape
    small = qkv[0].shape[1] // 3
    wide = (wide - small) // 2
    return call(
        total_body,
        (
            shape((rows, small), F32),
            shape((rows, wide), F32),
            shape((rows, wide), F32),
            shape((3, rows, small), F32),
            shape((8, gains_one.shape[1]), F32),
        ),
        (),
        tuple(rest) + tuple(qkv) + (gains_one, gains_two),
        moved=12 * rest[0].size,
        room=16,
    )


def adam_body(parts, scale_ref, *refs):
    sums, grads, refs = refs[:parts], refs[parts : parts + 4], refs[parts + 4 :]
    far, outs, norm_ref, held, sems = refs[:20], refs[20:44], refs[44], refs[45:65], refs[65]
    copies = fetch(tuple(zip(far, held)), sems)
    total = sums[0][...]
    if parts == 4:
        total = (total + sums[1][...]) + (sums[2][...] + sums[3][...])
    gains = total[0:4]
    square = jnp.sum(total[4:5]) + jnp.sum(gains * gains)
    norm = jnp.sqrt(jnp.broadcast_to(square, (1, 1)))
    norm_ref[0, 0] = jnp.sum(norm)
    factor = jnp.minimum(1.0, clip_limit / (norm + 1e-06))
    fixed_one, fixed_two = scale_ref[0], scale_ref[1]
    for copy in copies:
        copy.wait()
    for k, (rate, decay) in enumerate(RATES):
        weight, moment, square, average = (ref[...] for ref in held[4 * k : 4 * k + 4])
        grad = grads[k][...] if k < 4 else gains
        new = adam_update(
            weight, grad, moment, square, average, rate, decay, factor, fixed_one, fixed_two
        )
        for i in range(4):
            outs[4 * k + i][...] = new[i]
        if k < 4:
            outs[20 + k][...] = new[0].astype(BF16)


def adam(sums, scales, grads, sets):
    outs = tuple(shape(s[0].shape, F32) for s in sets for _ in range(4))
    outs += tuple(shape(s[0].shape, BF16) for s in sets[:4]) + (shape((1, 1), F32),)
    got = call(
        functools.partial(adam_body, len(sums)),
        outs,
        (scales,),
        tuple(sums) + tuple(grads),
        sum((tuple(s) for s in sets), ()),
        tuple(VMEM(a.shape, F32) for s in sets for a in s) + (pltpu.SemaphoreType.DMA((20,)),),
        flops=30 * sum(s[0].size for s in sets),
        moved=38 * sum(s[0].size for s in sets),
        room=16,
        small=(24,),
    )
    return [got[4 * k : 4 * k + 4] for k in range(5)], got[20:24], got[24]


def per_device(
    grid,
    tokens,
    cotangent,
    clip_ids,
    frame_ids,
    step,
    w_qkv,
    w_out,
    w_up,
    w_down,
    norm_params,
    moment_qkv,
    moment_out,
    moment_up,
    moment_down,
    moment_norm,
    square_qkv,
    square_out,
    square_up,
    square_down,
    square_norm,
    average_qkv,
    average_out,
    average_up,
    average_down,
    average_norm,
):
    n, d = tokens.shape
    back_steps = CLIP // n
    mp_index = lax.axis_index("mp")

    def shifted(value, k):
        pairs = [(i, i + k) for i in range(grid.mp) if 0 <= i + k < grid.mp]
        return lax.ppermute(value, "mp", pairs)

    frames = lax.dynamic_slice_in_dim(frame_ids, mp_index * n, n, 0)
    low = (CLIP + jnp.arange(n, dtype=jnp.int32)) // FRAME - frames
    first = low[::TQ] * FRAME // TK
    low = low.reshape(1, n)

    low_qkv, low_out, low_up, low_down = (
        jnp.concatenate([w_qkv[0], w_qkv[1], w_qkv[2]], axis=1).astype(BF16)
        if grid.fast
        else w_qkv.astype(BF16),
        w_out.T.astype(BF16),
        w_up.astype(BF16),
        w_down.T.astype(BF16),
    )
    if grid.fast:
        slots, spots, side = grid.slots(), grid.spots(), grid.sides()
        rest = jnp.concatenate([low_out, low_up, low_down], axis=1)
        near, halo = joined(grid.gather_z(low_qkv), shifted(tokens, 1))
        rest = after(rest, near)
        near_rest = grid.gather_z(rest)
        near_rest, *held = joined(near_rest, *grid.gather_plane(near))
        far = tuple(held) + grid.across(held)
        held = grid.gather_plane(near_rest)
        qkv, kt, vt, xt, full_qkv = project(first, tokens, halo, norm_params, None, spots, far)
        mixture, logs = attend(first, low, qkv, vt)
        mixture, *held = joined(mixture, *held)
        far = tuple(held) + grid.across(held)
        block_out, gmix, gmid, gains_two, sent, *parts = feed(
            in_hbm(tokens), mixture, in_hbm(cotangent), norm_params, None, 4 * low_up.shape[1],
            spots, slots, side, far,
        )
        kept = feed_kept(slots, side, mixture, *parts)
        got, gmix, kept = joined(grid.scatter_core(sent), gmix, kept)
        held = grid.scatter_plane(kept, got)
        gt, kept_qkv, sent = attend_back(
            first, low, qkv, kt, xt, mixture, logs, gmix, slots, side
        )
        sent, gt, *held = joined(sent, gt, *held)
        near_rest = grid.scatter_z(held)
        held = grid.scatter_plane(kept_qkv, grid.scatter_core(sent))
        grad_rows, back, gains_one = first_back(
            first, tokens, halo, norm_params, full_qkv, gmid, gt
        )
        back, *got = joined(back, *near_rest, *held)
        near_rest, held = got[:4], got[4:]
        near_qkv = grid.scatter_z(held)
        back, *near_qkv = joined(shifted(back, -1), *near_qkv)
        grad_out, grad_up, grad_down, grad_qkv, sums = totals(
            near_rest, near_qkv, gains_one, gains_two
        )
        sums = sums + grid.swap(sums, c=1)
        plane = [grid.swap(sums, y=b, x=a) for a, b in ((1, 0), (0, 1), (1, 1))]
        grad_tokens = after(grad_rows, sums) + back.astype(F32)
        sums = (sums + plane[0]) + (plane[1] + plane[2])
        sums = [sums] + [grid.swap(sums, z=k) for k in (1, 2, 3)]
        *sums, grad_tokens = joined(*sums, grad_tokens)
    else:
        halo = jnp.concatenate([shifted(tokens, k) for k in range(back_steps, 0, -1)])
        full_qkv = beside(whole_of(low_qkv))
        full = tuple(whole_of(a) for a in (low_out, low_up, low_down))
        qkv, kt, vt, xt = project(first, tokens, halo, norm_params, full_qkv)
        mixture, logs = attend(first, low, qkv, vt)
        block_out, gmix, gmid, gains_two, gup, gdown, gout = feed(
            tokens, mixture, cotangent, norm_params, full, full[1].shape[1]
        )
        grad_up, grad_down, grad_out = share_of(gup), share_of(gdown), share_of(gout)
        gt, gqkv = attend_back(first, low, qkv, kt, xt, mixture, logs, gmix)
        grad_qkv = share_of(apart(gqkv))
        grad_rows, back, gains_one = first_back(
            first, tokens, halo, norm_params, full_qkv, gmid, gt
        )
        grad_tokens = grad_rows
        for i, hop in enumerate(range(back_steps, 0, -1)):
            grad_tokens = grad_tokens + shifted(back[i * n : (i + 1) * n], -hop).astype(F32)
        weight_square = (
            jnp.sum(grad_qkv * grad_qkv)
            + jnp.sum(grad_out * grad_out)
            + jnp.sum(grad_up * grad_up)
            + jnp.sum(grad_down * grad_down)
        )
        row = jnp.zeros((4, d), F32).at[0, 0].set(weight_square)
        sums = [lax.psum(jnp.concatenate([gains_one, gains_two, row]), BOTH)]
    step_count = step[0].astype(F32)
    scales = jnp.stack(
        [1.0 - jnp.power(beta_one, step_count), 1.0 - jnp.power(beta_two, step_count)]
    )
    sets, copies, norm_value = adam(
        sums,
        scales,
        (grad_qkv, grad_out, grad_up, grad_down),
        (
            (w_qkv, moment_qkv, square_qkv, average_qkv),
            (w_out.T, moment_out.T, square_out.T, average_out.T),
            (w_up, moment_up, square_up, average_up),
            (w_down.T, moment_down.T, square_down.T, average_down.T),
            (norm_params, moment_norm, square_norm, average_norm),
        ),
    )
    norm_value = norm_value.reshape(())

    def turned(k, value):
        return value.T if k in (1, 3) else value

    return (
        (block_out, grad_tokens, norm_value)
        + tuple(turned(k, s[0]) for k, s in enumerate(sets))
        + tuple(turned(k, s[1]) for k, s in enumerate(sets))
        + tuple(turned(k, s[2]) for k, s in enumerate(sets))
        + tuple(turned(k, c) for k, c in enumerate(copies))
        + tuple(turned(k, s[3]) for k, s in enumerate(sets))
    )


def solution(mesh):
    rows = P(BOTH, None)
    weights = (P(None, "dp", "mp"), P("mp", "dp"), P("dp", "mp"), P("mp", "dp"))
    states = weights + (P(),)
    return jax.shard_map(
        functools.partial(per_device, Grid(mesh.shape["dp"], mesh.shape["mp"])),
        mesh=mesh,
        in_specs=(rows, rows, P("dp"), P("dp"), P()) + states * 4,
        out_specs=(rows, rows, P()) + states * 3 + weights + states,
        check_vma=False,
    )
```

```python
import functools

import jax
import jax.numpy as jnp
from jax import lax
from jax.experimental import pallas as pl
from jax.experimental.pallas import tpu as pltpu
from jax.sharding import PartitionSpec as P

HEAD = 64
CLIP = 1024
FRAME = 64

norm_eps = 1e-05
beta_one = 0.9
beta_two = 0.95
adam_eps = 1e-08
clip_limit = 1.0
ema_decay = 0.75

F32 = jnp.float32
BF16 = jnp.bfloat16
BOTH = ("dp", "mp")
VMEM = pltpu.VMEM
MASKED = -1e30
PAIR = 2 * HEAD
TQ = 256
TK = 256
ROWS = 256
FEED_ROWS = 1024


def mm(a, b):
    return lax.dot_general(a, b, (((1,), (0,)), ((), ())), preferred_element_type=F32)


def mm_nt(a, b):
    return lax.dot_general(a, b, (((1,), (1,)), ((), ())), preferred_element_type=F32)


def mm_tn(a, b):
    return lax.dot_general(a, b, (((0,), (0,)), ((), ())), preferred_element_type=F32)


def shape(dims, kind):
    return jax.ShapeDtypeStruct(tuple(dims), kind)


def call(body, outs, smem, ins, far=(), scratch=(), flops=0, moved=0, room=60, loose=(), small=()):
    return pl.pallas_call(
        body,
        out_shape=outs,
        in_specs=[pl.BlockSpec(memory_space=pltpu.SMEM)] * len(smem)
        + [pl.BlockSpec(memory_space=VMEM)] * len(ins)
        + [pl.BlockSpec(memory_space=pl.ANY)] * len(far),
        out_specs=tuple(
            pl.BlockSpec(
                memory_space=pl.ANY if i in loose else pltpu.SMEM if i in small else VMEM
            )
            for i in range(len(outs))
        ),
        scratch_shapes=list(scratch),
        compiler_params=pltpu.CompilerParams(vmem_limit_bytes=room << 20),
        cost_estimate=pl.CostEstimate(
            flops=int(flops), bytes_accessed=int(moved), transcendentals=0
        ),
    )(*smem, *ins, *far)


def rows_at(tile, base=0):
    return pl.ds(pl.multiple_of(base + tile * ROWS, ROWS), ROWS)


def normalize(rows):
    center = rows - jnp.mean(rows, axis=-1, keepdims=True)
    inverse = lax.rsqrt(jnp.mean(center * center, axis=-1, keepdims=True) + norm_eps)
    return center * inverse, inverse


def norm_back(grad, xhat, inverse, gain_row):
    gy = grad * gain_row
    return inverse * (
        gy
        - jnp.mean(gy, axis=-1, keepdims=True)
        - xhat * jnp.mean(gy * xhat, axis=-1, keepdims=True)
    )


def place(spots_ref, far, sems, parts):
    copies = []
    for s in range(32):
        row, col = spots_ref[s] // 4, spots_ref[s] % 4
        for t, (start, wide, whole) in enumerate(parts):
            block = far[s // 4].at[s % 4]
            rows = block.shape[-2]
            at = (
                pl.ds(pl.multiple_of(row * rows, rows), rows),
                pl.ds(pl.multiple_of(col * wide, wide), wide),
            )
            lead = (slice(None),) * (len(block.shape) - 2)
            copies.append(
                pltpu.make_async_copy(
                    block.at[lead + (slice(None), pl.ds(start, wide))],
                    whole.at[lead + at],
                    sems.at[s * len(parts) + t],
                )
            )
    for copy in copies:
        copy.start()
    return copies


def fetch(pairs, sems, start=0):
    copies = [
        pltpu.make_async_copy(far, near, sems.at[start + k]) for k, (far, near) in enumerate(pairs)
    ]
    for copy in copies:
        copy.start()
    return copies


def project_body(fast, first_ref, *refs):
    if fast:
        spots_ref, norm_ref, own_far, halo_far = refs[:4]
        far, refs = refs[4:12], refs[12:]
        qkv_ref, kt_ref, vt_ref, xt_ref, w_ref, own_ref, halo_ref, sems = refs
        copies = place(spots_ref, far, sems, [(0, far[0].shape[-1], w_ref)])
        copies += fetch(((own_far, own_ref), (halo_far, halo_ref)), sems, 32)
        for copy in copies:
            copy.wait()
    else:
        own_ref, halo_ref, norm_ref, w_ref, qkv_ref, kt_ref, vt_ref, xt_ref = refs
    gain, shift = norm_ref[0:1, :], norm_ref[1:2, :]
    pairs = w_ref.shape[1] // (3 * PAIR)

    def rows_of(ref, tile, base):
        to = rows_at(tile, base)
        xhat, _ = normalize(ref[rows_at(tile), :].astype(F32))
        xn = xhat * gain + shift
        xt_ref[:, to] = xn.T.astype(BF16)
        xn = xn.astype(BF16)
        for p in range(pairs):
            at, lanes = p * 3 * PAIR, slice(p * PAIR, (p + 1) * PAIR)
            qkv = mm(xn, w_ref[:, at : at + 3 * PAIR])
            qkv_ref[to, at : at + 3 * PAIR] = qkv.astype(BF16)
            kt_ref[lanes, to] = qkv[:, PAIR : 2 * PAIR].T.astype(BF16)
            vt_ref[lanes, to] = qkv[:, 2 * PAIR :].T.astype(BF16)

    @pl.loop(jnp.minimum(first_ref[0], CLIP // ROWS), CLIP // ROWS)
    def _(tile):
        rows_of(halo_ref, tile, 0)

    @pl.loop(0, own_ref.shape[0] // ROWS)
    def _(tile):
        rows_of(own_ref, tile, CLIP)


def project(first, own, halo, norms, w_qkv, spots=None, far=()):
    n, d = own.shape
    total = n + CLIP
    fast = len(far) > 0
    outs = (
        shape((total, 3 * d), BF16),
        shape((d, total), BF16),
        shape((d, total), BF16),
        shape((d, total), BF16),
    )
    if fast:
        outs += (shape((d, 3 * d), BF16),)
    return call(
        functools.partial(project_body, fast),
        outs,
        (first, spots) if fast else (first,),
        (norms,) if fast else (own, halo, norms, w_qkv),
        (own, halo) + tuple(far) if fast else (),
        (VMEM(own.shape, BF16), VMEM(halo.shape, BF16), pltpu.SemaphoreType.DMA((34,)))
        if fast
        else (),
        flops=6 * d * d * total,
        moved=2 * d * (6 * total + 2 * n) + 6 * d * d,
        room=24,
    )


def split_heads(pair):
    zero = jnp.zeros((HEAD, pair.shape[1]), pair.dtype)
    return jnp.concatenate(
        [
            jnp.concatenate([pair[:HEAD], zero], axis=1),
            jnp.concatenate([zero, pair[HEAD:]], axis=1),
        ]
    )


def twice(row):
    return jnp.concatenate([row, row], axis=1)


def sight(low_ref, at, i):
    spot = lax.broadcasted_iota(jnp.int32, (1, TQ), 1)
    last = ((CLIP + i * TQ) + spot) >> 6
    frame = lax.broadcasted_iota(jnp.int32, (TK, 2 * TQ), 0) >> 6
    return twice(low_ref[0:1, at]), twice(last), frame


def attend_body(
    first_ref, low_ref, qkv_ref, vt_ref, mix_ref, log_ref, qt, acc, top, total, s_ref, p_ref
):
    pairs = mix_ref.shape[1] // PAIR

    @pl.loop(0, mix_ref.shape[0] // TQ)
    def _(i):
        at = pl.ds(pl.multiple_of(i * TQ, TQ), TQ)
        low, last, frame = sight(low_ref, at, i)
        here = pl.ds(pl.multiple_of(CLIP + i * TQ, TQ), TQ)
        for p in range(pairs):
            query = qkv_ref[here, p * 3 * PAIR : (p * 3 + 1) * PAIR] * HEAD**-0.5
            qt[p] = split_heads(query.T)
        acc[...] = jnp.zeros_like(acc)
        top[...] = jnp.full_like(top, MASKED)
        total[...] = jnp.zeros_like(total)

        def step(j, carry):
            keys = pl.ds(pl.multiple_of(j * TK, TK), TK)
            shift = j * (TK // FRAME)
            visible = (frame >= low - shift) & (frame <= last - shift)
            for p in range(pairs):
                scores = mm(qkv_ref[keys, (p * 3 + 1) * PAIR : (p * 3 + 2) * PAIR], qt[p])
                s_ref[p] = jnp.where(visible, scores, MASKED)
            for p in range(pairs):
                scores = s_ref[p]
                old = top[p]
                new = jnp.maximum(old, jnp.max(scores, axis=0, keepdims=True))
                weights = jnp.exp(scores - new)
                keep = jnp.exp(old - new)
                top[p] = new
                total[p] = total[p] * keep + jnp.sum(weights, axis=0, keepdims=True)
                p_ref[p] = weights.astype(BF16)
                for h in range(2):
                    part = slice(h * HEAD, (h + 1) * HEAD)
                    acc[p, part, :] = acc[p, part, :] * keep[:, h * TQ : (h + 1) * TQ]
            for p in range(pairs):
                for h in range(2):
                    part = slice(h * HEAD, (h + 1) * HEAD)
                    values = vt_ref[p * PAIR + h * HEAD : p * PAIR + (h + 1) * HEAD, keys]
                    acc[p, part, :] += mm(values, p_ref[p, :, h * TQ : (h + 1) * TQ])
            return carry

        lax.fori_loop(first_ref[i], (CLIP + (i + 1) * TQ + TK - 1) // TK, step, 0)
        for p in range(pairs):
            sums = total[p]
            logs = top[p] + jnp.log(sums)
            inverse = 1.0 / sums
            for h in range(2):
                part = slice(h * HEAD, (h + 1) * HEAD)
                wide = slice(h * TQ, (h + 1) * TQ)
                acc[p, part, :] = acc[p, part, :] * inverse[:, wide]
                log_ref[2 * p + h : 2 * p + h + 1, at] = logs[:, wide]
            mix_ref[at, p * PAIR : (p + 1) * PAIR] = acc[p].T.astype(BF16)


def attend(first, low, qkv, vt):
    d, total = vt.shape
    n = total - CLIP
    pairs = d // PAIR
    return call(
        attend_body,
        (shape((n, d), BF16), shape((d // HEAD, n), F32)),
        (first,),
        (low, qkv, vt),
        scratch=(
            VMEM((pairs, PAIR, 2 * TQ), BF16),
            VMEM((pairs, PAIR, TQ), F32),
            VMEM((pairs, 1, 2 * TQ), F32),
            VMEM((pairs, 1, 2 * TQ), F32),
            VMEM((pairs, TK, 2 * TQ), F32),
            VMEM((pairs, TK, 2 * TQ), BF16),
        ),
        flops=16 * n * 1024 * d,
        moved=2 * d * (2 * n + 4 * total),
        room=24,
    )


def attend_back_body(fast, first_ref, *refs):
    if fast:
        slots_ref, side_ref, refs = refs[0], refs[1], refs[2:]
    low_ref, qkv_ref, kt_ref, xt_ref, mix_ref, log_ref, grad_ref, gt_ref = refs[:8]
    outs, refs = refs[8 : 10 if fast else 9], refs[10 if fast else 9 :]
    qt, gt, qs, gs, acc, dk_acc, dv_acc, s_ref, d_ref, p_ref, ds_ref, rows_ref, g_acc = refs
    n, d = grad_ref.shape
    pairs = d // PAIR
    start = jnp.minimum(first_ref[0], CLIP // ROWS)
    tiles = qkv_ref.shape[0] // ROWS

    @pl.loop(start, tiles)
    def _(tile):
        dk_acc[:, rows_at(tile)] = jnp.zeros((d, ROWS), F32)
        dv_acc[:, rows_at(tile)] = jnp.zeros((d, ROWS), F32)

    @pl.loop(start, CLIP // ROWS)
    def _(tile):
        for p in range(pairs):
            gt_ref[p * 3 * PAIR : (p * 3 + 1) * PAIR, rows_at(tile)] = jnp.zeros((PAIR, ROWS), BF16)

    @pl.loop(0, n // TQ)
    def _(i):
        at = pl.ds(pl.multiple_of(i * TQ, TQ), TQ)
        here = pl.ds(pl.multiple_of(CLIP + i * TQ, TQ), TQ)
        low, last, frame = sight(low_ref, at, i)
        for p in range(pairs):
            lanes = slice(p * PAIR, (p + 1) * PAIR)
            query = (qkv_ref[here, p * 3 * PAIR : (p * 3 + 1) * PAIR] * HEAD**-0.5).T
            grad = grad_ref[at, lanes]
            both = (grad.astype(F32) * mix_ref[at, lanes].astype(F32)).T
            grad = grad.T
            qt[p] = query
            gt[p] = grad
            qs[p] = split_heads(query)
            gs[p] = split_heads(grad)
            for h in range(2):
                wide = slice(h * TQ, (h + 1) * TQ)
                rows_ref[p, 0:1, wide] = jnp.sum(
                    both[h * HEAD : (h + 1) * HEAD], axis=0, keepdims=True
                )
                rows_ref[p, 1:2, wide] = log_ref[2 * p + h : 2 * p + h + 1, at]
        acc[...] = jnp.zeros_like(acc)

        def step(j, carry):
            keys = pl.ds(pl.multiple_of(j * TK, TK), TK)
            shift = j * (TK // FRAME)
            visible = (frame >= low - shift) & (frame <= last - shift)
            for p in range(pairs):
                one = (p * 3 + 1) * PAIR
                scores = mm(qkv_ref[keys, one : one + PAIR], qs[p])
                s_ref[p] = jnp.where(visible, scores, MASKED)
                d_ref[p] = mm(qkv_ref[keys, one + PAIR : one + 2 * PAIR], gs[p])
            for p in range(pairs):
                probs = jnp.exp(s_ref[p] - rows_ref[p, 1:2, :])
                p_ref[p] = probs.astype(BF16)
                ds_ref[p] = (probs * (d_ref[p] - rows_ref[p, 0:1, :])).astype(BF16)
            for p in range(pairs):
                for h in range(2):
                    part = slice(h * HEAD, (h + 1) * HEAD)
                    rows = slice(p * PAIR + h * HEAD, p * PAIR + (h + 1) * HEAD)
                    wide = slice(h * TQ, (h + 1) * TQ)
                    dv_acc[rows, keys] += mm_nt(gt[p, part, :], p_ref[p, :, wide])
                    dk_acc[rows, keys] += mm_nt(qt[p, part, :], ds_ref[p, :, wide])
                    acc[p, part, :] += mm(kt_ref[rows, keys], ds_ref[p, :, wide])
            return carry

        lax.fori_loop(first_ref[i], (CLIP + (i + 1) * TQ + TK - 1) // TK, step, 0)
        for p in range(pairs):
            gt_ref[p * 3 * PAIR : (p * 3 + 1) * PAIR, here] = (acc[p] * HEAD**-0.5).astype(BF16)

    @pl.loop(start, tiles)
    def _(tile):
        at = rows_at(tile)
        for p in range(pairs):
            one, rows = (p * 3 + 1) * PAIR, slice(p * PAIR, (p + 1) * PAIR)
            gt_ref[one : one + PAIR, at] = dk_acc[rows, at].astype(BF16)
            gt_ref[one + PAIR : one + 2 * PAIR, at] = dv_acc[rows, at].astype(BF16)

    wide = 6 * PAIR

    def weights(side):
        rows = pl.ds(pl.multiple_of(side * wide, wide), wide)
        g_acc[...] = mm_nt(xt_ref[:, CLIP:], gt_ref[rows, CLIP:])

        @pl.loop(start, CLIP // ROWS)
        def _(tile):
            g_acc[...] += mm_nt(xt_ref[:, rows_at(tile)], gt_ref[rows, rows_at(tile)])

    if not fast:
        for side in range(d // (2 * PAIR)):
            weights(side)
            outs[0][:, side * wide : (side + 1) * wide] = g_acc[...].astype(BF16)
        return
    rows = d // 8
    for k in range(2):
        side = side_ref[k]
        weights(side)
        for x in range(2):
            for r in range(8):
                slot = slots_ref[r * 4 + side * 2 + x] & 15
                outs[k][slot] = g_acc[
                    r * rows : (r + 1) * rows, x * 3 * PAIR : (x + 1) * 3 * PAIR
                ].astype(BF16)


def attend_back(first, low, qkv, kt, xt, mixture, logs, grad, slots=None, side=None):
    n, d = grad.shape
    total = qkv.shape[0]
    pairs = d // PAIR
    fast = slots is not None
    outs = (shape((3 * d, total), BF16),)
    if fast:
        outs += (shape((16, d // 8, 3 * d // 4), BF16),) * 2
    else:
        outs += (shape((d, 3 * d), BF16),)
    return call(
        functools.partial(attend_back_body, fast),
        outs,
        (first, slots, side) if fast else (first,),
        (low, qkv, kt, xt, mixture, logs, grad),
        scratch=(
            VMEM((pairs, PAIR, TQ), BF16),
            VMEM((pairs, PAIR, TQ), BF16),
            VMEM((pairs, PAIR, 2 * TQ), BF16),
            VMEM((pairs, PAIR, 2 * TQ), BF16),
            VMEM((pairs, PAIR, TQ), F32),
            VMEM((d, total), F32),
            VMEM((d, total), F32),
            VMEM((pairs, TK, 2 * TQ), F32),
            VMEM((pairs, TK, 2 * TQ), F32),
            VMEM((pairs, TK, 2 * TQ), BF16),
            VMEM((pairs, TK, 2 * TQ), BF16),
            VMEM((pairs, 8, 2 * TQ), F32),
            VMEM((d, 6 * PAIR), F32),
        ),
        flops=40 * n * 1024 * d,
        moved=2 * d * (2 * n + 8 * total),
        room=38,
    )


def chunks_of(far, near, size):
    return [
        (far.at[pl.ds(i, size), :], near.at[pl.ds(i, size), :])
        for i in range(0, near.shape[0], size)
    ]


def feed_blocks(slots_ref, side, mix_ref, act_ref, gh_ref, n2t_ref, lowt_ref, cott_ref, out_ref):
    d = n2t_ref.shape[0]
    one, wide, rows = d // 4, act_ref.shape[1] // 2, d // 8
    small = pl.ds(pl.multiple_of(side * 2 * one, 2 * one), 2 * one)
    spots = [[slots_ref[r * 4 + side * 2 + x] & 15 for r in range(8)] for x in range(2)]
    for start, size, left, right in (
        (0, one, lowt_ref, mix_ref[:, small]),
        (one, wide, n2t_ref, gh_ref),
        (one + wide, wide, cott_ref, act_ref),
    ):
        for x in range(2):
            grad = mm(left[...], right[:, x * size : (x + 1) * size]).astype(BF16)
            for r in range(8):
                out_ref[spots[x][r], :, start : start + size] = grad[r * rows : (r + 1) * rows]


def feed_kept_body(slots_ref, side_ref, *refs):
    feed_blocks(slots_ref, side_ref[0], *refs)


def feed_kept(slots, side, mixture, act, gh, n2t, lowt, cott):
    n, half = act.shape
    d = n2t.shape[0]
    return call(
        feed_kept_body,
        (shape((16, d // 8, d // 4 + half), BF16),),
        (slots, side),
        (mixture, act, gh, n2t, lowt, cott),
        flops=n * d * (4 * half + d),
        moved=2 * n * (4 * d + 2 * half),
        room=20,
    )[0]


def feed_body(fast, *refs):
    late = []
    if fast:
        spots_ref, slots_ref, side_ref, mix_ref, norm_ref, x_far, cot_far = refs[:7]
        far, refs = refs[7:15], refs[15:]
        out_ref, gmix_ref, gmid_ref, gain_ref, sent_ref, act_kept, gh_kept = refs[:7]
        (n2t_ref, lowt_ref, cott_ref), refs = refs[7:10], refs[10:]
        wo_ref, up_ref, down_ref, x_ref, cot_ref, sems, act_sent, gh_sent = refs
        acts, ghs = (act_kept, act_sent), (gh_kept, gh_sent)
        one, ff = wo_ref.shape[1] // 4, up_ref.shape[1] // 4
        near = fetch(chunks_of(x_far, x_ref, 256) + chunks_of(cot_far, cot_ref, 256), sems, 96)
        copies = place(
            spots_ref, far, sems,
            [(0, one, wo_ref), (one, ff, up_ref), (one + ff, ff, down_ref)],
        )
        late = [copy for k, copy in enumerate(copies) if k % 3]
        for copy in near + copies[::3]:
            copy.wait()
    else:
        x_ref, mix_ref, cot_ref, norm_ref, wo_ref, up_ref, down_ref = refs[:7]
        out_ref, gmix_ref, gmid_ref, gain_ref = refs[7:11]
        outs, refs = refs[11:14], refs[14:]
        act_ref, gh_ref, n2t_ref, lowt_ref, cott_ref = refs
        acts, ghs = (act_ref,), (gh_ref,)
    gain, shift = norm_ref[2:3, :], norm_ref[3:4, :]
    ff = up_ref.shape[1]
    d = x_ref.shape[1]
    wide = min(512, ff)
    held = acts[0].shape[1]
    root = 0.7978845608028654
    gain_ref[...] = jnp.zeros_like(gain_ref)
    rows = min(FEED_ROWS, x_ref.shape[0])

    @pl.loop(0, x_ref.shape[0] // rows)
    def _(tile):
        at = pl.ds(pl.multiple_of(tile * rows, rows), rows)
        cot = cot_ref[at, :]
        cott_ref[:, at] = cot.T
        middle = x_ref[at, :].astype(F32) + mm_nt(mix_ref[at, :], wo_ref[...])
        xhat, inverse = normalize(middle)
        n2 = xhat * gain + shift
        n2t_ref[:, at] = n2.T.astype(BF16)
        n2 = n2.astype(BF16)
        if late:

            @pl.when(tile == 0)
            def _():
                for copy in late:
                    copy.wait()

        out = middle
        second = jnp.zeros_like(middle)
        for k in range(len(acts)):
            base = side_ref[k] * held if fast else 0
            for c in range(held // wide):
                cols = pl.ds(pl.multiple_of(base + c * wide, wide), wide)
                to = slice(c * wide, (c + 1) * wide)
                hidden = mm(n2, up_ref[:, cols])
                square = hidden * hidden
                bent = jnp.tanh(hidden * (root + (root * 0.044715) * square))
                half = 0.5 + 0.5 * bent
                active = (hidden * half).astype(BF16)
                slope = half + hidden * (1.0 - bent * bent) * (
                    0.5 * root + (0.5 * root * 3 * 0.044715) * square
                )
                acts[k][at, to] = active
                out += mm_nt(active, down_ref[:, cols])
                gh = (mm(cot, down_ref[:, cols]) * slope).astype(BF16)
                ghs[k][at, to] = gh
                second += mm_nt(gh, up_ref[:, cols])
        out_ref[at, :] = out.astype(BF16)
        gain_ref[0:1, :] += jnp.sum(second * xhat, axis=0, keepdims=True)
        gain_ref[1:2, :] += jnp.sum(second, axis=0, keepdims=True)
        gmid = cot.astype(F32) + norm_back(second, xhat, inverse, gain)
        gmid_ref[at, :] = gmid
        lowt_ref[:, at] = gmid.T.astype(BF16)
        gmix_ref[at, :] = mm(gmid.astype(BF16), wo_ref[...]).astype(BF16)

    if fast:
        feed_blocks(
            slots_ref, side_ref[1], mix_ref, acts[1], ghs[1], n2t_ref, lowt_ref, cott_ref, sent_ref
        )
        return
    gup_ref, gdown_ref, gout_ref = outs
    for c in range(ff // wide):
        cols = slice(c * wide, (c + 1) * wide)
        gup_ref[:, cols] = mm(n2t_ref[...], gh_ref[:, cols]).astype(BF16)
        gdown_ref[:, cols] = mm(cott_ref[...], act_ref[:, cols]).astype(BF16)
    gout_ref[...] = mm(lowt_ref[...], mix_ref[...]).astype(BF16)


def feed(x, mixture, cot, norms, full, ff, spots=None, slots=None, side=None, far=()):
    n, d = x.shape
    fast = len(far) > 0
    outs = (shape((n, d), BF16), shape((n, d), BF16), shape((n, d), F32), shape((2, d), F32))
    turned = (shape((d, n), BF16),) * 3
    if fast:
        outs += (shape((16, d // 8, d // 4 + ff // 2), BF16),)
        outs += (shape((n, ff // 2), BF16),) * 2 + turned
        scratch = (
            VMEM((d, d), BF16),
            VMEM((d, ff), BF16),
            VMEM((d, ff), BF16),
            VMEM((n, d), BF16),
            VMEM((n, d), BF16),
            pltpu.SemaphoreType.DMA((96 + 2 * (n // 256),)),
            VMEM((n, ff // 2), BF16),
            VMEM((n, ff // 2), BF16),
        )
    else:
        outs += (shape((d, ff), BF16), shape((d, ff), BF16), shape((d, d), BF16))
        scratch = (VMEM((n, ff), BF16),) * 2 + tuple(VMEM(t.shape, BF16) for t in turned)
    return call(
        functools.partial(feed_body, fast),
        outs,
        (spots, slots, side) if fast else (),
        (mixture, norms) if fast else (x, mixture, cot, norms) + tuple(full),
        (x, cot) + tuple(far) if fast else (),
        scratch,
        flops=2 * n * d * (6 * ff + 3 * d),
        moved=2 * n * 6 * d + 8 * d * ff,
        room=34,
    )


def first_back_body(
    first_ref, norm_ref, w_ref, gmid_ref, gt_ref, own_far, halo_far, grad_ref, back_ref, gain_ref,
    own_ref, halo_ref, sems,
):
    for copy in fetch(((own_far, own_ref), (halo_far, halo_ref)), sems):
        copy.wait()
    gain = norm_ref[0:1, :]
    gain_ref[...] = jnp.zeros_like(gain_ref)
    start = jnp.minimum(first_ref[0], CLIP // ROWS)

    def rows_of(ref, tile, base, own):
        at = rows_at(tile)
        first = mm(w_ref[...], gt_ref[:, rows_at(tile, base)]).T
        xhat, inverse = normalize(ref[at, :].astype(F32))
        gain_ref[0:1, :] += jnp.sum(first * xhat, axis=0, keepdims=True)
        gain_ref[1:2, :] += jnp.sum(first, axis=0, keepdims=True)
        grad = norm_back(first, xhat, inverse, gain)
        if own:
            grad_ref[at, :] = gmid_ref[at, :] + grad
        else:
            back_ref[at, :] = grad.astype(BF16)

    @pl.loop(0, start)
    def _(tile):
        back_ref[rows_at(tile), :] = jnp.zeros((ROWS, back_ref.shape[1]), BF16)

    @pl.loop(start, CLIP // ROWS)
    def _(tile):
        rows_of(halo_ref, tile, 0, False)

    @pl.loop(0, own_ref.shape[0] // ROWS)
    def _(tile):
        rows_of(own_ref, tile, CLIP, True)


def first_back(first, own, halo, norms, w_qkv, gmid, gt):
    n, d = own.shape
    total = n + CLIP
    return call(
        first_back_body,
        (shape((n, d), F32), shape((CLIP, d), BF16), shape((2, d), F32)),
        (first,),
        (norms, w_qkv, gmid, gt),
        (own, halo),
        (VMEM(own.shape, BF16), VMEM(halo.shape, BF16), pltpu.SemaphoreType.DMA((2,))),
        flops=6 * d * d * total,
        moved=2 * d * (4 * total + 6 * n),
        room=24,
    )


class Grid:
    def __init__(self, dp, mp):
        self.dp, self.mp = dp, mp
        self.fast = (dp, mp) == (8, 4)

    def swap(self, value, z=0, y=0, x=0, c=0):
        bits = z * 8 + y * 4 + x * 2 + c
        return lax.ppermute(value, BOTH, [(i, i ^ bits) for i in range(self.dp * self.mp)])

    def spot(self):
        dp, mp = lax.axis_index("dp"), lax.axis_index("mp")
        return dp // 2, dp % 2, mp // 2, mp % 2

    def slots(self):
        z, y, x, c = self.spot()
        s = jnp.arange(32, dtype=jnp.int32)
        oz, oy, oc, ox = s >> 3, (s >> 2) & 1, (s >> 1) & 1, s & 1
        return (oc ^ c) * 16 + (ox ^ x) * 8 + (oy ^ y) * 4 + (oz ^ z)

    def spots(self):
        z, y, x, c = self.spot()
        s = jnp.arange(32, dtype=jnp.int32)
        oc, ox, oy, oz = (s >> 4) ^ c, ((s >> 3) & 1) ^ x, ((s >> 2) & 1) ^ y, (s & 3) ^ z
        return ((oz * 2 + oy) * 2 + oc) * 2 + ox

    def sides(self):
        c = lax.axis_index("mp") % 2
        return jnp.stack([c, 1 - c]).astype(jnp.int32)

    def gather_z(self, block):
        return jnp.stack([block] + [self.swap(block, z=k) for k in (1, 2, 3)])

    def across(self, held):
        return tuple(self.swap(a, c=1) for a in held)

    def gather_plane(self, near):
        return near, self.swap(near, y=1), self.swap(near, x=1), self.swap(near, y=1, x=1)

    def scatter_core(self, sent):
        return self.swap(sent, c=1)

    def scatter_plane(self, kept, got):
        own, one, two, three = (added(kept[k : k + 4], got[k : k + 4]) for k in (0, 4, 8, 12))
        return own, self.swap(one, y=1), self.swap(two, x=1), self.swap(three, y=1, x=1)

    def scatter_z(self, held):
        parts = [sum(a[k].astype(F32) for a in held).astype(BF16) for k in range(4)]
        return [parts[0]] + [self.swap(parts[k], z=k) for k in (1, 2, 3)]


def added(a, b):
    return (a.astype(F32) + b.astype(F32)).astype(BF16)


def whole_of(block):
    m = block.ndim - 2
    half = lax.all_gather(block, "dp", axis=m, tiled=True)
    return lax.all_gather(half, "mp", axis=m + 1, tiled=True)


def share_of(whole):
    m = whole.ndim - 2
    half = lax.psum_scatter(whole, "mp", scatter_dimension=m + 1, tiled=True)
    return lax.psum_scatter(half, "dp", scatter_dimension=m, tiled=True).astype(F32)


def beside(whole):
    d = whole.shape[1]
    return whole.reshape(3, d, d // PAIR, PAIR).transpose(1, 2, 0, 3).reshape(d, 3 * d)


def apart(wide):
    d = wide.shape[0]
    return wide.reshape(d, d // PAIR, 3, PAIR).transpose(2, 0, 1, 3).reshape(3, d, d)


def after(value, *others):
    return lax.optimization_barrier((value,) + others)[0]


def in_hbm(value):
    return pltpu.with_memory_space_constraint(value, pltpu.HBM)


def joined(*values):
    return lax.optimization_barrier(values)


def adam_update(
    weight, gradient, moment, square, average, step_rate, decay_rate, factor, fixed_one, fixed_two
):
    gradient = gradient * factor
    moment = beta_one * moment + (1.0 - beta_one) * gradient
    square = beta_two * square + (1.0 - beta_two) * gradient * gradient
    weight = weight - step_rate * (
        moment / fixed_one / (jnp.sqrt(square / fixed_two) + adam_eps) + decay_rate * weight
    )
    average = ema_decay * average + (1.0 - ema_decay) * weight
    return (weight, moment, square, average)


RATES = ((0.03, 0.1), (0.09, 0.1), (0.03, 0.1), (0.015, 0.1), (0.2, 0.0))


def total_body(*refs):
    rest, qkv, (one_ref, two_ref) = refs[:4], refs[4:8], refs[8:10]
    out_ref, up_ref, down_ref, qkv_ref, sums_ref = refs[10:]
    small, wide = out_ref.shape[1], up_ref.shape[1]
    width = sums_ref.shape[1]

    def sum_of(parts, at, size):
        a, b, c, d = (p[:, at : at + size].astype(F32) for p in parts)
        return (a + b) + (c + d)

    def squares(value):
        row = jnp.sum(value * value, axis=0, keepdims=True)
        return row if row.shape[1] == width else jnp.concatenate([row] + [jnp.zeros_like(row)] * (width // row.shape[1] - 1), axis=1)

    grad = sum_of(rest, 0, small)
    out_ref[...] = grad
    square = squares(grad)
    for ref, at in ((up_ref, small), (down_ref, small + wide)):
        grad = sum_of(rest, at, wide)
        ref[...] = grad
        square += squares(grad)
    for k in range(3):
        grad = sum_of(qkv, k * PAIR, PAIR)
        qkv_ref[k] = grad
        square += squares(grad)
    sums_ref[...] = jnp.zeros_like(sums_ref)
    sums_ref[0:2, :] = one_ref[...]
    sums_ref[2:4, :] = two_ref[...]
    sums_ref[4:5, :] = square


def totals(rest, qkv, gains_one, gains_two):
    rows, wide = rest[0].shape
    small = qkv[0].shape[1] // 3
    wide = (wide - small) // 2
    return call(
        total_body,
        (
            shape((rows, small), F32),
            shape((rows, wide), F32),
            shape((rows, wide), F32),
            shape((3, rows, small), F32),
            shape((8, gains_one.shape[1]), F32),
        ),
        (),
        tuple(rest) + tuple(qkv) + (gains_one, gains_two),
        moved=12 * rest[0].size,
        room=16,
    )


def load_body(*refs):
    count = len(refs) // 2
    copies = fetch(tuple(zip(refs[:count], refs[count:-1])), refs[-1])
    for copy in copies:
        copy.wait()


def load(values):
    return call(
        load_body,
        tuple(shape(v.shape, v.dtype) for v in values),
        (),
        (),
        tuple(in_hbm(v) for v in values),
        (pltpu.SemaphoreType.DMA((len(values),)),),
        moved=8 * sum(v.size for v in values),
        room=16,
    )


def adam_body(parts, scale_ref, *refs):
    sums, grads, refs = refs[:parts], refs[parts : parts + 4], refs[parts + 4 :]
    held, outs, norm_ref = refs[:20], refs[20:44], refs[44]
    total = sums[0][...]
    if parts == 4:
        total = (total + sums[1][...]) + (sums[2][...] + sums[3][...])
    gains = total[0:4]
    square = jnp.sum(total[4:5]) + jnp.sum(gains * gains)
    norm = jnp.sqrt(jnp.broadcast_to(square, (1, 1)))
    norm_ref[0, 0] = jnp.sum(norm)
    factor = jnp.minimum(1.0, clip_limit / (norm + 1e-06))
    fixed_one, fixed_two = scale_ref[0], scale_ref[1]
    for k, (rate, decay) in enumerate(RATES):
        weight, moment, square, average = (ref[...] for ref in held[4 * k : 4 * k + 4])
        grad = grads[k][...] if k < 4 else gains
        new = adam_update(
            weight, grad, moment, square, average, rate, decay, factor, fixed_one, fixed_two
        )
        for i in range(4):
            outs[4 * k + i][...] = new[i]
        if k < 4:
            outs[20 + k][...] = new[0].astype(BF16)


def adam(sums, scales, grads, sets):
    outs = tuple(shape(s[0].shape, F32) for s in sets for _ in range(4))
    outs += tuple(shape(s[0].shape, BF16) for s in sets[:4]) + (shape((1, 1), F32),)
    got = call(
        functools.partial(adam_body, len(sums)),
        outs,
        (scales,),
        tuple(sums) + tuple(grads) + sum((tuple(s) for s in sets), ()),
        flops=30 * sum(s[0].size for s in sets),
        moved=38 * sum(s[0].size for s in sets),
        room=16,
        small=(24,),
    )
    return [got[4 * k : 4 * k + 4] for k in range(5)], got[20:24], got[24]


def per_device(
    grid,
    tokens,
    cotangent,
    clip_ids,
    frame_ids,
    step,
    w_qkv,
    w_out,
    w_up,
    w_down,
    norm_params,
    moment_qkv,
    moment_out,
    moment_up,
    moment_down,
    moment_norm,
    square_qkv,
    square_out,
    square_up,
    square_down,
    square_norm,
    average_qkv,
    average_out,
    average_up,
    average_down,
    average_norm,
):
    n, d = tokens.shape
    back_steps = CLIP // n
    mp_index = lax.axis_index("mp")

    def shifted(value, k):
        pairs = [(i, i + k) for i in range(grid.mp) if 0 <= i + k < grid.mp]
        return lax.ppermute(value, "mp", pairs)

    frames = lax.dynamic_slice_in_dim(frame_ids, mp_index * n, n, 0)
    low = (CLIP + jnp.arange(n, dtype=jnp.int32)) // FRAME - frames
    first = low[::TQ] * FRAME // TK
    low = low.reshape(1, n)

    low_qkv, low_out, low_up, low_down = (
        jnp.concatenate([w_qkv[0], w_qkv[1], w_qkv[2]], axis=1).astype(BF16)
        if grid.fast
        else w_qkv.astype(BF16),
        w_out.T.astype(BF16),
        w_up.astype(BF16),
        w_down.T.astype(BF16),
    )
    if grid.fast:
        slots, spots, side = grid.slots(), grid.spots(), grid.sides()
        rest = jnp.concatenate([low_out, low_up, low_down], axis=1)
        near, halo = joined(grid.gather_z(low_qkv), shifted(tokens, 1))
        rest = after(rest, near)
        near_rest = grid.gather_z(rest)
        near_rest, *held = joined(near_rest, *grid.gather_plane(near))
        far = tuple(held) + grid.across(held)
        held = grid.gather_plane(near_rest)
        qkv, kt, vt, xt, full_qkv = project(first, tokens, halo, norm_params, None, spots, far)
        mixture, logs = attend(first, low, qkv, vt)
        mixture, *held = joined(mixture, *held)
        far = tuple(held) + grid.across(held)
        block_out, gmix, gmid, gains_two, sent, *parts = feed(
            in_hbm(tokens), mixture, in_hbm(cotangent), norm_params, None, 4 * low_up.shape[1],
            spots, slots, side, far,
        )
        kept = feed_kept(slots, side, mixture, *parts)
        got, gmix, kept = joined(grid.scatter_core(sent), gmix, kept)
        held = grid.scatter_plane(kept, got)
        gt, kept_qkv, sent = attend_back(
            first, low, qkv, kt, xt, mixture, logs, gmix, slots, side
        )
        sent, gt, *held = joined(sent, gt, *held)
        near_rest = grid.scatter_z(held)
        held = grid.scatter_plane(kept_qkv, grid.scatter_core(sent))
        grad_rows, back, gains_one = first_back(
            first, tokens, halo, norm_params, full_qkv, gmid, gt
        )
        back, *got = joined(back, *near_rest, *held)
        near_rest, held = got[:4], got[4:]
        near_qkv = grid.scatter_z(held)
        near_qkv = joined(*near_qkv)
        back = shifted(after(back, near_qkv[1]), -1)
        grad_out, grad_up, grad_down, grad_qkv, sums = totals(
            near_rest, near_qkv, gains_one, gains_two
        )
        sums = sums + grid.swap(sums, c=1)
        line = [grid.swap(sums, z=k) for k in (1, 2, 3)]
        sums = (sums + line[0]) + (line[1] + line[2])
        grad_tokens = grad_rows + back.astype(F32)
        sums = [sums] + [grid.swap(sums, y=b, x=a) for a, b in ((1, 0), (0, 1), (1, 1))]
        *sums, grad_tokens = joined(*sums, grad_tokens)
    else:
        halo = jnp.concatenate([shifted(tokens, k) for k in range(back_steps, 0, -1)])
        full_qkv = beside(whole_of(low_qkv))
        full = tuple(whole_of(a) for a in (low_out, low_up, low_down))
        qkv, kt, vt, xt = project(first, tokens, halo, norm_params, full_qkv)
        mixture, logs = attend(first, low, qkv, vt)
        block_out, gmix, gmid, gains_two, gup, gdown, gout = feed(
            tokens, mixture, cotangent, norm_params, full, full[1].shape[1]
        )
        grad_up, grad_down, grad_out = share_of(gup), share_of(gdown), share_of(gout)
        gt, gqkv = attend_back(first, low, qkv, kt, xt, mixture, logs, gmix)
        grad_qkv = share_of(apart(gqkv))
        grad_rows, back, gains_one = first_back(
            first, tokens, halo, norm_params, full_qkv, gmid, gt
        )
        grad_tokens = grad_rows
        for i, hop in enumerate(range(back_steps, 0, -1)):
            grad_tokens = grad_tokens + shifted(back[i * n : (i + 1) * n], -hop).astype(F32)
        weight_square = (
            jnp.sum(grad_qkv * grad_qkv)
            + jnp.sum(grad_out * grad_out)
            + jnp.sum(grad_up * grad_up)
            + jnp.sum(grad_down * grad_down)
        )
        row = jnp.zeros((4, d), F32).at[0, 0].set(weight_square)
        sums = [lax.psum(jnp.concatenate([gains_one, gains_two, row]), BOTH)]
    step_count = step[0].astype(F32)
    scales = jnp.stack(
        [1.0 - jnp.power(beta_one, step_count), 1.0 - jnp.power(beta_two, step_count)]
    )
    states = (
        (w_qkv, moment_qkv, square_qkv, average_qkv),
        (w_out.T, moment_out.T, square_out.T, average_out.T),
        (w_up, moment_up, square_up, average_up),
        (w_down.T, moment_down.T, square_down.T, average_down.T),
        (norm_params, moment_norm, square_norm, average_norm),
    )
    if grid.fast:
        flat = load(sum(states, ()))
        states = tuple(tuple(flat[4 * k : 4 * k + 4]) for k in range(5))
    sets, copies, norm_value = adam(
        sums, scales, (grad_qkv, grad_out, grad_up, grad_down), states
    )
    norm_value = norm_value.reshape(())

    def turned(k, value):
        return value.T if k in (1, 3) else value

    return (
        (block_out, grad_tokens, norm_value)
        + tuple(turned(k, s[0]) for k, s in enumerate(sets))
        + tuple(turned(k, s[1]) for k, s in enumerate(sets))
        + tuple(turned(k, s[2]) for k, s in enumerate(sets))
        + tuple(turned(k, c) for k, c in enumerate(copies))
        + tuple(turned(k, s[3]) for k, s in enumerate(sets))
    )


def solution(mesh):
    rows = P(BOTH, None)
    weights = (P(None, "dp", "mp"), P("mp", "dp"), P("dp", "mp"), P("mp", "dp"))
    states = weights + (P(),)
    return jax.shard_map(
        functools.partial(per_device, Grid(mesh.shape["dp"], mesh.shape["mp"])),
        mesh=mesh,
        in_specs=(rows, rows, P("dp"), P("dp"), P()) + states * 4,
        out_specs=(rows, rows, P()) + states * 3 + weights + states,
        check_vma=False,
    )
```

```python
import functools

import jax
import jax.numpy as jnp
from jax import lax
from jax.experimental import pallas as pl
from jax.experimental.pallas import tpu as pltpu
from jax.sharding import PartitionSpec as P

HEAD = 64
CLIP = 1024
FRAME = 64

norm_eps = 1e-05
beta_one = 0.9
beta_two = 0.95
adam_eps = 1e-08
clip_limit = 1.0
ema_decay = 0.75

F32 = jnp.float32
BF16 = jnp.bfloat16
BOTH = ("dp", "mp")
VMEM = pltpu.VMEM
MASKED = -1e30
PAIR = 2 * HEAD
TQ = 256
TK = 256
ROWS = 256
FEED_ROWS = 1024


def mm(a, b):
    return lax.dot_general(a, b, (((1,), (0,)), ((), ())), preferred_element_type=F32)


def mm_nt(a, b):
    return lax.dot_general(a, b, (((1,), (1,)), ((), ())), preferred_element_type=F32)


def mm_tn(a, b):
    return lax.dot_general(a, b, (((0,), (0,)), ((), ())), preferred_element_type=F32)


def shape(dims, kind):
    return jax.ShapeDtypeStruct(tuple(dims), kind)


def call(body, outs, smem, ins, far=(), scratch=(), flops=0, moved=0, room=60, loose=(), small=()):
    return pl.pallas_call(
        body,
        out_shape=outs,
        in_specs=[pl.BlockSpec(memory_space=pltpu.SMEM)] * len(smem)
        + [pl.BlockSpec(memory_space=VMEM)] * len(ins)
        + [pl.BlockSpec(memory_space=pl.ANY)] * len(far),
        out_specs=tuple(
            pl.BlockSpec(
                memory_space=pl.ANY if i in loose else pltpu.SMEM if i in small else VMEM
            )
            for i in range(len(outs))
        ),
        scratch_shapes=list(scratch),
        compiler_params=pltpu.CompilerParams(vmem_limit_bytes=room << 20),
        cost_estimate=pl.CostEstimate(
            flops=int(flops), bytes_accessed=int(moved), transcendentals=0
        ),
    )(*smem, *ins, *far)


def rows_at(tile, base=0):
    return pl.ds(pl.multiple_of(base + tile * ROWS, ROWS), ROWS)


def normalize(rows):
    center = rows - jnp.mean(rows, axis=-1, keepdims=True)
    inverse = lax.rsqrt(jnp.mean(center * center, axis=-1, keepdims=True) + norm_eps)
    return center * inverse, inverse


def norm_back(grad, xhat, inverse, gain_row):
    gy = grad * gain_row
    return inverse * (
        gy
        - jnp.mean(gy, axis=-1, keepdims=True)
        - xhat * jnp.mean(gy * xhat, axis=-1, keepdims=True)
    )


def place(spots_ref, far, sems, parts):
    copies = []
    for s in range(32):
        row, col = spots_ref[s] // 4, spots_ref[s] % 4
        for t, (start, wide, whole) in enumerate(parts):
            block = far[s // 4].at[s % 4]
            rows = block.shape[-2]
            at = (
                pl.ds(pl.multiple_of(row * rows, rows), rows),
                pl.ds(pl.multiple_of(col * wide, wide), wide),
            )
            lead = (slice(None),) * (len(block.shape) - 2)
            copies.append(
                pltpu.make_async_copy(
                    block.at[lead + (slice(None), pl.ds(start, wide))],
                    whole.at[lead + at],
                    sems.at[s * len(parts) + t],
                )
            )
    for copy in copies:
        copy.start()
    return copies


def fetch(pairs, sems, start=0):
    copies = [
        pltpu.make_async_copy(far, near, sems.at[start + k]) for k, (far, near) in enumerate(pairs)
    ]
    for copy in copies:
        copy.start()
    return copies


def project_body(fast, first_ref, *refs):
    if fast:
        spots_ref, norm_ref, own_far, halo_far = refs[:4]
        far, refs = refs[4:12], refs[12:]
        qkv_ref, kt_ref, vt_ref, xt_ref, w_ref, own_ref, halo_ref, sems = refs
        copies = place(spots_ref, far, sems, [(0, far[0].shape[-1], w_ref)])
        copies += fetch(((own_far, own_ref), (halo_far, halo_ref)), sems, 32)
        for copy in copies:
            copy.wait()
    else:
        own_ref, halo_ref, norm_ref, w_ref, qkv_ref, kt_ref, vt_ref, xt_ref = refs
    gain, shift = norm_ref[0:1, :], norm_ref[1:2, :]
    pairs = w_ref.shape[1] // (3 * PAIR)

    def rows_of(ref, tile, base):
        to = rows_at(tile, base)
        xhat, _ = normalize(ref[rows_at(tile), :].astype(F32))
        xn = xhat * gain + shift
        xt_ref[:, to] = xn.T.astype(BF16)
        xn = xn.astype(BF16)
        for p in range(pairs):
            at, lanes = p * 3 * PAIR, slice(p * PAIR, (p + 1) * PAIR)
            qkv = mm(xn, w_ref[:, at : at + 3 * PAIR])
            qkv_ref[to, at : at + 3 * PAIR] = qkv.astype(BF16)
            kt_ref[lanes, to] = qkv[:, PAIR : 2 * PAIR].T.astype(BF16)
            vt_ref[lanes, to] = qkv[:, 2 * PAIR :].T.astype(BF16)

    @pl.loop(jnp.minimum(first_ref[0], CLIP // ROWS), CLIP // ROWS)
    def _(tile):
        rows_of(halo_ref, tile, 0)

    @pl.loop(0, own_ref.shape[0] // ROWS)
    def _(tile):
        rows_of(own_ref, tile, CLIP)


def project(first, own, halo, norms, w_qkv, spots=None, far=()):
    n, d = own.shape
    total = n + CLIP
    fast = len(far) > 0
    outs = (
        shape((total, 3 * d), BF16),
        shape((d, total), BF16),
        shape((d, total), BF16),
        shape((d, total), BF16),
    )
    if fast:
        outs += (shape((d, 3 * d), BF16),)
    return call(
        functools.partial(project_body, fast),
        outs,
        (first, spots) if fast else (first,),
        (norms,) if fast else (own, halo, norms, w_qkv),
        (own, halo) + tuple(far) if fast else (),
        (VMEM(own.shape, BF16), VMEM(halo.shape, BF16), pltpu.SemaphoreType.DMA((34,)))
        if fast
        else (),
        flops=6 * d * d * total,
        moved=2 * d * (6 * total + 2 * n) + 6 * d * d,
        room=24,
    )


def split_heads(pair):
    zero = jnp.zeros((HEAD, pair.shape[1]), pair.dtype)
    return jnp.concatenate(
        [
            jnp.concatenate([pair[:HEAD], zero], axis=1),
            jnp.concatenate([zero, pair[HEAD:]], axis=1),
        ]
    )


def twice(row):
    return jnp.concatenate([row, row], axis=1)


def sight(low_ref, at, i):
    spot = lax.broadcasted_iota(jnp.int32, (1, TQ), 1)
    last = ((CLIP + i * TQ) + spot) >> 6
    frame = lax.broadcasted_iota(jnp.int32, (TK, 2 * TQ), 0) >> 6
    return twice(low_ref[0:1, at]), twice(last), frame


def attend_body(
    first_ref, low_ref, qkv_ref, vt_ref, mix_ref, log_ref, qt, acc, top, total, s_ref, p_ref
):
    pairs = mix_ref.shape[1] // PAIR

    @pl.loop(0, mix_ref.shape[0] // TQ)
    def _(i):
        at = pl.ds(pl.multiple_of(i * TQ, TQ), TQ)
        low, last, frame = sight(low_ref, at, i)
        here = pl.ds(pl.multiple_of(CLIP + i * TQ, TQ), TQ)
        for p in range(pairs):
            query = qkv_ref[here, p * 3 * PAIR : (p * 3 + 1) * PAIR] * HEAD**-0.5
            qt[p] = split_heads(query.T)
        acc[...] = jnp.zeros_like(acc)
        top[...] = jnp.full_like(top, MASKED)
        total[...] = jnp.zeros_like(total)

        def step(j, carry):
            keys = pl.ds(pl.multiple_of(j * TK, TK), TK)
            shift = j * (TK // FRAME)
            visible = (frame >= low - shift) & (frame <= last - shift)
            for p in range(pairs):
                scores = mm(qkv_ref[keys, (p * 3 + 1) * PAIR : (p * 3 + 2) * PAIR], qt[p])
                s_ref[p] = jnp.where(visible, scores, MASKED)
            for p in range(pairs):
                scores = s_ref[p]
                old = top[p]
                new = jnp.maximum(old, jnp.max(scores, axis=0, keepdims=True))
                weights = jnp.exp(scores - new)
                keep = jnp.exp(old - new)
                top[p] = new
                total[p] = total[p] * keep + jnp.sum(weights, axis=0, keepdims=True)
                p_ref[p] = weights.astype(BF16)
                for h in range(2):
                    part = slice(h * HEAD, (h + 1) * HEAD)
                    acc[p, part, :] = acc[p, part, :] * keep[:, h * TQ : (h + 1) * TQ]
            for p in range(pairs):
                for h in range(2):
                    part = slice(h * HEAD, (h + 1) * HEAD)
                    values = vt_ref[p * PAIR + h * HEAD : p * PAIR + (h + 1) * HEAD, keys]
                    acc[p, part, :] += mm(values, p_ref[p, :, h * TQ : (h + 1) * TQ])
            return carry

        lax.fori_loop(first_ref[i], (CLIP + (i + 1) * TQ + TK - 1) // TK, step, 0)
        for p in range(pairs):
            sums = total[p]
            logs = top[p] + jnp.log(sums)
            inverse = 1.0 / sums
            for h in range(2):
                part = slice(h * HEAD, (h + 1) * HEAD)
                wide = slice(h * TQ, (h + 1) * TQ)
                acc[p, part, :] = acc[p, part, :] * inverse[:, wide]
                log_ref[2 * p + h : 2 * p + h + 1, at] = logs[:, wide]
            mix_ref[at, p * PAIR : (p + 1) * PAIR] = acc[p].T.astype(BF16)


def attend(first, low, qkv, vt):
    d, total = vt.shape
    n = total - CLIP
    pairs = d // PAIR
    return call(
        attend_body,
        (shape((n, d), BF16), shape((d // HEAD, n), F32)),
        (first,),
        (low, qkv, vt),
        scratch=(
            VMEM((pairs, PAIR, 2 * TQ), BF16),
            VMEM((pairs, PAIR, TQ), F32),
            VMEM((pairs, 1, 2 * TQ), F32),
            VMEM((pairs, 1, 2 * TQ), F32),
            VMEM((pairs, TK, 2 * TQ), F32),
            VMEM((pairs, TK, 2 * TQ), BF16),
        ),
        flops=16 * n * 1024 * d,
        moved=2 * d * (2 * n + 4 * total),
        room=24,
    )


def attend_back_body(fast, first_ref, *refs):
    if fast:
        slots_ref, side_ref, refs = refs[0], refs[1], refs[2:]
    low_ref, qkv_ref, kt_ref, xt_ref, mix_ref, log_ref, grad_ref, gt_ref = refs[:8]
    outs, refs = refs[8 : 10 if fast else 9], refs[10 if fast else 9 :]
    qt, gt, qs, gs, acc, dk_acc, dv_acc, s_ref, d_ref, p_ref, ds_ref, rows_ref, g_acc = refs
    n, d = grad_ref.shape
    pairs = d // PAIR
    start = jnp.minimum(first_ref[0], CLIP // ROWS)
    tiles = qkv_ref.shape[0] // ROWS

    @pl.loop(start, tiles)
    def _(tile):
        dk_acc[:, rows_at(tile)] = jnp.zeros((d, ROWS), F32)
        dv_acc[:, rows_at(tile)] = jnp.zeros((d, ROWS), F32)

    @pl.loop(start, CLIP // ROWS)
    def _(tile):
        for p in range(pairs):
            gt_ref[p * 3 * PAIR : (p * 3 + 1) * PAIR, rows_at(tile)] = jnp.zeros((PAIR, ROWS), BF16)

    @pl.loop(0, n // TQ)
    def _(i):
        at = pl.ds(pl.multiple_of(i * TQ, TQ), TQ)
        here = pl.ds(pl.multiple_of(CLIP + i * TQ, TQ), TQ)
        low, last, frame = sight(low_ref, at, i)
        for p in range(pairs):
            lanes = slice(p * PAIR, (p + 1) * PAIR)
            query = (qkv_ref[here, p * 3 * PAIR : (p * 3 + 1) * PAIR] * HEAD**-0.5).T
            grad = grad_ref[at, lanes]
            both = (grad.astype(F32) * mix_ref[at, lanes].astype(F32)).T
            grad = grad.T
            qt[p] = query
            gt[p] = grad
            qs[p] = split_heads(query)
            gs[p] = split_heads(grad)
            for h in range(2):
                wide = slice(h * TQ, (h + 1) * TQ)
                rows_ref[p, 0:1, wide] = jnp.sum(
                    both[h * HEAD : (h + 1) * HEAD], axis=0, keepdims=True
                )
                rows_ref[p, 1:2, wide] = log_ref[2 * p + h : 2 * p + h + 1, at]
        acc[...] = jnp.zeros_like(acc)

        def step(j, carry):
            keys = pl.ds(pl.multiple_of(j * TK, TK), TK)
            shift = j * (TK // FRAME)
            visible = (frame >= low - shift) & (frame <= last - shift)
            for p in range(pairs):
                one = (p * 3 + 1) * PAIR
                scores = mm(qkv_ref[keys, one : one + PAIR], qs[p])
                s_ref[p] = jnp.where(visible, scores, MASKED)
                d_ref[p] = mm(qkv_ref[keys, one + PAIR : one + 2 * PAIR], gs[p])
            for p in range(pairs):
                probs = jnp.exp(s_ref[p] - rows_ref[p, 1:2, :])
                p_ref[p] = probs.astype(BF16)
                ds_ref[p] = (probs * (d_ref[p] - rows_ref[p, 0:1, :])).astype(BF16)
            for p in range(pairs):
                for h in range(2):
                    part = slice(h * HEAD, (h + 1) * HEAD)
                    rows = slice(p * PAIR + h * HEAD, p * PAIR + (h + 1) * HEAD)
                    wide = slice(h * TQ, (h + 1) * TQ)
                    dv_acc[rows, keys] += mm_nt(gt[p, part, :], p_ref[p, :, wide])
                    dk_acc[rows, keys] += mm_nt(qt[p, part, :], ds_ref[p, :, wide])
                    acc[p, part, :] += mm(kt_ref[rows, keys], ds_ref[p, :, wide])
            return carry

        lax.fori_loop(first_ref[i], (CLIP + (i + 1) * TQ + TK - 1) // TK, step, 0)
        for p in range(pairs):
            gt_ref[p * 3 * PAIR : (p * 3 + 1) * PAIR, here] = (acc[p] * HEAD**-0.5).astype(BF16)

    @pl.loop(start, tiles)
    def _(tile):
        at = rows_at(tile)
        for p in range(pairs):
            one, rows = (p * 3 + 1) * PAIR, slice(p * PAIR, (p + 1) * PAIR)
            gt_ref[one : one + PAIR, at] = dk_acc[rows, at].astype(BF16)
            gt_ref[one + PAIR : one + 2 * PAIR, at] = dv_acc[rows, at].astype(BF16)

    wide = 6 * PAIR

    def weights(side):
        rows = pl.ds(pl.multiple_of(side * wide, wide), wide)
        g_acc[...] = mm_nt(xt_ref[:, CLIP:], gt_ref[rows, CLIP:])

        @pl.loop(start, CLIP // ROWS)
        def _(tile):
            g_acc[...] += mm_nt(xt_ref[:, rows_at(tile)], gt_ref[rows, rows_at(tile)])

    if not fast:
        for side in range(d // (2 * PAIR)):
            weights(side)
            outs[0][:, side * wide : (side + 1) * wide] = g_acc[...].astype(BF16)
        return
    rows = d // 8
    for k in range(2):
        side = side_ref[k]
        weights(side)
        for x in range(2):
            for r in range(8):
                slot = slots_ref[r * 4 + side * 2 + x] & 15
                outs[k][slot] = g_acc[
                    r * rows : (r + 1) * rows, x * 3 * PAIR : (x + 1) * 3 * PAIR
                ].astype(BF16)


def attend_back(first, low, qkv, kt, xt, mixture, logs, grad, slots=None, side=None):
    n, d = grad.shape
    total = qkv.shape[0]
    pairs = d // PAIR
    fast = slots is not None
    outs = (shape((3 * d, total), BF16),)
    if fast:
        outs += (shape((16, d // 8, 3 * d // 4), BF16),) * 2
    else:
        outs += (shape((d, 3 * d), BF16),)
    return call(
        functools.partial(attend_back_body, fast),
        outs,
        (first, slots, side) if fast else (first,),
        (low, qkv, kt, xt, mixture, logs, grad),
        scratch=(
            VMEM((pairs, PAIR, TQ), BF16),
            VMEM((pairs, PAIR, TQ), BF16),
            VMEM((pairs, PAIR, 2 * TQ), BF16),
            VMEM((pairs, PAIR, 2 * TQ), BF16),
            VMEM((pairs, PAIR, TQ), F32),
            VMEM((d, total), F32),
            VMEM((d, total), F32),
            VMEM((pairs, TK, 2 * TQ), F32),
            VMEM((pairs, TK, 2 * TQ), F32),
            VMEM((pairs, TK, 2 * TQ), BF16),
            VMEM((pairs, TK, 2 * TQ), BF16),
            VMEM((pairs, 8, 2 * TQ), F32),
            VMEM((d, 6 * PAIR), F32),
        ),
        flops=40 * n * 1024 * d,
        moved=2 * d * (2 * n + 8 * total),
        room=38,
    )


def chunks_of(far, near, size):
    return [
        (far.at[pl.ds(i, size), :], near.at[pl.ds(i, size), :])
        for i in range(0, near.shape[0], size)
    ]


def feed_blocks(slots_ref, side, mix_ref, act_ref, gh_ref, n2t_ref, lowt_ref, cott_ref, out_ref):
    d = n2t_ref.shape[0]
    one, wide, rows = d // 4, act_ref.shape[1] // 2, d // 8
    small = pl.ds(pl.multiple_of(side * 2 * one, 2 * one), 2 * one)
    spots = [[slots_ref[r * 4 + side * 2 + x] & 15 for r in range(8)] for x in range(2)]
    for start, size, left, right in (
        (0, one, lowt_ref, mix_ref[:, small]),
        (one, wide, n2t_ref, gh_ref),
        (one + wide, wide, cott_ref, act_ref),
    ):
        for x in range(2):
            grad = mm(left[...], right[:, x * size : (x + 1) * size]).astype(BF16)
            for r in range(8):
                out_ref[spots[x][r], :, start : start + size] = grad[r * rows : (r + 1) * rows]


def feed_kept_body(slots_ref, side_ref, *refs):
    feed_blocks(slots_ref, side_ref[0], *refs)


def feed_kept(slots, side, mixture, act, gh, n2t, lowt, cott):
    n, half = act.shape
    d = n2t.shape[0]
    return call(
        feed_kept_body,
        (shape((16, d // 8, d // 4 + half), BF16),),
        (slots, side),
        (mixture, act, gh, n2t, lowt, cott),
        flops=n * d * (4 * half + d),
        moved=2 * n * (4 * d + 2 * half),
        room=20,
    )[0]


def feed_body(fast, *refs):
    late = []
    if fast:
        spots_ref, slots_ref, side_ref, mix_ref, norm_ref, x_far, cot_far = refs[:7]
        far, refs = refs[7:15], refs[15:]
        out_ref, gmix_ref, gmid_ref, gain_ref, sent_ref, act_kept, gh_kept = refs[:7]
        (n2t_ref, lowt_ref, cott_ref), refs = refs[7:10], refs[10:]
        wo_ref, up_ref, down_ref, x_ref, cot_ref, sems, act_sent, gh_sent = refs
        acts, ghs = (act_kept, act_sent), (gh_kept, gh_sent)
        one, ff = wo_ref.shape[1] // 4, up_ref.shape[1] // 4
        near = fetch(chunks_of(x_far, x_ref, 256) + chunks_of(cot_far, cot_ref, 256), sems, 96)
        copies = place(
            spots_ref, far, sems,
            [(0, one, wo_ref), (one, ff, up_ref), (one + ff, ff, down_ref)],
        )
        late = [copy for k, copy in enumerate(copies) if k % 3]
        for copy in near + copies[::3]:
            copy.wait()
    else:
        x_ref, mix_ref, cot_ref, norm_ref, wo_ref, up_ref, down_ref = refs[:7]
        out_ref, gmix_ref, gmid_ref, gain_ref = refs[7:11]
        outs, refs = refs[11:14], refs[14:]
        act_ref, gh_ref, n2t_ref, lowt_ref, cott_ref = refs
        acts, ghs = (act_ref,), (gh_ref,)
    gain, shift = norm_ref[2:3, :], norm_ref[3:4, :]
    ff = up_ref.shape[1]
    d = x_ref.shape[1]
    wide = min(1024, ff)
    held = acts[0].shape[1]
    root = 0.7978845608028654
    gain_ref[...] = jnp.zeros_like(gain_ref)
    rows = min(FEED_ROWS, x_ref.shape[0])

    @pl.loop(0, x_ref.shape[0] // rows)
    def _(tile):
        at = pl.ds(pl.multiple_of(tile * rows, rows), rows)
        cot = cot_ref[at, :]
        cott_ref[:, at] = cot.T
        middle = x_ref[at, :].astype(F32) + mm_nt(mix_ref[at, :], wo_ref[...])
        xhat, inverse = normalize(middle)
        n2 = xhat * gain + shift
        n2t_ref[:, at] = n2.T.astype(BF16)
        n2 = n2.astype(BF16)
        if late:

            @pl.when(tile == 0)
            def _():
                for copy in late:
                    copy.wait()

        out = middle
        second = jnp.zeros_like(middle)
        for k in range(len(acts)):
            base = side_ref[k] * held if fast else 0
            for c in range(held // wide):
                cols = pl.ds(pl.multiple_of(base + c * wide, wide), wide)
                to = slice(c * wide, (c + 1) * wide)
                hidden = mm(n2, up_ref[:, cols])
                square = hidden * hidden
                bent = jnp.tanh(hidden * (root + (root * 0.044715) * square))
                half = 0.5 + 0.5 * bent
                active = (hidden * half).astype(BF16)
                slope = half + hidden * (1.0 - bent * bent) * (
                    0.5 * root + (0.5 * root * 3 * 0.044715) * square
                )
                acts[k][at, to] = active
                out += mm_nt(active, down_ref[:, cols])
                gh = (mm(cot, down_ref[:, cols]) * slope).astype(BF16)
                ghs[k][at, to] = gh
                second += mm_nt(gh, up_ref[:, cols])
        out_ref[at, :] = out.astype(BF16)
        gain_ref[0:1, :] += jnp.sum(second * xhat, axis=0, keepdims=True)
        gain_ref[1:2, :] += jnp.sum(second, axis=0, keepdims=True)
        gmid = cot.astype(F32) + norm_back(second, xhat, inverse, gain)
        gmid_ref[at, :] = gmid
        lowt_ref[:, at] = gmid.T.astype(BF16)
        gmix_ref[at, :] = mm(gmid.astype(BF16), wo_ref[...]).astype(BF16)

    if fast:
        feed_blocks(
            slots_ref, side_ref[1], mix_ref, acts[1], ghs[1], n2t_ref, lowt_ref, cott_ref, sent_ref
        )
        return
    gup_ref, gdown_ref, gout_ref = outs
    for c in range(ff // wide):
        cols = slice(c * wide, (c + 1) * wide)
        gup_ref[:, cols] = mm(n2t_ref[...], gh_ref[:, cols]).astype(BF16)
        gdown_ref[:, cols] = mm(cott_ref[...], act_ref[:, cols]).astype(BF16)
    gout_ref[...] = mm(lowt_ref[...], mix_ref[...]).astype(BF16)


def feed(x, mixture, cot, norms, full, ff, spots=None, slots=None, side=None, far=()):
    n, d = x.shape
    fast = len(far) > 0
    outs = (shape((n, d), BF16), shape((n, d), BF16), shape((n, d), F32), shape((2, d), F32))
    turned = (shape((d, n), BF16),) * 3
    if fast:
        outs += (shape((16, d // 8, d // 4 + ff // 2), BF16),)
        outs += (shape((n, ff // 2), BF16),) * 2 + turned
        scratch = (
            VMEM((d, d), BF16),
            VMEM((d, ff), BF16),
            VMEM((d, ff), BF16),
            VMEM((n, d), BF16),
            VMEM((n, d), BF16),
            pltpu.SemaphoreType.DMA((96 + 2 * (n // 256),)),
            VMEM((n, ff // 2), BF16),
            VMEM((n, ff // 2), BF16),
        )
    else:
        outs += (shape((d, ff), BF16), shape((d, ff), BF16), shape((d, d), BF16))
        scratch = (VMEM((n, ff), BF16),) * 2 + tuple(VMEM(t.shape, BF16) for t in turned)
    return call(
        functools.partial(feed_body, fast),
        outs,
        (spots, slots, side) if fast else (),
        (mixture, norms) if fast else (x, mixture, cot, norms) + tuple(full),
        (x, cot) + tuple(far) if fast else (),
        scratch,
        flops=2 * n * d * (6 * ff + 3 * d),
        moved=2 * n * 6 * d + 8 * d * ff,
        room=36,
    )


def first_back_body(
    first_ref, norm_ref, w_ref, gmid_ref, gt_ref, own_far, halo_far, grad_ref, back_ref, gain_ref,
    own_ref, halo_ref, sems,
):
    for copy in fetch(((own_far, own_ref), (halo_far, halo_ref)), sems):
        copy.wait()
    gain = norm_ref[0:1, :]
    gain_ref[...] = jnp.zeros_like(gain_ref)
    start = jnp.minimum(first_ref[0], CLIP // ROWS)

    def rows_of(ref, tile, base, own):
        at = rows_at(tile)
        first = mm(w_ref[...], gt_ref[:, rows_at(tile, base)]).T
        xhat, inverse = normalize(ref[at, :].astype(F32))
        gain_ref[0:1, :] += jnp.sum(first * xhat, axis=0, keepdims=True)
        gain_ref[1:2, :] += jnp.sum(first, axis=0, keepdims=True)
        grad = norm_back(first, xhat, inverse, gain)
        if own:
            grad_ref[at, :] = gmid_ref[at, :] + grad
        else:
            back_ref[at, :] = grad.astype(BF16)

    @pl.loop(0, start)
    def _(tile):
        back_ref[rows_at(tile), :] = jnp.zeros((ROWS, back_ref.shape[1]), BF16)

    @pl.loop(start, CLIP // ROWS)
    def _(tile):
        rows_of(halo_ref, tile, 0, False)

    @pl.loop(0, own_ref.shape[0] // ROWS)
    def _(tile):
        rows_of(own_ref, tile, CLIP, True)


def first_back(first, own, halo, norms, w_qkv, gmid, gt):
    n, d = own.shape
    total = n + CLIP
    return call(
        first_back_body,
        (shape((n, d), F32), shape((CLIP, d), BF16), shape((2, d), F32)),
        (first,),
        (norms, w_qkv, gmid, gt),
        (own, halo),
        (VMEM(own.shape, BF16), VMEM(halo.shape, BF16), pltpu.SemaphoreType.DMA((2,))),
        flops=6 * d * d * total,
        moved=2 * d * (4 * total + 6 * n),
        room=24,
    )


class Grid:
    def __init__(self, dp, mp):
        self.dp, self.mp = dp, mp
        self.fast = (dp, mp) == (8, 4)

    def swap(self, value, z=0, y=0, x=0, c=0):
        bits = z * 8 + y * 4 + x * 2 + c
        return lax.ppermute(value, BOTH, [(i, i ^ bits) for i in range(self.dp * self.mp)])

    def spot(self):
        dp, mp = lax.axis_index("dp"), lax.axis_index("mp")
        return dp // 2, dp % 2, mp // 2, mp % 2

    def slots(self):
        z, y, x, c = self.spot()
        s = jnp.arange(32, dtype=jnp.int32)
        oz, oy, oc, ox = s >> 3, (s >> 2) & 1, (s >> 1) & 1, s & 1
        return (oc ^ c) * 16 + (ox ^ x) * 8 + (oy ^ y) * 4 + (oz ^ z)

    def spots(self):
        z, y, x, c = self.spot()
        s = jnp.arange(32, dtype=jnp.int32)
        oc, ox, oy, oz = (s >> 4) ^ c, ((s >> 3) & 1) ^ x, ((s >> 2) & 1) ^ y, (s & 3) ^ z
        return ((oz * 2 + oy) * 2 + oc) * 2 + ox

    def sides(self):
        c = lax.axis_index("mp") % 2
        return jnp.stack([c, 1 - c]).astype(jnp.int32)

    def gather_z(self, block):
        return jnp.stack([block] + [self.swap(block, z=k) for k in (1, 2, 3)])

    def across(self, held):
        return tuple(self.swap(a, c=1) for a in held)

    def gather_plane(self, near):
        return near, self.swap(near, y=1), self.swap(near, x=1), self.swap(near, y=1, x=1)

    def scatter_core(self, sent):
        return self.swap(sent, c=1)

    def scatter_plane(self, kept, got):
        own, one, two, three = (added(kept[k : k + 4], got[k : k + 4]) for k in (0, 4, 8, 12))
        return own, self.swap(one, y=1), self.swap(two, x=1), self.swap(three, y=1, x=1)

    def scatter_z(self, held):
        parts = [sum(a[k].astype(F32) for a in held).astype(BF16) for k in range(4)]
        return [parts[0]] + [self.swap(parts[k], z=k) for k in (1, 2, 3)]


def added(a, b):
    return (a.astype(F32) + b.astype(F32)).astype(BF16)


def whole_of(block):
    m = block.ndim - 2
    half = lax.all_gather(block, "dp", axis=m, tiled=True)
    return lax.all_gather(half, "mp", axis=m + 1, tiled=True)


def share_of(whole):
    m = whole.ndim - 2
    half = lax.psum_scatter(whole, "mp", scatter_dimension=m + 1, tiled=True)
    return lax.psum_scatter(half, "dp", scatter_dimension=m, tiled=True).astype(F32)


def beside(whole):
    d = whole.shape[1]
    return whole.reshape(3, d, d // PAIR, PAIR).transpose(1, 2, 0, 3).reshape(d, 3 * d)


def apart(wide):
    d = wide.shape[0]
    return wide.reshape(d, d // PAIR, 3, PAIR).transpose(2, 0, 1, 3).reshape(3, d, d)


def after(value, *others):
    return lax.optimization_barrier((value,) + others)[0]


def in_hbm(value):
    return pltpu.with_memory_space_constraint(value, pltpu.HBM)


def joined(*values):
    return lax.optimization_barrier(values)


def adam_update(
    weight, gradient, moment, square, average, step_rate, decay_rate, factor, fixed_one, fixed_two
):
    gradient = gradient * factor
    moment = beta_one * moment + (1.0 - beta_one) * gradient
    square = beta_two * square + (1.0 - beta_two) * gradient * gradient
    weight = weight - step_rate * (
        moment / fixed_one / (jnp.sqrt(square / fixed_two) + adam_eps) + decay_rate * weight
    )
    average = ema_decay * average + (1.0 - ema_decay) * weight
    return (weight, moment, square, average)


RATES = ((0.03, 0.1), (0.09, 0.1), (0.03, 0.1), (0.015, 0.1), (0.2, 0.0))


def total_body(*refs):
    rest, qkv, (one_ref, two_ref) = refs[:4], refs[4:8], refs[8:10]
    out_ref, up_ref, down_ref, qkv_ref, sums_ref = refs[10:]
    small, wide = out_ref.shape[1], up_ref.shape[1]
    width = sums_ref.shape[1]

    def sum_of(parts, at, size):
        a, b, c, d = (p[:, at : at + size].astype(F32) for p in parts)
        return (a + b) + (c + d)

    def squares(value):
        row = jnp.sum(value * value, axis=0, keepdims=True)
        return row if row.shape[1] == width else jnp.concatenate([row] + [jnp.zeros_like(row)] * (width // row.shape[1] - 1), axis=1)

    grad = sum_of(rest, 0, small)
    out_ref[...] = grad
    square = squares(grad)
    for ref, at in ((up_ref, small), (down_ref, small + wide)):
        grad = sum_of(rest, at, wide)
        ref[...] = grad
        square += squares(grad)
    for k in range(3):
        grad = sum_of(qkv, k * PAIR, PAIR)
        qkv_ref[k] = grad
        square += squares(grad)
    sums_ref[...] = jnp.zeros_like(sums_ref)
    sums_ref[0:2, :] = one_ref[...]
    sums_ref[2:4, :] = two_ref[...]
    sums_ref[4:5, :] = square


def totals(rest, qkv, gains_one, gains_two):
    rows, wide = rest[0].shape
    small = qkv[0].shape[1] // 3
    wide = (wide - small) // 2
    return call(
        total_body,
        (
            shape((rows, small), F32),
            shape((rows, wide), F32),
            shape((rows, wide), F32),
            shape((3, rows, small), F32),
            shape((8, gains_one.shape[1]), F32),
        ),
        (),
        tuple(rest) + tuple(qkv) + (gains_one, gains_two),
        moved=12 * rest[0].size,
        room=16,
    )


def load_body(*refs):
    count = len(refs) // 2
    copies = fetch(tuple(zip(refs[:count], refs[count:-1])), refs[-1])
    for copy in copies:
        copy.wait()


def load(values):
    return call(
        load_body,
        tuple(shape(v.shape, v.dtype) for v in values),
        (),
        (),
        tuple(in_hbm(v) for v in values),
        (pltpu.SemaphoreType.DMA((len(values),)),),
        moved=8 * sum(v.size for v in values),
        room=16,
    )


def adam_body(parts, scale_ref, *refs):
    sums, grads, refs = refs[:parts], refs[parts : parts + 4], refs[parts + 4 :]
    held, outs, norm_ref = refs[:20], refs[20:44], refs[44]
    total = sums[0][...]
    if parts == 4:
        total = (total + sums[1][...]) + (sums[2][...] + sums[3][...])
    gains = total[0:4]
    square = jnp.sum(total[4:5]) + jnp.sum(gains * gains)
    norm = jnp.sqrt(jnp.broadcast_to(square, (1, 1)))
    norm_ref[0, 0] = jnp.sum(norm)
    factor = jnp.minimum(1.0, clip_limit / (norm + 1e-06))
    fixed_one, fixed_two = scale_ref[0], scale_ref[1]
    for k, (rate, decay) in enumerate(RATES):
        weight, moment, square, average = (ref[...] for ref in held[4 * k : 4 * k + 4])
        grad = grads[k][...] if k < 4 else gains
        new = adam_update(
            weight, grad, moment, square, average, rate, decay, factor, fixed_one, fixed_two
        )
        for i in range(4):
            outs[4 * k + i][...] = new[i]
        if k < 4:
            outs[20 + k][...] = new[0].astype(BF16)


def adam(sums, scales, grads, sets):
    outs = tuple(shape(s[0].shape, F32) for s in sets for _ in range(4))
    outs += tuple(shape(s[0].shape, BF16) for s in sets[:4]) + (shape((1, 1), F32),)
    got = call(
        functools.partial(adam_body, len(sums)),
        outs,
        (scales,),
        tuple(sums) + tuple(grads) + sum((tuple(s) for s in sets), ()),
        flops=30 * sum(s[0].size for s in sets),
        moved=38 * sum(s[0].size for s in sets),
        room=16,
        small=(24,),
    )
    return [got[4 * k : 4 * k + 4] for k in range(5)], got[20:24], got[24]


def per_device(
    grid,
    tokens,
    cotangent,
    clip_ids,
    frame_ids,
    step,
    w_qkv,
    w_out,
    w_up,
    w_down,
    norm_params,
    moment_qkv,
    moment_out,
    moment_up,
    moment_down,
    moment_norm,
    square_qkv,
    square_out,
    square_up,
    square_down,
    square_norm,
    average_qkv,
    average_out,
    average_up,
    average_down,
    average_norm,
):
    n, d = tokens.shape
    back_steps = CLIP // n
    mp_index = lax.axis_index("mp")

    def shifted(value, k):
        pairs = [(i, i + k) for i in range(grid.mp) if 0 <= i + k < grid.mp]
        return lax.ppermute(value, "mp", pairs)

    frames = lax.dynamic_slice_in_dim(frame_ids, mp_index * n, n, 0)
    low = (CLIP + jnp.arange(n, dtype=jnp.int32)) // FRAME - frames
    first = low[::TQ] * FRAME // TK
    low = low.reshape(1, n)

    low_qkv, low_out, low_up, low_down = (
        jnp.concatenate([w_qkv[0], w_qkv[1], w_qkv[2]], axis=1).astype(BF16)
        if grid.fast
        else w_qkv.astype(BF16),
        w_out.T.astype(BF16),
        w_up.astype(BF16),
        w_down.T.astype(BF16),
    )
    if grid.fast:
        slots, spots, side = grid.slots(), grid.spots(), grid.sides()
        rest = jnp.concatenate([low_out, low_up, low_down], axis=1)
        near, halo = joined(grid.gather_z(low_qkv), shifted(tokens, 1))
        rest = after(rest, near)
        near_rest = grid.gather_z(rest)
        near_rest, *held = joined(near_rest, *grid.gather_plane(near))
        far = tuple(held) + grid.across(held)
        held = grid.gather_plane(near_rest)
        qkv, kt, vt, xt, full_qkv = project(first, tokens, halo, norm_params, None, spots, far)
        mixture, logs = attend(first, low, qkv, vt)
        mixture, *held = joined(mixture, *held)
        far = tuple(held) + grid.across(held)
        block_out, gmix, gmid, gains_two, sent, *parts = feed(
            in_hbm(tokens), mixture, in_hbm(cotangent), norm_params, None, 4 * low_up.shape[1],
            spots, slots, side, far,
        )
        kept = feed_kept(slots, side, mixture, *parts)
        got, gmix, kept = joined(grid.scatter_core(sent), gmix, kept)
        held = grid.scatter_plane(kept, got)
        gt, kept_qkv, sent = attend_back(
            first, low, qkv, kt, xt, mixture, logs, gmix, slots, side
        )
        sent, gt, *held = joined(sent, gt, *held)
        near_rest = grid.scatter_z(held)
        held = grid.scatter_plane(kept_qkv, grid.scatter_core(sent))
        grad_rows, back, gains_one = first_back(
            first, tokens, halo, norm_params, full_qkv, gmid, gt
        )
        back, *got = joined(back, *near_rest, *held)
        near_rest, held = got[:4], got[4:]
        near_qkv = grid.scatter_z(held)
        near_qkv = joined(*near_qkv)
        back = shifted(after(back, near_qkv[1]), -1)
        grad_out, grad_up, grad_down, grad_qkv, sums = totals(
            near_rest, near_qkv, gains_one, gains_two
        )
        sums = sums + grid.swap(sums, c=1)
        line = [grid.swap(sums, z=k) for k in (1, 2, 3)]
        sums = (sums + line[0]) + (line[1] + line[2])
        grad_tokens = grad_rows + back.astype(F32)
        sums = [sums] + [grid.swap(sums, y=b, x=a) for a, b in ((1, 0), (0, 1), (1, 1))]
        *sums, grad_tokens = joined(*sums, grad_tokens)
    else:
        halo = jnp.concatenate([shifted(tokens, k) for k in range(back_steps, 0, -1)])
        full_qkv = beside(whole_of(low_qkv))
        full = tuple(whole_of(a) for a in (low_out, low_up, low_down))
        qkv, kt, vt, xt = project(first, tokens, halo, norm_params, full_qkv)
        mixture, logs = attend(first, low, qkv, vt)
        block_out, gmix, gmid, gains_two, gup, gdown, gout = feed(
            tokens, mixture, cotangent, norm_params, full, full[1].shape[1]
        )
        grad_up, grad_down, grad_out = share_of(gup), share_of(gdown), share_of(gout)
        gt, gqkv = attend_back(first, low, qkv, kt, xt, mixture, logs, gmix)
        grad_qkv = share_of(apart(gqkv))
        grad_rows, back, gains_one = first_back(
            first, tokens, halo, norm_params, full_qkv, gmid, gt
        )
        grad_tokens = grad_rows
        for i, hop in enumerate(range(back_steps, 0, -1)):
            grad_tokens = grad_tokens + shifted(back[i * n : (i + 1) * n], -hop).astype(F32)
        weight_square = (
            jnp.sum(grad_qkv * grad_qkv)
            + jnp.sum(grad_out * grad_out)
            + jnp.sum(grad_up * grad_up)
            + jnp.sum(grad_down * grad_down)
        )
        row = jnp.zeros((4, d), F32).at[0, 0].set(weight_square)
        sums = [lax.psum(jnp.concatenate([gains_one, gains_two, row]), BOTH)]
    step_count = step[0].astype(F32)
    scales = jnp.stack(
        [1.0 - jnp.power(beta_one, step_count), 1.0 - jnp.power(beta_two, step_count)]
    )
    states = (
        (w_qkv, moment_qkv, square_qkv, average_qkv),
        (w_out.T, moment_out.T, square_out.T, average_out.T),
        (w_up, moment_up, square_up, average_up),
        (w_down.T, moment_down.T, square_down.T, average_down.T),
        (norm_params, moment_norm, square_norm, average_norm),
    )
    if grid.fast:
        flat = load(sum(states, ()))
        states = tuple(tuple(flat[4 * k : 4 * k + 4]) for k in range(5))
    sets, copies, norm_value = adam(
        sums, scales, (grad_qkv, grad_out, grad_up, grad_down), states
    )
    norm_value = norm_value.reshape(())

    def turned(k, value):
        return value.T if k in (1, 3) else value

    return (
        (block_out, grad_tokens, norm_value)
        + tuple(turned(k, s[0]) for k, s in enumerate(sets))
        + tuple(turned(k, s[1]) for k, s in enumerate(sets))
        + tuple(turned(k, s[2]) for k, s in enumerate(sets))
        + tuple(turned(k, c) for k, c in enumerate(copies))
        + tuple(turned(k, s[3]) for k, s in enumerate(sets))
    )


def solution(mesh):
    rows = P(BOTH, None)
    weights = (P(None, "dp", "mp"), P("mp", "dp"), P("dp", "mp"), P("mp", "dp"))
    states = weights + (P(),)
    return jax.shard_map(
        functools.partial(per_device, Grid(mesh.shape["dp"], mesh.shape["mp"])),
        mesh=mesh,
        in_specs=(rows, rows, P("dp"), P("dp"), P()) + states * 4,
        out_specs=(rows, rows, P()) + states * 3 + weights + states,
        check_vma=False,
    )
```
